32 devices in a mesh: dom: 8 (over z, y), sub: 4 (over x, core).
Axes of the slice: x: 2, y: 2, z: 4, core: 2. Of those that a mesh axis runs over, the one named last changes fastest.
Arguments:
- diag_block: bfloat16 [30, 30, 4096], P(None, None, ('dom', 'sub')), may hold values from -6 to 6
- face_block: bfloat16 [6, 30, 30, 4096], P(None, None, None, ('dom', 'sub')), may hold values from -3 to 3
- restrict1: bfloat16 [30, 30, 4096], P(None, None, ('dom', 'sub')), may hold values from -1 to 1
- neighbour: int32 [6, 4096], P(None, ('dom', 'sub')), may hold values from 0 to 319
- face_slot: int32 [6, 4096], P(None, ('dom', 'sub')), may hold values from 0 to 7
- agg_map: int32 [4096], P(('dom', 'sub')), may hold values from 0 to 15, as said below
- send_list: int32 [6, 1024], P(None, ('dom', 'sub')), may hold values from 0 to 127
- restrict2: float32 [30, 30, 512], P(None, None, ('dom', 'sub')), may hold values from -0.5 to 0.5
- coarse_nbr: int32 [8, 512], P(None, ('dom', 'sub')), may hold values from 0 to 63
- agg2_map: int32 [512], P(('dom', 'sub')), may hold values from 0 to 7, as said below
- coarse_slot: int32 [8, 512], P(None, ('dom', 'sub')), may hold values from 0 to 7
Outputs:
- coarse_one: float32 [8, 30, 30, 512], P(None, None, None, ('dom', 'sub'))
- coarse_two: float32 [8, 30, 30, 64], P(None, None, None, ('dom', 'sub'))
The draws below stay inside these ranges and needn't reach their ends.
Inputs may be any that keep to these rules, and one draw needn't show every extreme that they name: `neighbour`: positions below 128 name the device's own elements; position 128 + r * 32 + h names entry h of the list that the partition at offset o_r sends. `agg_map`: on each device every value is taken by exactly 8 elements. `send_list`: indices of the device's own elements. `coarse_nbr`: index among the subgroup's first-level agglomerates, in device order. `agg2_map`: within each subgroup every value is taken by exactly 8 first-level agglomerates.
All inputs are finite; a program needn't handle non-finite values.
Results may differ from the reference program's by a relative error of at most 0.0029.
Values may be sent and summed in bfloat16 or wider, within the bound.
No kernel may reach another device: no remote copies, remote signals or barrier semaphores. Data moves between devices by JAX's collectives and lax.ppermute only.
A program may use at most 128 MiB of HBM per device.

```python
import jax
import jax.numpy as jnp
from jax import lax

NB = 30
E_DEV = 128
FACES = 6
SLOTS1 = 8
SLOTS2 = 8
RANGE = 3
HALO = 32
ELEMS = 4096
AGGS1 = 512
N_DOM = 8
N_SUB = 4
DEVICES = 32


def draw_agg_map(key, part):
    keys = jax.random.split(jax.random.fold_in(key, 11), N_DOM * N_SUB)
    shuffled = jax.vmap(lambda single_key: jax.random.permutation(single_key, E_DEV))(keys)
    return (shuffled // 8).reshape(-1).astype(jnp.int32)


def draw_agg2_map(key, part):
    keys = jax.random.split(jax.random.fold_in(key, 23), N_DOM)
    shuffled = jax.vmap(lambda single_key: jax.random.permutation(single_key, N_SUB * (E_DEV // 8)))(keys)
    return (shuffled // 8).reshape(-1).astype(jnp.int32)


def set_ends(array, own_key, least, high):
    shape = array.shape
    place = [jax.random.randint(jax.random.fold_in(own_key, axis), (), 0, shape[axis]) for axis in range(len(shape))]
    array = array.at[tuple(place)].set(least)
    longest = shape.index(max(shape))
    place[longest] = (place[longest] + 1) % shape[longest]
    return array.at[tuple(place)].set(high)


def block_scale(own_key, extent, cuts, smallest, top_value):
    level = 1.0
    for dim, parts in cuts:
        heights = jax.random.uniform(jax.random.fold_in(jax.random.fold_in(own_key, 6), dim), (parts,), jnp.float32, smallest / len(cuts), top_value / len(cuts))
        level = level * jnp.repeat(jnp.exp(heights), extent[dim] // parts).reshape((-1,) + (1,) * (len(extent) - 1 - dim))
    return level


def centred(stream_key, dims, width, reach, shards=(), held_as=jnp.bfloat16):
    drawn = width * jax.random.normal(stream_key, dims, jnp.float32)
    if shards:
        drawn = drawn * block_scale(stream_key, dims, shards, -0.22, 0.18)
    return jnp.clip(drawn, -reach, reach).astype(held_as)


def setup_inputs(seed: int = 0) -> dict:
    splits = jax.random.split(jax.random.key(seed), 12)
    return {
        "diag_block": centred(splits[0], (NB, NB, ELEMS), 1.0, 6.0, ((2, 32),)),
        "face_block": centred(splits[1], (FACES, NB, NB, ELEMS), 0.5, 3.0, ((3, 32),)),
        "restrict1": centred(splits[2], (NB, NB, ELEMS), NB ** -0.5, 1.0, ((2, 32),)),
        "neighbour": set_ends(jax.random.randint(splits[3], (FACES, ELEMS), 0, E_DEV + 2 * RANGE * HALO), jax.random.fold_in(splits[3], 1), 0, (E_DEV + 2 * RANGE * HALO) - 1).astype(jnp.int32),
        "face_slot": set_ends(jax.random.randint(splits[4], (FACES, ELEMS), 0, SLOTS1), jax.random.fold_in(splits[4], 1), 0, SLOTS1 - 1).astype(jnp.int32),
        "agg_map": draw_agg_map(jax.random.fold_in(splits[11], 71), 0),
        "send_list": set_ends(jax.random.randint(splits[6], (2 * RANGE, DEVICES * HALO), 0, E_DEV), jax.random.fold_in(splits[6], 1), 0, E_DEV - 1).astype(jnp.int32),
        "restrict2": centred(splits[7], (NB, NB, AGGS1), (4 * NB) ** -0.5, 0.5, ((2, 32),), jnp.float32),
        "coarse_nbr": set_ends(jax.random.randint(splits[8], (SLOTS1, AGGS1), 0, N_SUB * (E_DEV // 8)), jax.random.fold_in(splits[8], 1), 0, (N_SUB * (E_DEV // 8)) - 1).astype(jnp.int32),
        "agg2_map": draw_agg2_map(jax.random.fold_in(splits[11], 71), 0),
        "coarse_slot": set_ends(jax.random.randint(splits[10], (SLOTS1, AGGS1), 0, SLOTS2), jax.random.fold_in(splits[10], 1), 0, SLOTS2 - 1).astype(jnp.int32),
    }


exact = lax.Precision.HIGHEST


def round_half(values):
    return lax.optimization_barrier(values.astype(jnp.bfloat16)).astype(jnp.float32)


def peer_offsets():
    return [step_index - RANGE if step_index < RANGE else step_index - RANGE + 1 for step_index in range(2 * RANGE)]


def level_one(device, diag_block, face_block, restrict1, neighbour, face_slot, agg_map, send_list):
    dom_index = device // N_SUB
    sub_index = device % N_SUB
    first_row = device * E_DEV
    own_maps = lax.dynamic_slice_in_dim(restrict1, first_row, E_DEV, 2)
    pieces = [own_maps]
    for step_index, offset in enumerate(peer_offsets()):
        source = ((dom_index + offset) % N_DOM) * N_SUB + sub_index
        listed = lax.dynamic_slice_in_dim(send_list[step_index], source * HALO, HALO, 0)
        pieces.append(jnp.take(restrict1, (source * E_DEV + listed).astype(jnp.int32), axis=2))
    extended = jnp.concatenate(pieces, axis=2).astype(jnp.float32)
    own_float = own_maps.astype(jnp.float32)
    diag_here = lax.dynamic_slice_in_dim(diag_block, first_row, E_DEV, 2).astype(jnp.float32)
    faces_here = lax.dynamic_slice_in_dim(face_block, first_row, E_DEV, 3).astype(jnp.float32)
    link_ids = lax.dynamic_slice_in_dim(neighbour, first_row, E_DEV, 1)
    slot_ids = lax.dynamic_slice_in_dim(face_slot, first_row, E_DEV, 1)
    groups = lax.dynamic_slice_in_dim(agg_map, first_row, E_DEV, 0)
    own_half = round_half(jnp.einsum('imb,jmb->ijb', diag_here, own_float, precision=exact))
    self_term = jnp.einsum('aib,ijb->ajb', own_float, own_half, precision=exact)
    far_maps = jnp.take(extended, link_ids.reshape(-1), axis=2).reshape(NB, NB, FACES, E_DEV)
    face_half = round_half(jnp.einsum('kimb,jmkb->kijb', faces_here, far_maps, precision=exact))
    face_term = jnp.einsum('aib,kijb->kajb', own_float, face_half, precision=exact)
    slot_index = jnp.arange(SLOTS1, dtype=jnp.int32)
    slot_pick = (slot_ids[None] == slot_index[:, None, None]).astype(jnp.float32)
    first_slot = (slot_index == 0).astype(jnp.float32)[:, None, None, None]
    per_elem = jnp.einsum('skb,kajb->sajb', slot_pick, face_term, precision=exact) + first_slot * self_term[None]
    summed = jax.ops.segment_sum(jnp.moveaxis(per_elem, 3, 0), groups, num_segments=E_DEV // 8)
    return jnp.moveaxis(summed, 0, 3)


def level_two(group, coarse_one, restrict2, coarse_nbr, agg2_map, coarse_slot):
    member_count = N_SUB * (E_DEV // 8)
    owned_count = member_count // 8
    first_row = group * member_count
    blocks = lax.dynamic_slice_in_dim(coarse_one, first_row, member_count, 3)
    level_maps = lax.dynamic_slice_in_dim(restrict2, first_row, member_count, 2)
    link_ids = lax.dynamic_slice_in_dim(coarse_nbr, first_row, member_count, 1)
    groups = lax.dynamic_slice_in_dim(agg2_map, first_row, member_count, 0)
    slot_ids = lax.dynamic_slice_in_dim(coarse_slot, first_row, member_count, 1)
    far_maps = jnp.take(level_maps, link_ids.reshape(-1), axis=2).reshape(NB, NB, SLOTS1, member_count)
    right_half = jnp.einsum('sijb,kjsb->sikb', blocks, far_maps, precision=exact)
    products = jnp.einsum('aib,sikb->sakb', level_maps, right_half, precision=exact)
    targets = (slot_ids * owned_count + groups[None]).reshape(-1).astype(jnp.int32)
    item_rows = jnp.moveaxis(products, 3, 1).reshape(SLOTS1 * member_count, NB, NB)
    summed = jax.ops.segment_sum(item_rows, targets, num_segments=SLOTS2 * owned_count)
    return jnp.moveaxis(summed.reshape(SLOTS2, owned_count, NB, NB), 1, 3)


def reference(diag_block, face_block, restrict1, neighbour, face_slot, agg_map, send_list, restrict2, coarse_nbr, agg2_map, coarse_slot):
    devices = jnp.arange(N_DOM * N_SUB, dtype=jnp.int32)
    per_device = lax.map(lambda device: level_one(device, diag_block, face_block, restrict1, neighbour, face_slot, agg_map, send_list), devices)
    coarse_one = jnp.moveaxis(per_device, 0, 3).reshape(SLOTS1, NB, NB, -1)
    subgroups = jnp.arange(N_DOM, dtype=jnp.int32)
    per_group = lax.map(lambda group: level_two(group, coarse_one, restrict2, coarse_nbr, agg2_map, coarse_slot), subgroups)
    coarse_two = jnp.moveaxis(per_group, 0, 3).reshape(SLOTS2, NB, NB, -1)
    return (coarse_one, coarse_two)
```

```python
import functools

import jax
import jax.numpy as jnp
from jax import lax
from jax.experimental import pallas as pl
from jax.experimental.pallas import tpu as pltpu
from jax.sharding import PartitionSpec as P

SLOTS2 = 8
PER_AGG = 8
PAD = 32
LANES = 128
SPLIT = LANES // PAD
PACK = PAD // SPLIT


F32 = jnp.float32
HALF = jnp.bfloat16

VMEM = pl.BlockSpec(memory_space=pltpu.VMEM)
SMEM = pl.BlockSpec(memory_space=pltpu.SMEM)
ANY = pl.BlockSpec(memory_space=pl.ANY)


def shifted(shard, axis, by):
    count = lax.axis_size(axis)
    return lax.ppermute(shard, axis, [(i, (i + by) % count) for i in range(count)])


def spread(rows):
    block = lax.broadcasted_iota(jnp.int32, rows.shape, 1) // PAD
    turned = [rows] + [pltpu.roll(rows, PAD * q, axis=1) for q in range(1, SPLIT)]
    results = []
    for part in range(SPLIT):
        result = turned[(SPLIT - 1 - part) % SPLIT]
        for b in range(SPLIT - 1):
            result = jnp.where(block == b, turned[(b - part) % SPLIT], result)
        results.append(result)
    return results


def unpacked(packed):
    return jnp.concatenate(spread(packed), axis=0)


def split_two(value):
    high = value.astype(HALF)
    return high, (value - high.astype(F32)).astype(HALF)


def transposed_rows(maps_ref, padded, packed):
    order, _, elems = maps_ref.shape
    padded[...] = jnp.zeros_like(padded)
    for j in range(order):
        padded[j * PAD : j * PAD + order, :] = maps_ref[j].astype(F32)
    for M in range(PACK):
        group = jnp.concatenate(
            [padded[pl.ds(q * PACK + M, PAD, stride=PAD), :] for q in range(SPLIT)], axis=0
        )
        packed[M * elems : (M + 1) * elems, :] = group.T


def padded_members(maps2_ref, padded):
    order, members, _ = maps2_ref.shape
    padded[...] = jnp.zeros_like(padded)
    for d in range(order):
        padded[d * members : (d + 1) * members, :order] = maps2_ref[d]


def set_masks(masks):
    slots = masks.shape[0] // 2
    block = lax.broadcasted_iota(jnp.int32, (PAD, LANES), 1) // PAD
    for s in range(slots):
        for h in range(2):
            masks[s * 2 + h] = jnp.where(block + h * SPLIT == s, 1.0, 0.0).astype(HALF)


def pack_kernel(send_ref, maps_ref, maps2_ref, *refs):
    send_rows, halo = send_ref.shape
    out_refs, own2_ref = refs[:send_rows], refs[send_rows]
    padded, packed, flat, padded2 = refs[send_rows + 1 :]
    members = maps2_ref.shape[1]
    elems = maps_ref.shape[2]
    transposed_rows(maps_ref, padded, packed)
    for r in range(send_rows):

        def body(i, carry, r=r):
            for u in range(8):
                h = i * 8 + u
                row = packed[pl.ds(send_ref[r, h], PACK, stride=elems), :]
                flat[pl.ds(pl.multiple_of(h * PACK, PACK), PACK), :] = row
            return carry

        lax.fori_loop(0, halo // 8, body, 0)
        out_refs[r][...] = flat[...].astype(HALF)
    padded_members(maps2_ref, padded2)
    for g in range(members // SPLIT):
        group = jnp.concatenate(
            [padded2[pl.ds(g * SPLIT + q, PAD, stride=members), :] for q in range(SPLIT)], axis=0
        )
        own2_ref[g] = group.T[:PAD]


def local_kernel(axis, agg_ref, nbr2_ref, slot2_ref, diag_ref, face_ref, maps_ref, maps2_ref, *refs):
    count = lax.axis_size(axis)
    two_refs = refs[:count]
    table_ref, g_ref, order_ref, pick2_ref, r2_ref = refs[count : count + 5]
    padded, packed, slab, left, right, seen, two_hi, two_lo, masks, padded2 = refs[count + 5 :]
    order, _, elems = maps_ref.shape
    faces = face_ref.shape[0]
    members = maps2_ref.shape[1]
    slots = nbr2_ref.shape[0]

    for a in range(members):
        seen[a] = a * PER_AGG

    def place(e, carry):
        at = seen[agg_ref[e]]
        order_ref[at] = e
        seen[agg_ref[e]] = at + 1
        return carry

    lax.fori_loop(0, elems, place, 0)

    transposed_rows(maps_ref, padded, packed)

    def table(i, carry):
        for u in range(4):
            e = i * 4 + u
            table_ref[e] = unpacked(packed[pl.ds(e, PACK, stride=elems), :]).astype(HALF)
        return carry

    lax.fori_loop(0, elems // 4, table, 0)

    slab[...] = jnp.zeros_like(slab)
    for half in (left, right):
        half[order * elems :, :] = jnp.zeros((half.shape[0] - order * elems, LANES), F32)
    for r in range(order):
        base = (r % 2) * 2 * LANES
        sources = [diag_ref[r]] + [face_ref[k, r] for k in range(faces)] + [maps_ref[r]]
        for k, source in enumerate(sources):
            slab[base + k * PAD : base + k * PAD + order, :] = source.astype(F32)
        left[r * elems : (r + 1) * elems, :] = slab[base : base + LANES, :].T
        right[r * elems : (r + 1) * elems, :] = slab[base + LANES : base + 2 * LANES, :].T

    def products(i, carry):
        for u in range(8):
            at = i * 8 + u
            e = order_ref[at]
            half0 = left[pl.ds(e, PAD, stride=elems), :]
            half1 = right[pl.ds(e, PAD, stride=elems), :]
            rows = jnp.concatenate([half0, half1], axis=1).astype(HALF)
            own = pltpu.roll(half1, PAD, axis=1).astype(HALF)[:, :PAD]
            high, low = split_two(jnp.dot(own, rows, preferred_element_type=F32))
            g_ref[at, 0:PAD, :] = high
            g_ref[at, PAD : 2 * PAD, :] = low
        return carry

    lax.fori_loop(0, elems // 8, products, 0)

    me = lax.axis_index(axis)
    for o in range(count):
        first = lax.rem(me + (count - o), count) * members
        for g in range(members // SPLIT):
            for q, block in enumerate(spread(two_refs[o][g])):
                high, low = split_two(block)
                two_hi[first + g * SPLIT + q] = high
                two_lo[first + g * SPLIT + q] = low
    set_masks(masks)

    def pick(i, carry):
        for j in range(slots):
            source = nbr2_ref[j, i]
            slot = slot2_ref[j, i]
            for which, two in enumerate((two_hi, two_lo)):
                block = two[source]
                for h in range(2):
                    pick2_ref[i, which, j * PAD : (j + 1) * PAD, h * LANES : (h + 1) * LANES] = (
                        block * masks[slot * 2 + h]
                    )
        return carry

    lax.fori_loop(0, members, pick, 0)
    padded_members(maps2_ref, padded2)
    for i in range(members):
        high, low = split_two(padded2[pl.ds(i, PAD, stride=members), :])
        r2_ref[i, 0:PAD, :] = high
        r2_ref[i, PAD : 2 * PAD, :] = low


def combine_kernel(axis, order_ref, nbr_ref, slot_ref, agg2_ref, *refs):
    count = lax.axis_size(axis)
    faces = nbr_ref.shape[0]
    elems = nbr_ref.shape[1]
    send_rows = len(refs) - (4 + 2 + count + 9)
    halo_refs = refs[:send_rows]
    own_ref, g_hbm, pick2_hbm, r2_ref = refs[send_rows : send_rows + 4]
    one_refs = refs[send_rows + 4 : send_rows + 6]
    part_refs = refs[send_rows + 6 : send_rows + 6 + count]
    table, masks, g_ref, pick2_ref, acc0, acc1, own_sem, g_sem, pick2_sem = refs[
        send_rows + 6 + count :
    ]
    halo = halo_refs[0].shape[0]
    members = agg2_ref.shape[0]
    steps = g_sem.shape[0]
    per_step = members // steps
    chunk = elems // steps
    copies = [
        pltpu.make_async_copy(
            g_hbm.at[pl.ds(s * chunk, chunk)], g_ref.at[pl.ds(s * chunk, chunk)], g_sem.at[s]
        )
        for s in range(steps)
    ]
    own_copy = pltpu.make_async_copy(own_ref, table.at[pl.ds(0, elems)], own_sem.at[0])
    pick_copy = pltpu.make_async_copy(pick2_hbm, pick2_ref, pick2_sem.at[0])
    own_copy.start()
    for copy in copies:
        copy.start()
    pick_copy.start()
    set_masks(masks)
    for r in range(send_rows):

        def arrive(i, carry, r=r):
            for u in range(4):
                h = i * 4 + u
                table[elems + r * halo + h] = unpacked(halo_refs[r][h].astype(F32)).astype(HALF)
            return carry

        lax.fori_loop(0, halo // 4, arrive, 0)
    own_copy.wait()

    def gather(i, carry):
        total = jnp.zeros((2 * PAD, 2 * LANES), F32)
        for u in range(PER_AGG):
            at = i * PER_AGG + u
            e = order_ref[at]
            rows = []
            for k in range(faces + 1):
                block = table[e if k == 0 else nbr_ref[k - 1, e]]
                slot = 0 if k == 0 else slot_ref[k - 1, e]
                rows.append(
                    jnp.concatenate([block * masks[slot * 2 + h] for h in range(2)], axis=1)
                )
            total = total + jnp.dot(
                g_ref[at][:, : (faces + 1) * PAD],
                jnp.concatenate(rows, axis=0),
                preferred_element_type=F32,
            )
        one = total[:PAD] + total[PAD:]
        first = pl.multiple_of(i * PAD, PAD)
        for h in range(2):
            one_refs[h][pl.ds(first, PAD), :] = one[:, h * LANES : (h + 1) * LANES]
        return carry

    for s in range(steps):
        copies[s].wait()
        lax.fori_loop(s * per_step, (s + 1) * per_step, gather, 0)
    acc0[...] = jnp.zeros_like(acc0)
    acc1[...] = jnp.zeros_like(acc1)
    pick_copy.wait()

    def second(i4, carry):
        for u in range(4):
            i = i4 * 4 + u
            first = pl.multiple_of(i * PAD, PAD)
            one = jnp.concatenate([ref[pl.ds(first, PAD), :] for ref in one_refs], axis=1)
            high, low = split_two(one)
            w = jnp.dot(
                jnp.concatenate([high, low], axis=0), pick2_ref[i, 0], preferred_element_type=F32
            )
            w = (w[:PAD] + w[PAD:]) + jnp.dot(high, pick2_ref[i, 1], preferred_element_type=F32)
            w_high, w_low = split_two(w)
            r2 = r2_ref[i][:, :PAD]
            z = jnp.dot(r2, w_high, preferred_element_type=F32)
            z = (z[:PAD] + z[PAD:]) + jnp.dot(r2[:PAD], w_low, preferred_element_type=F32)
            to = agg2_ref[i]
            acc0[to] = acc0[to] + z[:, :LANES]
            acc1[to] = acc1[to] + z[:, LANES:]
        return carry

    lax.fori_loop(0, members // 4, second, 0)
    me = lax.axis_index(axis)
    owned = acc0.shape[0] // count
    for o in range(count):
        first = lax.rem(me + o, count) * owned
        for h, acc in enumerate((acc0, acc1)):
            for k in range(owned):
                part_refs[o][h, k * PAD : (k + 1) * PAD, :] = acc[first + k]


def one_kernel(one0_ref, one1_ref, out_ref):
    slots, order, members, _ = out_ref.shape
    for a in range(order):
        for h, ref in enumerate((one0_ref, one1_ref)):
            rows = ref[pl.ds(a, members, stride=PAD), :]
            for q in range(SPLIT):
                turned = rows if q == 0 else pltpu.roll(rows, LANES - q * PAD, axis=1)
                out_ref[h * SPLIT + q, a] = turned[:, :order]


def two_kernel(*refs):
    part_refs, out_ref, total = refs[:-2], refs[-2], refs[-1]
    slots, order, owned, _ = out_ref.shape
    value = part_refs[0][...]
    for ref in part_refs[1:]:
        value = value + ref[...]
    total[...] = value
    for a in range(order):
        for h in range(2):
            rows = total[h, pl.ds(a, owned, stride=PAD), :]
            for q in range(SPLIT):
                turned = rows if q == 0 else pltpu.roll(rows, LANES - q * PAD, axis=1)
                out_ref[h * SPLIT + q, a] = turned[:, :order]


def per_device(
    diag_block,
    face_block,
    restrict1,
    neighbour,
    face_slot,
    agg_map,
    send_list,
    restrict2,
    coarse_nbr,
    agg2_map,
    coarse_slot,
):
    order, _, elems = restrict1.shape
    faces = face_block.shape[0]
    send_rows, halo = send_list.shape
    reach = send_rows // 2
    slots = coarse_nbr.shape[0]
    members = elems // PER_AGG
    owned = members // PER_AGG
    count = lax.axis_size("sub")
    offsets = [r - reach if r < reach else r - reach + 1 for r in range(send_rows)]
    shape = jax.ShapeDtypeStruct
    maps2 = jnp.transpose(restrict2, (0, 2, 1))

    packed = pl.pallas_call(
        pack_kernel,
        name="pack",
        in_specs=[SMEM, VMEM, VMEM],
        out_specs=[VMEM] * (send_rows + 1),
        out_shape=[shape((halo * PACK, LANES), HALF)] * send_rows
        + [shape((members // SPLIT, PAD, LANES), F32)],
        scratch_shapes=[
            pltpu.VMEM((PAD * PAD, elems), F32),
            pltpu.VMEM((PACK * elems, LANES), F32),
            pltpu.VMEM((halo * PACK, LANES), F32),
            pltpu.VMEM((PAD * members, LANES), F32),
        ],
    )(send_list, restrict1, maps2)
    sends, own2 = packed[:send_rows], packed[send_rows]
    two = [own2] + [shifted(own2, "sub", o) for o in range(1, count)]
    arrived = [shifted(sends[r], "dom", -offset) for r, offset in enumerate(offsets)]

    table, g, order_list, pick2, r2 = pl.pallas_call(
        functools.partial(local_kernel, "sub"),
        name="local",
        in_specs=[SMEM] * 3 + [VMEM] * (4 + count),
        out_specs=[VMEM, VMEM, SMEM, VMEM, VMEM],
        out_shape=[
            shape((elems, PAD, LANES), HALF),
            shape((elems, 2 * PAD, 2 * LANES), HALF),
            shape((elems,), jnp.int32),
            shape((members, 2, slots * PAD, 2 * LANES), HALF),
            shape((members, 2 * PAD, LANES), HALF),
        ],
        scratch_shapes=[
            pltpu.VMEM((PAD * PAD, elems), F32),
            pltpu.VMEM((PACK * elems, LANES), F32),
            pltpu.VMEM((4 * LANES, elems), F32),
            pltpu.VMEM((PAD * elems, LANES), F32),
            pltpu.VMEM((PAD * elems, LANES), F32),
            pltpu.SMEM((members,), jnp.int32),
            pltpu.VMEM((count * members, PAD, LANES), HALF),
            pltpu.VMEM((count * members, PAD, LANES), HALF),
            pltpu.VMEM((2 * SLOTS2, PAD, LANES), HALF),
            pltpu.VMEM((PAD * members, LANES), F32),
        ],
        cost_estimate=pl.CostEstimate(
            flops=20_000_000_000, bytes_accessed=40_000_000, transcendentals=0
        ),
    )(agg_map, coarse_nbr, coarse_slot, diag_block, face_block, restrict1, maps2, *two)

    steps = 4
    combined = pl.pallas_call(
        functools.partial(combine_kernel, "sub"),
        name="combine",
        in_specs=[SMEM] * 4 + [VMEM] * send_rows + [ANY, ANY, ANY, VMEM],
        out_specs=[VMEM] * (2 + count),
        out_shape=[shape((members * PAD, LANES), F32)] * 2
        + [shape((2, owned * PAD, LANES), F32)] * count,
        scratch_shapes=[
            pltpu.VMEM((elems + send_rows * halo, PAD, LANES), HALF),
            pltpu.VMEM((2 * SLOTS2, PAD, LANES), HALF),
            pltpu.VMEM(g.shape, HALF),
            pltpu.VMEM(pick2.shape, HALF),
            pltpu.VMEM((count * owned, PAD, LANES), F32),
            pltpu.VMEM((count * owned, PAD, LANES), F32),
            pltpu.SemaphoreType.DMA((1,)),
            pltpu.SemaphoreType.DMA((steps,)),
            pltpu.SemaphoreType.DMA((1,)),
        ],
    )(
        order_list,
        neighbour,
        face_slot,
        agg2_map,
        *[block.reshape(halo, PACK, LANES) for block in arrived],
        table,
        g,
        pick2,
        r2,
    )
    one0, one1, parts = combined[0], combined[1], combined[2:]
    landed = [parts[0]] + [shifted(parts[o], "sub", o) for o in range(1, count)]
    coarse_one = pl.pallas_call(
        one_kernel,
        name="first",
        in_specs=[VMEM] * 2,
        out_specs=VMEM,
        out_shape=shape((slots, order, members, order), F32),
        cost_estimate=pl.CostEstimate(
            flops=2_000_000_000, bytes_accessed=4_000_000, transcendentals=0
        ),
    )(one0, one1)
    coarse_two = pl.pallas_call(
        two_kernel,
        name="second",
        in_specs=[VMEM] * count,
        out_specs=VMEM,
        out_shape=shape((SLOTS2, order, owned, order), F32),
        scratch_shapes=[pltpu.VMEM((2, owned * PAD, LANES), F32)],
    )(*landed)
    return (
        jnp.transpose(coarse_one, (0, 1, 3, 2)),
        jnp.transpose(coarse_two, (0, 1, 3, 2)),
    )


def solution(mesh):
    placed = (
        P(None, None, ("dom", "sub")),
        P(None, None, None, ("dom", "sub")),
        P(None, None, ("dom", "sub")),
        P(None, ("dom", "sub")),
        P(None, ("dom", "sub")),
        P(("dom", "sub")),
        P(None, ("dom", "sub")),
        P(None, None, ("dom", "sub")),
        P(None, ("dom", "sub")),
        P(("dom", "sub")),
        P(None, ("dom", "sub")),
    )
    return jax.shard_map(
        per_device,
        mesh=mesh,
        in_specs=placed,
        out_specs=(P(None, None, None, ("dom", "sub")), P(None, None, None, ("dom", "sub"))),
        check_vma=False,
    )
```

```python
import functools

import jax
import jax.numpy as jnp
from jax import lax
from jax.experimental import pallas as pl
from jax.experimental.pallas import tpu as pltpu
from jax.sharding import PartitionSpec as P

SLOTS2 = 8
PER_AGG = 8
PAD = 32
LANES = 128
SPLIT = LANES // PAD
PACK = PAD // SPLIT


F32 = jnp.float32
HALF = jnp.bfloat16

VMEM = pl.BlockSpec(memory_space=pltpu.VMEM)
SMEM = pl.BlockSpec(memory_space=pltpu.SMEM)
ANY = pl.BlockSpec(memory_space=pl.ANY)


def shifted(shard, axis, by):
    count = lax.axis_size(axis)
    return lax.ppermute(shard, axis, [(i, (i + by) % count) for i in range(count)])


def spread(rows):
    block = lax.broadcasted_iota(jnp.int32, rows.shape, 1) // PAD
    turned = [rows] + [pltpu.roll(rows, PAD * q, axis=1) for q in range(1, SPLIT)]
    results = []
    for part in range(SPLIT):
        result = turned[(SPLIT - 1 - part) % SPLIT]
        for b in range(SPLIT - 1):
            result = jnp.where(block == b, turned[(b - part) % SPLIT], result)
        results.append(result)
    return results


def unpacked(packed):
    return jnp.concatenate(spread(packed), axis=0)


def split_two(value):
    high = value.astype(HALF)
    return high, (value - high.astype(F32)).astype(HALF)


def transposed_rows(maps_ref, padded, packed):
    order, _, elems = maps_ref.shape
    padded[...] = jnp.zeros_like(padded)
    for j in range(order):
        padded[j, :order, :] = maps_ref[j].astype(F32)
    rows = []
    for M in range(PACK):
        rows.append([])
    turned = [
        [jnp.swapaxes(padded[8 * b : 8 * b + 8, 8 * q : 8 * q + 8, :], 0, 1) for b in range(PAD // 8)]
        for q in range(SPLIT)
    ]
    packs = [
        jnp.concatenate([turned[q][b][M] for q in range(SPLIT) for b in range(PAD // 8)], axis=0).T
        for M in range(PACK)
    ]
    for e in range(0, elems, 8):
        group = jnp.stack([pack[e : e + 8, :] for pack in packs], axis=0)
        packed[e : e + 8] = jnp.swapaxes(group, 0, 1)


def padded_members(maps2_ref, padded, turned):
    order, members, _ = maps2_ref.shape
    padded[...] = jnp.zeros_like(padded)
    for d in range(order):
        padded[d, :, :order] = maps2_ref[d]
    for d in range(0, PAD, 8):
        for i in range(0, members, 8):
            turned[i : i + 8, d : d + 8, :] = jnp.swapaxes(padded[d : d + 8, i : i + 8, :], 0, 1)


def in_order(agg, elems):
    across = jnp.broadcast_to(agg, (elems, elems)).astype(F32)
    here = lax.broadcasted_iota(jnp.int32, (elems, elems), 0)
    there = lax.broadcasted_iota(jnp.int32, (elems, elems), 1)
    ahead = (across.T == across) & (here < there)
    rank = jnp.sum(jnp.where(ahead, 1.0, 0.0), axis=0, keepdims=True)
    place = jnp.broadcast_to(agg.astype(F32) * PER_AGG + rank, (elems, elems)).T
    found = jnp.where(place == there.astype(F32), here.astype(F32), 0.0)
    return jnp.sum(found, axis=0, keepdims=True).astype(jnp.int32)


def set_masks(masks):
    slots = masks.shape[0] // 2
    block = lax.broadcasted_iota(jnp.int32, (8, LANES), 1) // PAD
    for s in range(slots):
        for h in range(2):
            masks[s * 2 + h] = jnp.where(block + h * SPLIT == s, 1.0, 0.0).astype(HALF)


def masked(block, mask):
    return (block.reshape(PAD // 8, 8, LANES) * mask[None]).reshape(PAD, LANES)


def pack_kernel(send_ref, maps_ref, maps2_ref, *refs):
    send_rows, halo = send_ref.shape
    out_refs, own2_ref, packed, turned2 = refs[:send_rows], *refs[send_rows : send_rows + 3]
    padded, flat, padded2 = refs[send_rows + 3 :]
    members = maps2_ref.shape[1]
    transposed_rows(maps_ref, padded, packed)
    for r in range(send_rows):
        for h in range(halo):
            flat[h * PACK : (h + 1) * PACK, :] = packed[send_ref[r, h]]
        out_refs[r][...] = flat[...].astype(HALF)
    padded_members(maps2_ref, padded2, turned2)
    for g in range(members // SPLIT):
        group = turned2[g * SPLIT : (g + 1) * SPLIT].reshape(SPLIT * PAD, LANES)
        own2_ref[g] = group.T[:PAD]


def local_kernel(axis, agg_ref, diag_ref, face_ref, maps_ref, packed, turned2, *refs):
    count = lax.axis_size(axis)
    two_refs = refs[:count]
    table_ref, g_ref, order_ref, two_hi, two_lo, r2_ref = refs[count : count + 6]
    slab, left, right, rows_ref, own_ref, order_row, order_sem = refs[count + 6 :]
    order, _, elems = maps_ref.shape
    faces = face_ref.shape[0]
    members = turned2.shape[0]

    order_row[...] = in_order(agg_ref[...], elems)
    order_copy = pltpu.make_async_copy(order_row, order_ref, order_sem.at[0])
    order_copy.start()

    def table(i, carry):
        for u in range(16):
            e = i * 16 + u
            table_ref[e] = unpacked(packed[e]).astype(HALF)
        return carry

    lax.fori_loop(0, elems // 16, table, 0)

    slab[...] = jnp.zeros_like(slab)
    tall = 2 * SPLIT * PAD
    for part in range(2):
        for rr in range(PAD // 2):
            r = part * (PAD // 2) + rr
            if r >= order:
                left[rr] = jnp.zeros((elems, LANES), F32)
                right[rr] = jnp.zeros((elems, LANES), F32)
                continue
            base = (r % 2) * tall
            sources = [diag_ref[r]] + [face_ref[k, r] for k in range(faces)] + [maps_ref[r]]
            for k, source in enumerate(sources):
                slab[base + k * PAD : base + k * PAD + order, :] = source
            turned = slab[base : base + tall, :].T.astype(F32)
            left[rr] = turned[:, :LANES]
            right[rr] = turned[:, LANES:]

        def shuffle(i, carry, part=part):
            for v in range(2):
                e = pl.multiple_of(i * 16 + v * 8, 8)
                for h, half in enumerate((left, right)):
                    top = jnp.swapaxes(half[0:8, pl.ds(e, 8), :], 0, 1)
                    low = jnp.swapaxes(half[8:16, pl.ds(e, 8), :], 0, 1)
                    for u in range(8):
                        both = jnp.concatenate([top[u], low[u]], axis=0)
                        to = slice(part * 16, part * 16 + 16)
                        rows_ref[e + u, to, h * LANES : (h + 1) * LANES] = both.astype(HALF)
                        if h == 1:
                            own_ref[e + u, to, :] = pltpu.roll(both, PAD, axis=1).astype(HALF)
            return carry

        lax.fori_loop(0, elems // 16, shuffle, 0)
    order_copy.wait()

    def products(i, carry):
        for u in range(16):
            at = i * 16 + u
            e = order_ref[0, at]
            high, low = split_two(
                jnp.dot(own_ref[e][:, :PAD], rows_ref[e], preferred_element_type=F32)
            )
            g_ref[at, 0:PAD, :] = high
            g_ref[at, PAD : 2 * PAD, :] = low
        return carry

    lax.fori_loop(0, elems // 16, products, 0)

    me = lax.axis_index(axis)
    for o in range(count):
        first = lax.rem(me + (count - o), count) * members
        for g in range(members // SPLIT):
            for q, block in enumerate(spread(two_refs[o][g])):
                high, low = split_two(block)
                two_hi[first + g * SPLIT + q] = high
                two_lo[first + g * SPLIT + q] = low
    for i in range(members):
        high, low = split_two(turned2[i])
        r2_ref[i, 0:PAD, :] = high
        r2_ref[i, PAD : 2 * PAD, :] = low


def combine_kernel(axis, order_ref, nbr_ref, slot_ref, agg2_ref, nbr2_ref, slot2_ref, *refs):
    count = lax.axis_size(axis)
    faces, elems = nbr_ref.shape
    slots = nbr2_ref.shape[0]
    send_rows = len(refs) - (5 + 2 + count + 5)
    halo_refs = refs[:send_rows]
    own_ref, g_ref, two_hi, two_lo, r2_ref = refs[send_rows : send_rows + 5]
    one_refs = refs[send_rows + 5 : send_rows + 7]
    part_refs = refs[send_rows + 7 : send_rows + 7 + count]
    table, masks, acc0, acc1, own_sem = refs[send_rows + 7 + count :]
    halo = halo_refs[0].shape[0]
    members = agg2_ref.shape[0]
    own_copy = pltpu.make_async_copy(own_ref, table.at[pl.ds(0, elems)], own_sem.at[0])
    own_copy.start()
    set_masks(masks)
    for r in range(send_rows):

        def arrive(i, carry, r=r):
            for u in range(16):
                h = i * 16 + u
                table[elems + r * halo + h] = unpacked(halo_refs[r][h].astype(F32)).astype(HALF)
            return carry

        lax.fori_loop(0, halo // 16, arrive, 0)
    acc0[...] = jnp.zeros_like(acc0)
    acc1[...] = jnp.zeros_like(acc1)
    own_copy.wait()

    def placed(block, slot):
        return jnp.concatenate([masked(block, masks[slot * 2 + h]) for h in range(2)], axis=1)

    def gather(i2, carry):
        for v in range(2):
            i = i2 * 2 + v
            total = jnp.zeros((2 * PAD, 2 * LANES), F32)
            for u in range(PER_AGG):
                at = i * PER_AGG + u
                e = order_ref[0, at]
                rows = [placed(table[e], 0)]
                rows += [placed(table[nbr_ref[k, e]], slot_ref[k, e]) for k in range(faces)]
                total = total + jnp.dot(
                    g_ref[at][:, : (faces + 1) * PAD],
                    jnp.concatenate(rows, axis=0),
                    preferred_element_type=F32,
                )
            one = total[:PAD] + total[PAD:]
            for h in range(2):
                one_refs[h][i] = one[:, h * LANES : (h + 1) * LANES]
        return carry

    lax.fori_loop(0, members // 2, gather, 0)

    def second(i4, carry):
        for u in range(4):
            i = i4 * 4 + u
            one = jnp.concatenate([ref[i] for ref in one_refs], axis=1)
            high, low = split_two(one)
            at = [(nbr2_ref[j, i], slot2_ref[j, i]) for j in range(slots)]
            w = jnp.dot(
                jnp.concatenate([high, low], axis=0),
                jnp.concatenate([placed(two_hi[source], slot) for source, slot in at], axis=0),
                preferred_element_type=F32,
            )
            w_corrected = jnp.dot(
                high,
                jnp.concatenate([placed(two_lo[source], slot) for source, slot in at], axis=0),
                preferred_element_type=F32,
            )
            w_high, w_low = split_two((w[:PAD] + w[PAD:]) + w_corrected)
            r2 = r2_ref[i][:, :PAD]
            z = jnp.dot(r2, w_high, preferred_element_type=F32)
            z = (z[:PAD] + z[PAD:]) + jnp.dot(r2[:PAD], w_low, preferred_element_type=F32)
            to = agg2_ref[i]
            acc0[to] = acc0[to] + z[:, :LANES]
            acc1[to] = acc1[to] + z[:, LANES:]
        return carry

    lax.fori_loop(0, members // 4, second, 0)
    me = lax.axis_index(axis)
    owned = acc0.shape[0] // count
    for o in range(count):
        first = lax.rem(me + o, count) * owned
        for h, acc in enumerate((acc0, acc1)):
            for k in range(owned):
                part_refs[o][h, k] = acc[first + k]


def write_rows(out_ref, h, a, rows):
    order = out_ref.shape[1]
    for q in range(SPLIT):
        turned = rows if q == 0 else pltpu.roll(rows, LANES - q * PAD, axis=1)
        out_ref[h * SPLIT + q, a] = turned[:, :order]


def one_kernel(one0_ref, one1_ref, out_ref):
    _, order, members, _ = out_ref.shape
    for h, ref in enumerate((one0_ref, one1_ref)):
        for b in range(0, PAD, 8):
            groups = [
                jnp.swapaxes(ref[i : i + 8, b : b + 8, :], 0, 1) for i in range(0, members, 8)
            ]
            for u in range(min(8, order - b)):
                write_rows(out_ref, h, b + u, jnp.concatenate([x[u] for x in groups], axis=0))


def two_kernel(*refs):
    part_refs, out_ref = refs[:-1], refs[-1]
    _, order, owned, _ = out_ref.shape
    for h in range(2):
        value = part_refs[0][h]
        for ref in part_refs[1:]:
            value = value + ref[h]
        for a in range(order):
            write_rows(
                out_ref, h, a, jnp.concatenate([value[k, a : a + 1] for k in range(owned)], axis=0)
            )


def per_device(
    diag_block,
    face_block,
    restrict1,
    neighbour,
    face_slot,
    agg_map,
    send_list,
    restrict2,
    coarse_nbr,
    agg2_map,
    coarse_slot,
):
    order, _, elems = restrict1.shape
    faces = face_block.shape[0]
    send_rows, halo = send_list.shape
    reach = send_rows // 2
    slots = coarse_nbr.shape[0]
    members = elems // PER_AGG
    owned = members // PER_AGG
    count = lax.axis_size("sub")
    offsets = [r - reach if r < reach else r - reach + 1 for r in range(send_rows)]
    shape = jax.ShapeDtypeStruct
    maps2 = jnp.transpose(restrict2, (0, 2, 1))

    near = pltpu.VMEM
    params = pltpu.CompilerParams(vmem_limit_bytes=36 * 2**20)
    packed = pl.pallas_call(
        pack_kernel,
        name="pack",
        compiler_params=params,
        in_specs=[SMEM, VMEM, VMEM],
        out_specs=[VMEM] * (send_rows + 3),
        out_shape=[near((halo * PACK, LANES), HALF)] * send_rows
        + [
            near((members // SPLIT, PAD, LANES), F32),
            near((elems, PACK, LANES), F32),
            near((members, PAD, LANES), F32),
        ],
        scratch_shapes=[
            pltpu.VMEM((PAD, PAD, elems), F32),
            pltpu.VMEM((halo * PACK, LANES), F32),
            pltpu.VMEM((PAD, members, LANES), F32),
        ],
    )(send_list, restrict1, maps2)
    sends = packed[:send_rows]
    own2, own_rows, turned2 = packed[send_rows:]
    two = [own2] + [shifted(own2, "sub", o) for o in range(1, count)]
    arrived = [shifted(sends[r], "dom", -offset) for r, offset in enumerate(offsets)]

    table, g, order_list, two_hi, two_lo, r2 = pl.pallas_call(
        functools.partial(local_kernel, "sub"),
        name="local",
        compiler_params=params,
        in_specs=[VMEM] * (6 + count),
        out_specs=[VMEM, VMEM, SMEM, VMEM, VMEM, VMEM],
        out_shape=[
            near((elems, PAD, LANES), HALF),
            near((elems, 2 * PAD, 2 * LANES), HALF),
            shape((1, elems), jnp.int32),
            near((count * members, PAD, LANES), HALF),
            near((count * members, PAD, LANES), HALF),
            near((members, 2 * PAD, LANES), HALF),
        ],
        scratch_shapes=[
            pltpu.VMEM((4 * LANES, elems), HALF),
            pltpu.VMEM((PAD // 2, elems, LANES), F32),
            pltpu.VMEM((PAD // 2, elems, LANES), F32),
            pltpu.VMEM((elems, PAD, 2 * LANES), HALF),
            pltpu.VMEM((elems, PAD, LANES), HALF),
            pltpu.VMEM((1, elems), jnp.int32),
            pltpu.SemaphoreType.DMA((1,)),
        ],
        cost_estimate=pl.CostEstimate(
            flops=20_000_000_000, bytes_accessed=40_000_000, transcendentals=0
        ),
    )(agg_map[None], diag_block, face_block, restrict1, own_rows, turned2, *two)

    combined = pl.pallas_call(
        functools.partial(combine_kernel, "sub"),
        name="combine",
        compiler_params=params,
        in_specs=[SMEM] * 6 + [VMEM] * (send_rows + 5),
        out_specs=[VMEM] * (2 + count),
        out_shape=[near((members, PAD, LANES), F32)] * 2
        + [near((2, owned, PAD, LANES), F32)] * count,
        scratch_shapes=[
            pltpu.VMEM((elems + send_rows * halo, PAD, LANES), HALF),
            pltpu.VMEM((2 * SLOTS2, 8, LANES), HALF),
            pltpu.VMEM((count * owned, PAD, LANES), F32),
            pltpu.VMEM((count * owned, PAD, LANES), F32),
            pltpu.SemaphoreType.DMA((1,)),
        ],
    )(
        order_list,
        neighbour,
        face_slot,
        agg2_map,
        coarse_nbr,
        coarse_slot,
        *[block.reshape(halo, PACK, LANES) for block in arrived],
        table,
        g,
        two_hi,
        two_lo,
        r2,
    )
    one0, one1, parts = combined[0], combined[1], combined[2:]
    landed = [parts[0]] + [shifted(parts[o], "sub", o) for o in range(1, count)]
    coarse_one = pl.pallas_call(
        one_kernel,
        name="first",
        compiler_params=params,
        in_specs=[VMEM] * 2,
        out_specs=VMEM,
        out_shape=shape((slots, order, members, order), F32),
        cost_estimate=pl.CostEstimate(
            flops=2_000_000_000, bytes_accessed=4_000_000, transcendentals=0
        ),
    )(one0, one1)
    coarse_two = pl.pallas_call(
        two_kernel,
        name="second",
        compiler_params=params,
        in_specs=[VMEM] * count,
        out_specs=VMEM,
        out_shape=shape((SLOTS2, order, owned, order), F32),
    )(*landed)
    return (
        jnp.transpose(coarse_one, (0, 1, 3, 2)),
        jnp.transpose(coarse_two, (0, 1, 3, 2)),
    )


def solution(mesh):
    placed = (
        P(None, None, ("dom", "sub")),
        P(None, None, None, ("dom", "sub")),
        P(None, None, ("dom", "sub")),
        P(None, ("dom", "sub")),
        P(None, ("dom", "sub")),
        P(("dom", "sub")),
        P(None, ("dom", "sub")),
        P(None, None, ("dom", "sub")),
        P(None, ("dom", "sub")),
        P(("dom", "sub")),
        P(None, ("dom", "sub")),
    )
    return jax.shard_map(
        per_device,
        mesh=mesh,
        in_specs=placed,
        out_specs=(P(None, None, None, ("dom", "sub")), P(None, None, None, ("dom", "sub"))),
        check_vma=False,
    )
```

```python
import functools

import jax
import jax.numpy as jnp
from jax import lax
from jax.experimental import pallas as pl
from jax.experimental.pallas import tpu as pltpu
from jax.sharding import PartitionSpec as P

SLOTS2 = 8
PER_AGG = 8
PAD = 32
LANES = 128
SPLIT = LANES // PAD
PACK = PAD // SPLIT


F32 = jnp.float32
HALF = jnp.bfloat16

VMEM = pl.BlockSpec(memory_space=pltpu.VMEM)
SMEM = pl.BlockSpec(memory_space=pltpu.SMEM)
FAR = pl.BlockSpec(memory_space=pltpu.HBM)


def rounds(reach):
    found = []
    for offset in range(reach, 0, -1):
        level = (offset & -offset).bit_length() - 1
        found += [(offset, level, side) for side in range(2)]
    return found


def exchanged(shard, axis, this):
    count = lax.axis_size(axis)
    offset, level, side = this
    if count % (2 << level):
        raise ValueError("ring length")
    pairs = [
        (i, (i + offset if (i >> level) & 1 == side else i - offset) % count) for i in range(count)
    ]
    return lax.ppermute(shard, axis, pairs)


def far(array):
    return pltpu.with_memory_space_constraint(array, pltpu.HBM)


def listed(offset, reach):
    return offset + reach if offset < 0 else offset + reach - 1


def row_of(axis, this, reach, sending):
    offset, level, side = this
    ahead = ((lax.axis_index(axis) >> level) & 1) == side
    plus, minus = listed(offset, reach), listed(-offset, reach)
    return jnp.where(ahead, minus, plus) if sending else jnp.where(ahead, plus, minus)


def partner(me, k, count):
    if count & (count - 1):
        raise ValueError("subgroup size")
    return me ^ k


def swapped(shard, axis, k):
    count = lax.axis_size(axis)
    return lax.ppermute(shard, axis, [(i, partner(i, k, count)) for i in range(count)])


def spread(rows):
    block = lax.broadcasted_iota(jnp.int32, rows.shape, 1) // PAD
    turned = [rows] + [pltpu.roll(rows, PAD * q, axis=1) for q in range(1, SPLIT)]
    results = []
    for part in range(SPLIT):
        result = turned[(SPLIT - 1 - part) % SPLIT]
        for b in range(SPLIT - 1):
            result = jnp.where(block == b, turned[(b - part) % SPLIT], result)
        results.append(result)
    return results


def unpacked(packed):
    return jnp.concatenate(spread(packed), axis=0)


def split_two(value):
    high = value.astype(HALF)
    return high, (value - high.astype(F32)).astype(HALF)


def transposed_rows(maps_ref, padded, packed):
    order, _, elems = maps_ref.shape
    padded[...] = jnp.zeros_like(padded)
    for j in range(order):
        padded[j, :order, :] = maps_ref[j].astype(F32)
    rows = []
    for M in range(PACK):
        rows.append([])
    turned = [
        [jnp.swapaxes(padded[8 * b : 8 * b + 8, 8 * q : 8 * q + 8, :], 0, 1) for b in range(PAD // 8)]
        for q in range(SPLIT)
    ]
    packs = [
        jnp.concatenate([turned[q][b][M] for q in range(SPLIT) for b in range(PAD // 8)], axis=0).T
        for M in range(PACK)
    ]
    for e in range(0, elems, 8):
        group = jnp.stack([pack[e : e + 8, :] for pack in packs], axis=0)
        packed[e : e + 8] = jnp.swapaxes(group, 0, 1)


def padded_members(maps2_ref, padded, turned):
    order, members, _ = maps2_ref.shape
    padded[...] = jnp.zeros_like(padded)
    for d in range(order):
        padded[d, :, :order] = maps2_ref[d]
    for d in range(0, PAD, 8):
        for i in range(0, members, 8):
            turned[i : i + 8, d : d + 8, :] = jnp.swapaxes(padded[d : d + 8, i : i + 8, :], 0, 1)


def in_order(agg, elems):
    across = jnp.broadcast_to(agg, (elems, elems)).astype(F32)
    here = lax.broadcasted_iota(jnp.int32, (elems, elems), 0)
    there = lax.broadcasted_iota(jnp.int32, (elems, elems), 1)
    ahead = (across.T == across) & (here < there)
    rank = jnp.sum(jnp.where(ahead, 1.0, 0.0), axis=0, keepdims=True)
    place = jnp.broadcast_to(agg.astype(F32) * PER_AGG + rank, (elems, elems)).T
    found = jnp.where(place == there.astype(F32), here.astype(F32), 0.0)
    return jnp.sum(found, axis=0, keepdims=True).astype(jnp.int32)


def set_masks(masks):
    slots = masks.shape[0] // 2
    block = lax.broadcasted_iota(jnp.int32, (8, LANES), 1) // PAD
    for s in range(slots):
        for h in range(2):
            masks[s * 2 + h] = jnp.where(block + h * SPLIT == s, 1.0, 0.0).astype(HALF)


def masked(block, mask):
    return (block.reshape(PAD // 8, 8, LANES) * mask[None]).reshape(PAD, LANES)


def pack_kernel(axis, send_far, maps_far, maps2_far, *refs):
    send_rows, halo = send_far.shape
    out_refs, own2_ref, packed, turned2 = refs[:send_rows], *refs[send_rows : send_rows + 3]
    padded, flat, padded2, send_ref, maps_ref, maps2_ref, sems = refs[send_rows + 3 :]
    members = maps2_ref.shape[1]
    reach = send_rows // 2
    copies = [
        pltpu.make_async_copy(far, near, sems.at[i])
        for i, (far, near) in enumerate(
            ((maps_far, maps_ref), (send_far, send_ref), (maps2_far, maps2_ref))
        )
    ]
    for copy in copies:
        copy.start()
    copies[0].wait()
    transposed_rows(maps_ref, padded, packed)
    copies[1].wait()
    for m, this in enumerate(rounds(reach)):
        row = row_of(axis, this, reach, True)
        for h in range(halo):
            flat[h * PACK : (h + 1) * PACK, :] = packed[send_ref[row, h]]
        out_refs[m][...] = flat[...].astype(HALF)
    copies[2].wait()
    padded_members(maps2_ref, padded2, turned2)
    for g in range(members // SPLIT):
        group = turned2[g * SPLIT : (g + 1) * SPLIT].reshape(SPLIT * PAD, LANES)
        own2_ref[g] = group.T[:PAD]


def local_kernel(axis, agg_far, diag_far, face_far, maps_far, packed, turned2, *refs):
    count = lax.axis_size(axis)
    two_refs = refs[:count]
    table_ref, g_ref, order_ref, two_hi, two_lo, r2_ref = refs[count : count + 6]
    slab, left, right, rows_ref, own_ref, order_row, agg_ref, diag_ref, face_ref, maps_ref, sems = (
        refs[count + 6 :]
    )
    order, _, elems = maps_ref.shape
    faces = face_ref.shape[0]
    members = turned2.shape[0]
    copies = [
        pltpu.make_async_copy(far, near, sems.at[i])
        for i, (far, near) in enumerate(
            (
                (agg_far, agg_ref),
                (face_far, face_ref),
                (diag_far, diag_ref),
                (maps_far, maps_ref),
            )
        )
    ]
    for copy in copies:
        copy.start()

    def table(i, carry):
        for u in range(16):
            e = i * 16 + u
            table_ref[e] = unpacked(packed[e]).astype(HALF)
        return carry

    lax.fori_loop(0, elems // 16, table, 0)

    me = lax.axis_index(axis)
    for o in range(count):
        first = partner(me, o, count) * members
        for g in range(members // SPLIT):
            for q, block in enumerate(spread(two_refs[o][g])):
                high, low = split_two(block)
                two_hi[first + g * SPLIT + q] = high
                two_lo[first + g * SPLIT + q] = low
    copies[0].wait()
    order_row[...] = in_order(agg_ref[...], elems)
    order_copy = pltpu.make_async_copy(order_row, order_ref, sems.at[len(copies)])
    order_copy.start()

    slab[...] = jnp.zeros_like(slab)
    for copy in copies[1:]:
        copy.wait()
    tall = 2 * SPLIT * PAD
    for part in range(2):
        for rr in range(PAD // 2):
            r = part * (PAD // 2) + rr
            if r >= order:
                left[rr] = jnp.zeros((elems, LANES), F32)
                right[rr] = jnp.zeros((elems, LANES), F32)
                continue
            base = (r % 2) * tall
            sources = [diag_ref[r]] + [face_ref[k, r] for k in range(faces)] + [maps_ref[r]]
            for k, source in enumerate(sources):
                slab[base + k * PAD : base + k * PAD + order, :] = source
            turned = slab[base : base + tall, :].T.astype(F32)
            left[rr] = turned[:, :LANES]
            right[rr] = turned[:, LANES:]

        def shuffle(i, carry, part=part):
            for v in range(2):
                e = pl.multiple_of(i * 16 + v * 8, 8)
                for h, half in enumerate((left, right)):
                    top = jnp.swapaxes(half[0:8, pl.ds(e, 8), :], 0, 1)
                    low = jnp.swapaxes(half[8:16, pl.ds(e, 8), :], 0, 1)
                    for u in range(8):
                        both = jnp.concatenate([top[u], low[u]], axis=0)
                        to = slice(part * 16, part * 16 + 16)
                        rows_ref[e + u, to, h * LANES : (h + 1) * LANES] = both.astype(HALF)
                        if h == 1:
                            own_ref[e + u, to, :] = pltpu.roll(both, PAD, axis=1).astype(HALF)
            return carry

        lax.fori_loop(0, elems // 16, shuffle, 0)
    order_copy.wait()

    def products(i, carry):
        for u in range(16):
            at = i * 16 + u
            e = order_ref[0, at]
            high, low = split_two(
                jnp.dot(own_ref[e][:, :PAD], rows_ref[e], preferred_element_type=F32)
            )
            g_ref[at, 0:PAD, :] = high
            g_ref[at, PAD : 2 * PAD, :] = low
        return carry

    lax.fori_loop(0, elems // 16, products, 0)

    for i in range(members):
        high, low = split_two(turned2[i])
        r2_ref[i, 0:PAD, :] = high
        r2_ref[i, PAD : 2 * PAD, :] = low


def combine_kernel(axis, sub_axis, order_ref, nbr_ref, slot_ref, agg2_ref, nbr2_ref, slot2_ref, *refs):
    count = lax.axis_size(sub_axis)
    faces, elems = nbr_ref.shape
    slots = nbr2_ref.shape[0]
    send_rows = len(refs) - (5 + 2 + count + 5)
    halo_refs = refs[:send_rows]
    own_ref, g_ref, two_hi, two_lo, r2_ref = refs[send_rows : send_rows + 5]
    one_refs = refs[send_rows + 5 : send_rows + 7]
    part_refs = refs[send_rows + 7 : send_rows + 7 + count]
    table, masks, acc0, acc1, own_sem = refs[send_rows + 7 + count :]
    halo = halo_refs[0].shape[0]
    members = agg2_ref.shape[0]
    own_copy = pltpu.make_async_copy(own_ref, table.at[pl.ds(0, elems)], own_sem.at[0])
    own_copy.start()
    set_masks(masks)
    reach = send_rows // 2
    for m, this in enumerate(rounds(reach)):
        first = elems + row_of(axis, this, reach, False) * halo

        def arrive(i, carry, m=m, first=first):
            for u in range(16):
                h = i * 16 + u
                table[first + h] = unpacked(halo_refs[m][h].astype(F32)).astype(HALF)
            return carry

        lax.fori_loop(0, halo // 16, arrive, 0)
    acc0[...] = jnp.zeros_like(acc0)
    acc1[...] = jnp.zeros_like(acc1)
    own_copy.wait()

    def placed(block, slot):
        return jnp.concatenate([masked(block, masks[slot * 2 + h]) for h in range(2)], axis=1)

    def gather(i2, carry):
        for v in range(2):
            i = i2 * 2 + v
            total = jnp.zeros((2 * PAD, 2 * LANES), F32)
            for u in range(PER_AGG):
                at = i * PER_AGG + u
                e = order_ref[0, at]
                rows = [placed(table[e], 0)]
                rows += [placed(table[nbr_ref[k, e]], slot_ref[k, e]) for k in range(faces)]
                total = total + jnp.dot(
                    g_ref[at][:, : (faces + 1) * PAD],
                    jnp.concatenate(rows, axis=0),
                    preferred_element_type=F32,
                )
            one = total[:PAD] + total[PAD:]
            for h in range(2):
                one_refs[h][i] = one[:, h * LANES : (h + 1) * LANES]
        return carry

    lax.fori_loop(0, members // 2, gather, 0)

    def second(i4, carry):
        for u in range(4):
            i = i4 * 4 + u
            one = jnp.concatenate([ref[i] for ref in one_refs], axis=1)
            high, low = split_two(one)
            at = [(nbr2_ref[j, i], slot2_ref[j, i]) for j in range(slots)]
            w = jnp.dot(
                jnp.concatenate([high, low], axis=0),
                jnp.concatenate([placed(two_hi[source], slot) for source, slot in at], axis=0),
                preferred_element_type=F32,
            )
            w_corrected = jnp.dot(
                high,
                jnp.concatenate([placed(two_lo[source], slot) for source, slot in at], axis=0),
                preferred_element_type=F32,
            )
            w_high, w_low = split_two((w[:PAD] + w[PAD:]) + w_corrected)
            r2 = r2_ref[i][:, :PAD]
            z = jnp.dot(r2, w_high, preferred_element_type=F32)
            z = (z[:PAD] + z[PAD:]) + jnp.dot(r2[:PAD], w_low, preferred_element_type=F32)
            to = agg2_ref[i]
            acc0[to] = acc0[to] + z[:, :LANES]
            acc1[to] = acc1[to] + z[:, LANES:]
        return carry

    lax.fori_loop(0, members // 4, second, 0)
    me = lax.axis_index(sub_axis)
    owned = acc0.shape[0] // count
    for o in range(count):
        first = partner(me, o, count) * owned
        for h, acc in enumerate((acc0, acc1)):
            for k in range(owned):
                part_refs[o][h, k] = acc[first + k]


def write_rows(out_ref, h, a, rows):
    order = out_ref.shape[1]
    for q in range(SPLIT):
        turned = rows if q == 0 else pltpu.roll(rows, LANES - q * PAD, axis=1)
        out_ref[h * SPLIT + q, a] = turned[:, :order]


def one_kernel(one0_ref, one1_ref, out_ref):
    _, order, members, _ = out_ref.shape
    for h, ref in enumerate((one0_ref, one1_ref)):
        for b in range(0, PAD, 8):
            groups = [
                jnp.swapaxes(ref[i : i + 8, b : b + 8, :], 0, 1) for i in range(0, members, 8)
            ]
            for u in range(min(8, order - b)):
                write_rows(out_ref, h, b + u, jnp.concatenate([x[u] for x in groups], axis=0))


def two_kernel(*refs):
    part_refs, out_ref = refs[:-1], refs[-1]
    _, order, owned, _ = out_ref.shape
    for h in range(2):
        value = part_refs[0][h]
        for ref in part_refs[1:]:
            value = value + ref[h]
        for a in range(order):
            write_rows(
                out_ref, h, a, jnp.concatenate([value[k, a : a + 1] for k in range(owned)], axis=0)
            )


def per_device(
    diag_block,
    face_block,
    restrict1,
    neighbour,
    face_slot,
    agg_map,
    send_list,
    restrict2,
    coarse_nbr,
    agg2_map,
    coarse_slot,
):
    order, _, elems = restrict1.shape
    faces = face_block.shape[0]
    send_rows, halo = send_list.shape
    reach = send_rows // 2
    slots = coarse_nbr.shape[0]
    members = elems // PER_AGG
    owned = members // PER_AGG
    count = lax.axis_size("sub")
    shape = jax.ShapeDtypeStruct
    maps2 = jnp.transpose(restrict2, (0, 2, 1))

    near = pltpu.VMEM
    params = pltpu.CompilerParams(vmem_limit_bytes=36 * 2**20)
    packed = pl.pallas_call(
        functools.partial(pack_kernel, "dom"),
        name="pack",
        compiler_params=params,
        in_specs=[FAR] * 3,
        out_specs=[VMEM] * (send_rows + 3),
        out_shape=[near((halo * PACK, LANES), HALF)] * send_rows
        + [
            near((members // SPLIT, PAD, LANES), F32),
            near((elems, PACK, LANES), F32),
            near((members, PAD, LANES), F32),
        ],
        scratch_shapes=[
            pltpu.VMEM((PAD, PAD, elems), F32),
            pltpu.VMEM((halo * PACK, LANES), F32),
            pltpu.VMEM((PAD, members, LANES), F32),
            pltpu.SMEM(send_list.shape, jnp.int32),
            pltpu.VMEM(restrict1.shape, HALF),
            pltpu.VMEM(maps2.shape, F32),
            pltpu.SemaphoreType.DMA((3,)),
        ],
    )(*[far(x) for x in (send_list, restrict1, maps2)])
    sends = packed[:send_rows]
    own2, own_rows, turned2 = packed[send_rows:]
    two = [own2] + [swapped(own2, "sub", k) for k in range(1, count)]
    arrived = [exchanged(send, "dom", this) for send, this in zip(sends, rounds(reach))]

    table, g, order_list, two_hi, two_lo, r2 = pl.pallas_call(
        functools.partial(local_kernel, "sub"),
        name="local",
        compiler_params=params,
        in_specs=[FAR] * 4 + [VMEM] * (2 + count),
        out_specs=[VMEM, VMEM, SMEM, VMEM, VMEM, VMEM],
        out_shape=[
            near((elems, PAD, LANES), HALF),
            near((elems, 2 * PAD, 2 * LANES), HALF),
            shape((1, elems), jnp.int32),
            near((count * members, PAD, LANES), HALF),
            near((count * members, PAD, LANES), HALF),
            near((members, 2 * PAD, LANES), HALF),
        ],
        scratch_shapes=[
            pltpu.VMEM((4 * LANES, elems), HALF),
            pltpu.VMEM((PAD // 2, elems, LANES), F32),
            pltpu.VMEM((PAD // 2, elems, LANES), F32),
            pltpu.VMEM((elems, PAD, 2 * LANES), HALF),
            pltpu.VMEM((elems, PAD, LANES), HALF),
            pltpu.VMEM((1, elems), jnp.int32),
            pltpu.VMEM((1, elems), jnp.int32),
            pltpu.VMEM(diag_block.shape, HALF),
            pltpu.VMEM(face_block.shape, HALF),
            pltpu.VMEM(restrict1.shape, HALF),
            pltpu.SemaphoreType.DMA((5,)),
        ],
        cost_estimate=pl.CostEstimate(
            flops=20_000_000_000, bytes_accessed=40_000_000, transcendentals=0
        ),
    )(
        *[far(x) for x in (agg_map[None], diag_block, face_block, restrict1)],
        own_rows,
        turned2,
        *two,
    )

    combined = pl.pallas_call(
        functools.partial(combine_kernel, "dom", "sub"),
        name="combine",
        compiler_params=params,
        in_specs=[SMEM] * 6 + [VMEM] * (send_rows + 5),
        out_specs=[VMEM] * (2 + count),
        out_shape=[near((members, PAD, LANES), F32)] * 2
        + [near((2, owned, PAD, LANES), F32)] * count,
        scratch_shapes=[
            pltpu.VMEM((elems + send_rows * halo, PAD, LANES), HALF),
            pltpu.VMEM((2 * SLOTS2, 8, LANES), HALF),
            pltpu.VMEM((count * owned, PAD, LANES), F32),
            pltpu.VMEM((count * owned, PAD, LANES), F32),
            pltpu.SemaphoreType.DMA((1,)),
        ],
    )(
        order_list,
        neighbour,
        face_slot,
        agg2_map,
        coarse_nbr,
        coarse_slot,
        *[block.reshape(halo, PACK, LANES) for block in arrived],
        table,
        g,
        two_hi,
        two_lo,
        r2,
    )
    one0, one1, parts = combined[0], combined[1], combined[2:]
    landed = [parts[0]] + [swapped(parts[k], "sub", k) for k in range(1, count)]
    coarse_one = pl.pallas_call(
        one_kernel,
        name="first",
        compiler_params=params,
        in_specs=[VMEM] * 2,
        out_specs=VMEM,
        out_shape=shape((slots, order, members, order), F32),
        cost_estimate=pl.CostEstimate(
            flops=2_000_000_000, bytes_accessed=4_000_000, transcendentals=0
        ),
    )(one0, one1)
    coarse_two = pl.pallas_call(
        two_kernel,
        name="second",
        compiler_params=params,
        in_specs=[VMEM] * count,
        out_specs=VMEM,
        out_shape=shape((SLOTS2, order, owned, order), F32),
    )(*landed)
    return (
        jnp.transpose(coarse_one, (0, 1, 3, 2)),
        jnp.transpose(coarse_two, (0, 1, 3, 2)),
    )


def solution(mesh):
    placed = (
        P(None, None, ("dom", "sub")),
        P(None, None, None, ("dom", "sub")),
        P(None, None, ("dom", "sub")),
        P(None, ("dom", "sub")),
        P(None, ("dom", "sub")),
        P(("dom", "sub")),
        P(None, ("dom", "sub")),
        P(None, None, ("dom", "sub")),
        P(None, ("dom", "sub")),
        P(("dom", "sub")),
        P(None, ("dom", "sub")),
    )
    return jax.shard_map(
        per_device,
        mesh=mesh,
        in_specs=placed,
        out_specs=(P(None, None, None, ("dom", "sub")), P(None, None, None, ("dom", "sub"))),
        check_vma=False,
    )
```

```python
import functools

import jax
import jax.numpy as jnp
from jax import lax
from jax.experimental import pallas as pl
from jax.experimental.pallas import tpu as pltpu
from jax.sharding import PartitionSpec as P

SLOTS2 = 8
PER_AGG = 8
PAD = 32
LANES = 128
SPLIT = LANES // PAD
PACK = PAD // SPLIT


F32 = jnp.float32
HALF = jnp.bfloat16

VMEM = pl.BlockSpec(memory_space=pltpu.VMEM)
SMEM = pl.BlockSpec(memory_space=pltpu.SMEM)
ANY = pl.BlockSpec(memory_space=pl.ANY)
FAR = pl.BlockSpec(memory_space=pltpu.HBM)


def rounds(reach):
    sides = [(offset, side) for side in (1, 0) for offset in range(1, reach + 1)]
    if reach == 3:
        sides = [(3, 1), (2, 1), (1, 1), (3, 0), (1, 0), (2, 0)]
    return [(offset, (offset & -offset).bit_length() - 1, side) for offset, side in sides]


def across(index, this, count):
    offset, level, side = this
    if count % (2 << level):
        raise ValueError("ring length")
    return (index + offset if (index >> level) & 1 == side else index - offset) % count


def exchanged(shard, axis, sub_axis, pair_rounds):
    count, members = lax.axis_size(axis), lax.axis_size(sub_axis)
    pairs = [
        (d * members + s, across(d, pair_rounds[s & 1], count) * members + s)
        for d in range(count)
        for s in range(members)
    ]
    return lax.ppermute(shard, (axis, sub_axis), pairs)


def far(array):
    return pltpu.with_memory_space_constraint(array, pltpu.HBM)


def listed(offset, reach):
    return offset + reach if offset < 0 else offset + reach - 1


def row_of(axis, this, reach, sending):
    offset, level, side = this
    ahead = ((lax.axis_index(axis) >> level) & 1) == side
    plus, minus = listed(offset, reach), listed(-offset, reach)
    return jnp.where(ahead, minus, plus) if sending else jnp.where(ahead, plus, minus)


def row_of_pair(axis, sub_axis, pair_rounds, reach, sending, mine):
    first = (lax.axis_index(sub_axis) & 1) == (0 if mine else 1)
    rows = [row_of(axis, this, reach, sending) for this in pair_rounds]
    return jnp.where(first, rows[0], rows[1])


def partner(me, k, count):
    if count != 4:
        raise ValueError("subgroup size")
    return me ^ k


def swapped(shard, axis, k):
    count = lax.axis_size(axis)
    return lax.ppermute(shard, axis, [(i, partner(i, k, count)) for i in range(count)])


def spread(rows):
    block = lax.broadcasted_iota(jnp.int32, rows.shape, 1) // PAD
    turned = [rows] + [pltpu.roll(rows, PAD * q, axis=1) for q in range(1, SPLIT)]
    results = []
    for part in range(SPLIT):
        result = turned[(SPLIT - 1 - part) % SPLIT]
        for b in range(SPLIT - 1):
            result = jnp.where(block == b, turned[(b - part) % SPLIT], result)
        results.append(result)
    return results


def unpacked(packed):
    return jnp.concatenate(spread(packed), axis=0)


def split_two(value):
    high = value.astype(HALF)
    return high, (value - high.astype(F32)).astype(HALF)


def transposed_rows(maps_ref, padded, packed):
    order, _, elems = maps_ref.shape
    padded[...] = jnp.zeros_like(padded)
    for j in range(order):
        padded[j, :order, :] = maps_ref[j].astype(F32)
    rows = []
    for M in range(PACK):
        rows.append([])
    turned = [
        [jnp.swapaxes(padded[8 * b : 8 * b + 8, 8 * q : 8 * q + 8, :], 0, 1) for b in range(PAD // 8)]
        for q in range(SPLIT)
    ]
    packs = [
        jnp.concatenate([turned[q][b][M] for q in range(SPLIT) for b in range(PAD // 8)], axis=0).T
        for M in range(PACK)
    ]
    for e in range(0, elems, 8):
        group = jnp.stack([pack[e : e + 8, :] for pack in packs], axis=0)
        packed[e : e + 8] = jnp.swapaxes(group, 0, 1)


def padded_members(maps2_ref, padded, turned):
    order, members, _ = maps2_ref.shape
    padded[...] = jnp.zeros_like(padded)
    for d in range(order):
        padded[d, :, :order] = maps2_ref[d]
    for d in range(0, PAD, 8):
        for i in range(0, members, 8):
            turned[i : i + 8, d : d + 8, :] = jnp.swapaxes(padded[d : d + 8, i : i + 8, :], 0, 1)


def in_order(agg, elems):
    across = jnp.broadcast_to(agg, (elems, elems)).astype(F32)
    here = lax.broadcasted_iota(jnp.int32, (elems, elems), 0)
    there = lax.broadcasted_iota(jnp.int32, (elems, elems), 1)
    ahead = (across.T == across) & (here < there)
    rank = jnp.sum(jnp.where(ahead, 1.0, 0.0), axis=0, keepdims=True)
    place = jnp.broadcast_to(agg.astype(F32) * PER_AGG + rank, (elems, elems)).T
    found = jnp.where(place == there.astype(F32), here.astype(F32), 0.0)
    return jnp.sum(found, axis=0, keepdims=True).astype(jnp.int32)


def set_masks(masks):
    slots = masks.shape[0] // 2
    block = lax.broadcasted_iota(jnp.int32, (8, LANES), 1) // PAD
    for s in range(slots):
        for h in range(2):
            masks[s * 2 + h] = jnp.where(block + h * SPLIT == s, 1.0, 0.0).astype(HALF)


def masked(block, mask):
    return (block.reshape(PAD // 8, 8, LANES) * mask[None]).reshape(PAD, LANES)


def pack_kernel(axis, sub_axis, send_far, maps_far, maps2_far, *refs):
    keep_ref, give_ref, packed, turned2 = refs[:4]
    padded, flat, padded2, send_ref, maps_ref, maps2_ref, sems = refs[4:]
    send_rows, halo = send_far.shape
    members = maps2_ref.shape[1]
    reach = send_rows // 2
    copies = [
        pltpu.make_async_copy(far, near, sems.at[i])
        for i, (far, near) in enumerate(
            ((maps_far, maps_ref), (send_far, send_ref), (maps2_far, maps2_ref))
        )
    ]
    for copy in copies:
        copy.start()
    copies[0].wait()
    transposed_rows(maps_ref, padded, packed)
    copies[1].wait()
    every = rounds(reach)
    for t in range(reach):
        for mine, out in ((False, give_ref), (True, keep_ref)):
            row = row_of_pair(axis, sub_axis, every[2 * t : 2 * t + 2], reach, True, mine)
            for h in range(halo):
                flat[h * PACK : (h + 1) * PACK, :] = packed[send_ref[row, h]]
            out[t] = flat[...].astype(HALF)
    copies[2].wait()
    padded_members(maps2_ref, padded2, turned2)
    groups = members // SPLIT
    for g in range(groups):
        group = turned2[g * SPLIT : (g + 1) * SPLIT].reshape(SPLIT * PAD, LANES)
        high, low = split_two(group.T[:PAD])
        give_ref[reach, g * PAD : (g + 1) * PAD, :] = high
        give_ref[reach, (groups + g) * PAD : (groups + g + 1) * PAD, :] = low


def join_kernel(keep_ref, own_ref, got_ref, *out_refs):
    reach = keep_ref.shape[0]
    for t, out in enumerate(out_refs):
        rows = got_ref.shape[1]
        out[:rows, :] = keep_ref[t] if t < reach else own_ref[reach]
        out[rows:, :] = got_ref[t]


def part_kernel(*refs):
    rows = refs[-1].shape[1]
    for t, ref in enumerate(refs[1:-1]):
        refs[-1][t] = ref[rows:, :]


def rows_kernel(agg_far, diag_far, face_far, maps_far, packed, turned2, after, *refs):
    table_ref, rows_ref, own_ref, order_ref, r2_ref = refs[:5]
    slab, left, right, agg_ref, diag_ref, face_ref, maps_ref, order_row, sems = refs[5:]
    order, _, elems = maps_ref.shape
    faces = face_ref.shape[0]
    copies = [
        pltpu.make_async_copy(far, near, sems.at[i])
        for i, (far, near) in enumerate(
            ((agg_far, agg_ref), (face_far, face_ref), (diag_far, diag_ref), (maps_far, maps_ref))
        )
    ]
    for copy in copies:
        copy.start()

    def table(i, carry):
        for u in range(16):
            e = i * 16 + u
            table_ref[e] = unpacked(packed[e]).astype(HALF)
        return carry

    lax.fori_loop(0, elems // 16, table, 0)
    for i in range(turned2.shape[0]):
        high, low = split_two(turned2[i])
        r2_ref[i, 0:PAD, :] = high
        r2_ref[i, PAD : 2 * PAD, :] = low
    copies[0].wait()
    order_row[...] = in_order(agg_ref[...], elems)
    order_copy = pltpu.make_async_copy(order_row, order_ref, sems.at[len(copies)])
    order_copy.start()
    for copy in copies[1:]:
        copy.wait()
    slab[...] = jnp.zeros_like(slab)
    tall = 2 * SPLIT * PAD
    for part in range(2):
        for rr in range(PAD // 2):
            r = part * (PAD // 2) + rr
            if r >= order:
                left[rr] = jnp.zeros((elems, LANES), F32)
                right[rr] = jnp.zeros((elems, LANES), F32)
                continue
            base = (r % 2) * tall
            sources = [diag_ref[r]] + [face_ref[k, r] for k in range(faces)] + [maps_ref[r]]
            for k, source in enumerate(sources):
                slab[base + k * PAD : base + k * PAD + order, :] = source
            turned = slab[base : base + tall, :].T.astype(F32)
            left[rr] = turned[:, :LANES]
            right[rr] = turned[:, LANES:]

        def shuffle(i, carry, part=part):
            for v in range(2):
                e = pl.multiple_of(i * 16 + v * 8, 8)
                for h, half in enumerate((left, right)):
                    top = jnp.swapaxes(half[0:8, pl.ds(e, 8), :], 0, 1)
                    low = jnp.swapaxes(half[8:16, pl.ds(e, 8), :], 0, 1)
                    for u in range(8):
                        both = jnp.concatenate([top[u], low[u]], axis=0)
                        to = slice(part * 16, part * 16 + 16)
                        rows_ref[e + u, to, h * LANES : (h + 1) * LANES] = both.astype(HALF)
                        if h == 1:
                            own_ref[e + u, to, :] = pltpu.roll(both, PAD, axis=1).astype(HALF)
            return carry

        lax.fori_loop(0, elems // 16, shuffle, 0)
    order_copy.wait()


def local_kernel(axis, order_ref, rows_ref, own_ref, mine_ref, mate_ref, other_ref, after, *refs):
    g_ref, two_hi, two_lo = refs
    count = lax.axis_size(axis)
    elems = rows_ref.shape[0]
    members = two_hi.shape[0] // count
    groups = members // SPLIT

    def products(i, carry):
        for u in range(16):
            at = i * 16 + u
            e = order_ref[0, at]
            high, low = split_two(
                jnp.dot(own_ref[e][:, :PAD], rows_ref[e], preferred_element_type=F32)
            )
            g_ref[at, 0:PAD, :] = high
            g_ref[at, PAD : 2 * PAD, :] = low
        return carry

    lax.fori_loop(0, elems // 16, products, 0)

    me = lax.axis_index(axis)
    last = mine_ref.shape[0] - 1
    tall = mine_ref.shape[1]
    for k in range(count):
        first = partner(me, k, count) * members
        for which, two in enumerate((two_hi, two_lo)):
            for g in range(groups):
                start = (which * groups + g) * PAD
                if k < 2:
                    rows = (mine_ref, mate_ref)[k][last, start : start + PAD, :]
                else:
                    start += (k - 2) * tall
                    rows = other_ref[start : start + PAD, :]
                for q, block in enumerate(spread(rows.astype(F32))):
                    two[first + g * SPLIT + q] = block.astype(HALF)


def combine_kernel(axis, sub_axis, order_ref, nbr_ref, slot_ref, agg2_ref, nbr2_ref, slot2_ref, *refs):
    count = lax.axis_size(sub_axis)
    faces, elems = nbr_ref.shape
    slots = nbr2_ref.shape[0]
    reach = len(refs) - (6 + 2 + count + 5)
    far_refs, post_ref = refs[:reach], refs[reach]
    own_ref, g_ref, two_hi, two_lo, r2_ref = refs[reach + 1 : reach + 6]
    one_refs = refs[reach + 6 : reach + 8]
    part_refs = refs[reach + 8 : reach + 8 + count]
    table, masks, acc0, acc1, own_sem = refs[reach + 8 + count :]
    halo = post_ref.shape[1]
    members = agg2_ref.shape[0]
    own_copy = pltpu.make_async_copy(own_ref, table.at[pl.ds(0, elems)], own_sem.at[0])
    own_copy.start()
    set_masks(masks)
    every = rounds(reach)
    for t in range(reach):
        for mine in (True, False):
            row = row_of_pair(axis, sub_axis, every[2 * t : 2 * t + 2], reach, False, mine)
            first = elems + row * halo

            def arrive(i, carry, t=t, mine=mine, first=first):
                for u in range(16):
                    h = i * 16 + u
                    packed = far_refs[t][h] if mine else post_ref[t, h]
                    table[first + h] = unpacked(packed.astype(F32)).astype(HALF)
                return carry

            lax.fori_loop(0, halo // 16, arrive, 0)
    acc0[...] = jnp.zeros_like(acc0)
    acc1[...] = jnp.zeros_like(acc1)
    own_copy.wait()

    def placed(block, slot):
        return jnp.concatenate([masked(block, masks[slot * 2 + h]) for h in range(2)], axis=1)

    def gather(i2, carry):
        for v in range(2):
            i = i2 * 2 + v
            total = jnp.zeros((2 * PAD, 2 * LANES), F32)
            for u in range(PER_AGG):
                at = i * PER_AGG + u
                e = order_ref[0, at]
                rows = [placed(table[e], 0)]
                rows += [placed(table[nbr_ref[k, e]], slot_ref[k, e]) for k in range(faces)]
                total = total + jnp.dot(
                    g_ref[at][:, : (faces + 1) * PAD],
                    jnp.concatenate(rows, axis=0),
                    preferred_element_type=F32,
                )
            one = total[:PAD] + total[PAD:]
            for h in range(2):
                one_refs[h][i] = one[:, h * LANES : (h + 1) * LANES]
        return carry

    lax.fori_loop(0, members // 2, gather, 0)

    def second(i4, carry):
        for u in range(4):
            i = i4 * 4 + u
            one = jnp.concatenate([ref[i] for ref in one_refs], axis=1)
            high, low = split_two(one)
            at = [(nbr2_ref[j, i], slot2_ref[j, i]) for j in range(slots)]
            w = jnp.dot(
                jnp.concatenate([high, low], axis=0),
                jnp.concatenate([placed(two_hi[source], slot) for source, slot in at], axis=0),
                preferred_element_type=F32,
            )
            w_corrected = jnp.dot(
                high,
                jnp.concatenate([placed(two_lo[source], slot) for source, slot in at], axis=0),
                preferred_element_type=F32,
            )
            w_high, w_low = split_two((w[:PAD] + w[PAD:]) + w_corrected)
            r2 = r2_ref[i][:, :PAD]
            z = jnp.dot(r2, w_high, preferred_element_type=F32)
            z = (z[:PAD] + z[PAD:]) + jnp.dot(r2[:PAD], w_low, preferred_element_type=F32)
            to = agg2_ref[i]
            acc0[to] = acc0[to] + z[:, :LANES]
            acc1[to] = acc1[to] + z[:, LANES:]
        return carry

    lax.fori_loop(0, members // 4, second, 0)
    me = lax.axis_index(sub_axis)
    owned = acc0.shape[0] // count
    for o in range(count):
        first = partner(me, o, count) * owned
        for h, acc in enumerate((acc0, acc1)):
            for k in range(owned):
                part_refs[o][h, k] = acc[first + k]


def write_rows(out_ref, h, a, rows):
    order = out_ref.shape[1]
    for q in range(SPLIT):
        turned = rows if q == 0 else pltpu.roll(rows, LANES - q * PAD, axis=1)
        out_ref[h * SPLIT + q, a] = turned[:, :order]


def one_kernel(one0_ref, one1_ref, out_ref):
    _, order, members, _ = out_ref.shape
    for h, ref in enumerate((one0_ref, one1_ref)):
        for b in range(0, PAD, 8):
            groups = [
                jnp.swapaxes(ref[i : i + 8, b : b + 8, :], 0, 1) for i in range(0, members, 8)
            ]
            for u in range(min(8, order - b)):
                write_rows(out_ref, h, b + u, jnp.concatenate([x[u] for x in groups], axis=0))


def two_kernel(*refs):
    part_refs, out_ref = refs[:-1], refs[-1]
    _, order, owned, _ = out_ref.shape
    for h in range(2):
        value = part_refs[0][h]
        for ref in part_refs[1:]:
            value = value + ref[h]
        for a in range(order):
            write_rows(
                out_ref, h, a, jnp.concatenate([value[k, a : a + 1] for k in range(owned)], axis=0)
            )


def per_device(
    diag_block,
    face_block,
    restrict1,
    neighbour,
    face_slot,
    agg_map,
    send_list,
    restrict2,
    coarse_nbr,
    agg2_map,
    coarse_slot,
):
    order, _, elems = restrict1.shape
    faces = face_block.shape[0]
    send_rows, halo = send_list.shape
    reach = send_rows // 2
    slots = coarse_nbr.shape[0]
    members = elems // PER_AGG
    owned = members // PER_AGG
    count = lax.axis_size("sub")
    shape = jax.ShapeDtypeStruct
    maps2 = jnp.transpose(restrict2, (0, 2, 1))

    near = pltpu.VMEM
    params = pltpu.CompilerParams(vmem_limit_bytes=36 * 2**20)
    tall = halo * PACK

    def call(kernel, name, in_specs, out_specs, out_shape, scratch, work):
        return pl.pallas_call(
            kernel,
            name=name,
            compiler_params=params,
            in_specs=in_specs,
            out_specs=out_specs,
            out_shape=out_shape,
            scratch_shapes=scratch,
            cost_estimate=pl.CostEstimate(
                flops=work * 1_000_000, bytes_accessed=work * 2_000, transcendentals=0
            ),
        )

    keep, give, own_rows, turned2 = call(
        functools.partial(pack_kernel, "dom", "sub"),
        "pack",
        [FAR] * 3,
        [VMEM] * 4,
        [
            near((reach, tall, LANES), HALF),
            near((reach + 1, tall, LANES), HALF),
            near((elems, PACK, LANES), F32),
            near((members, PAD, LANES), F32),
        ],
        [
            pltpu.VMEM((PAD, PAD, elems), F32),
            pltpu.VMEM((tall, LANES), F32),
            pltpu.VMEM((PAD, members, LANES), F32),
            pltpu.SMEM(send_list.shape, jnp.int32),
            pltpu.VMEM(restrict1.shape, HALF),
            pltpu.VMEM(maps2.shape, F32),
            pltpu.SemaphoreType.DMA((3,)),
        ],
        1000,
    )(*[far(x) for x in (send_list, restrict1, maps2)])
    if 2 * members * PAD // SPLIT != tall:
        raise ValueError("payload rows")
    got = swapped(give, "sub", 1)
    joined = call(
        join_kernel,
        "join",
        [VMEM] * 3,
        [VMEM] * (reach + 1),
        [near((2 * tall, LANES), HALF)] * (reach + 1),
        [],
        300,
    )(keep, give, got)
    other = swapped(joined[reach], "sub", 2)
    every = rounds(reach)
    arrived = [
        exchanged(joined[t], "dom", "sub", every[2 * t : 2 * t + 2]) for t in range(reach)
    ]
    table, rows, own, order_list, r2 = call(
        rows_kernel,
        "rows",
        [FAR] * 4 + [VMEM, VMEM, ANY],
        [VMEM] * 3 + [SMEM, VMEM],
        [
            near((elems, PAD, LANES), HALF),
            near((elems, PAD, 2 * LANES), HALF),
            near((elems, PAD, LANES), HALF),
            shape((1, elems), jnp.int32),
            near((members, 2 * PAD, LANES), HALF),
        ],
        [
            pltpu.VMEM((4 * LANES, elems), HALF),
            pltpu.VMEM((PAD // 2, elems, LANES), F32),
            pltpu.VMEM((PAD // 2, elems, LANES), F32),
            pltpu.VMEM((1, elems), jnp.int32),
            pltpu.VMEM(diag_block.shape, HALF),
            pltpu.VMEM(face_block.shape, HALF),
            pltpu.VMEM(restrict1.shape, HALF),
            pltpu.VMEM((1, elems), jnp.int32),
            pltpu.SemaphoreType.DMA((5,)),
        ],
        8000,
    )(
        *[far(x) for x in (agg_map[None], diag_block, face_block, restrict1)],
        own_rows,
        turned2,
        joined[0],
    )
    post = call(
        part_kernel,
        "part",
        [ANY] + [VMEM] * reach,
        VMEM,
        near((reach, tall, LANES), HALF),
        [],
        300,
    )(own, *arrived)
    landed_post = swapped(post, "sub", 1)
    g, two_hi, two_lo = call(
        functools.partial(local_kernel, "sub"),
        "local",
        [SMEM] + [VMEM] * 5 + [ANY],
        [VMEM] * 3,
        [
            near((elems, 2 * PAD, 2 * LANES), HALF),
            near((count * members, PAD, LANES), HALF),
            near((count * members, PAD, LANES), HALF),
        ],
        [],
        2000,
    )(order_list, rows, own, give, got, other, post)

    combined = pl.pallas_call(
        functools.partial(combine_kernel, "dom", "sub"),
        name="combine",
        compiler_params=params,
        in_specs=[SMEM] * 6 + [VMEM] * (reach + 6),
        out_specs=[VMEM] * (2 + count),
        out_shape=[near((members, PAD, LANES), F32)] * 2
        + [near((2, owned, PAD, LANES), F32)] * count,
        scratch_shapes=[
            pltpu.VMEM((elems + send_rows * halo, PAD, LANES), HALF),
            pltpu.VMEM((2 * SLOTS2, 8, LANES), HALF),
            pltpu.VMEM((count * owned, PAD, LANES), F32),
            pltpu.VMEM((count * owned, PAD, LANES), F32),
            pltpu.SemaphoreType.DMA((1,)),
        ],
    )(
        order_list,
        neighbour,
        face_slot,
        agg2_map,
        coarse_nbr,
        coarse_slot,
        *[block.reshape(2 * halo, PACK, LANES) for block in arrived],
        landed_post.reshape(reach, halo, PACK, LANES),
        table,
        g,
        two_hi,
        two_lo,
        r2,
    )
    one0, one1, parts = combined[0], combined[1], combined[2:]
    landed = [parts[0]] + [swapped(parts[k], "sub", k) for k in range(1, count)]
    coarse_one = pl.pallas_call(
        one_kernel,
        name="first",
        compiler_params=params,
        in_specs=[VMEM] * 2,
        out_specs=VMEM,
        out_shape=shape((slots, order, members, order), F32),
        cost_estimate=pl.CostEstimate(
            flops=2_000_000_000, bytes_accessed=4_000_000, transcendentals=0
        ),
    )(one0, one1)
    coarse_two = pl.pallas_call(
        two_kernel,
        name="second",
        compiler_params=params,
        in_specs=[VMEM] * count,
        out_specs=VMEM,
        out_shape=shape((SLOTS2, order, owned, order), F32),
    )(*landed)
    return (
        jnp.transpose(coarse_one, (0, 1, 3, 2)),
        jnp.transpose(coarse_two, (0, 1, 3, 2)),
    )


def solution(mesh):
    placed = (
        P(None, None, ("dom", "sub")),
        P(None, None, None, ("dom", "sub")),
        P(None, None, ("dom", "sub")),
        P(None, ("dom", "sub")),
        P(None, ("dom", "sub")),
        P(("dom", "sub")),
        P(None, ("dom", "sub")),
        P(None, None, ("dom", "sub")),
        P(None, ("dom", "sub")),
        P(("dom", "sub")),
        P(None, ("dom", "sub")),
    )
    return jax.shard_map(
        per_device,
        mesh=mesh,
        in_specs=placed,
        out_specs=(P(None, None, None, ("dom", "sub")), P(None, None, None, ("dom", "sub"))),
        check_vma=False,
    )
```

```python
import functools

import jax
import jax.numpy as jnp
from jax import lax
from jax.experimental import pallas as pl
from jax.experimental.pallas import tpu as pltpu
from jax.sharding import PartitionSpec as P

SLOTS2 = 8
PER_AGG = 8
PAD = 32
LANES = 128
SPLIT = LANES // PAD
PACK = PAD // SPLIT


F32 = jnp.float32
HALF = jnp.bfloat16

VMEM = pl.BlockSpec(memory_space=pltpu.VMEM)
SMEM = pl.BlockSpec(memory_space=pltpu.SMEM)
ANY = pl.BlockSpec(memory_space=pl.ANY)
FAR = pl.BlockSpec(memory_space=pltpu.HBM)


def rounds(reach):
    sides = [(offset, side) for side in (1, 0) for offset in range(1, reach + 1)]
    if reach == 3:
        sides = [(3, 1), (2, 1), (1, 1), (3, 0), (1, 0), (2, 0)]
    return [(offset, (offset & -offset).bit_length() - 1, side) for offset, side in sides]


def across(index, this, count):
    offset, level, side = this
    if count % (2 << level):
        raise ValueError("ring length")
    return (index + offset if (index >> level) & 1 == side else index - offset) % count


def exchanged(shard, axis, sub_axis, pair_rounds):
    count, members = lax.axis_size(axis), lax.axis_size(sub_axis)
    pairs = [
        (d * members + s, across(d, pair_rounds[s & 1], count) * members + s)
        for d in range(count)
        for s in range(members)
    ]
    return lax.ppermute(shard, (axis, sub_axis), pairs)


def far(array):
    return pltpu.with_memory_space_constraint(array, pltpu.HBM)


def listed(offset, reach):
    return offset + reach if offset < 0 else offset + reach - 1


def row_of(axis, this, reach, sending):
    offset, level, side = this
    ahead = ((lax.axis_index(axis) >> level) & 1) == side
    plus, minus = listed(offset, reach), listed(-offset, reach)
    return jnp.where(ahead, minus, plus) if sending else jnp.where(ahead, plus, minus)


def row_of_pair(axis, sub_axis, pair_rounds, reach, sending, mine):
    first = (lax.axis_index(sub_axis) & 1) == (0 if mine else 1)
    rows = [row_of(axis, this, reach, sending) for this in pair_rounds]
    return jnp.where(first, rows[0], rows[1])


def partner(me, k, count):
    if count != 4:
        raise ValueError("subgroup size")
    return me ^ k


def swapped(shard, axis, k):
    count = lax.axis_size(axis)
    return lax.ppermute(shard, axis, [(i, partner(i, k, count)) for i in range(count)])


def spread(rows):
    block = lax.broadcasted_iota(jnp.int32, rows.shape, 1) // PAD
    turned = [rows] + [pltpu.roll(rows, PAD * q, axis=1) for q in range(1, SPLIT)]
    results = []
    for part in range(SPLIT):
        result = turned[(SPLIT - 1 - part) % SPLIT]
        for b in range(SPLIT - 1):
            result = jnp.where(block == b, turned[(b - part) % SPLIT], result)
        results.append(result)
    return results


def unpacked(packed):
    return jnp.concatenate(spread(packed), axis=0)


def split_two(value):
    high = value.astype(HALF)
    return high, (value - high.astype(F32)).astype(HALF)


def transposed_rows(maps_ref, padded, packed):
    order, _, elems = maps_ref.shape
    padded[...] = jnp.zeros_like(padded)
    for j in range(order):
        padded[j, :order, :] = maps_ref[j].astype(F32)
    rows = []
    for M in range(PACK):
        rows.append([])
    turned = [
        [jnp.swapaxes(padded[8 * b : 8 * b + 8, 8 * q : 8 * q + 8, :], 0, 1) for b in range(PAD // 8)]
        for q in range(SPLIT)
    ]
    packs = [
        jnp.concatenate([turned[q][b][M] for q in range(SPLIT) for b in range(PAD // 8)], axis=0).T
        for M in range(PACK)
    ]
    for e in range(0, elems, 8):
        group = jnp.stack([pack[e : e + 8, :] for pack in packs], axis=0)
        packed[e : e + 8] = jnp.swapaxes(group, 0, 1)


def padded_members(maps2_ref, padded, turned):
    order, members, _ = maps2_ref.shape
    padded[...] = jnp.zeros_like(padded)
    for d in range(order):
        padded[d, :, :order] = maps2_ref[d]
    for d in range(0, PAD, 8):
        for i in range(0, members, 8):
            turned[i : i + 8, d : d + 8, :] = jnp.swapaxes(padded[d : d + 8, i : i + 8, :], 0, 1)


def in_order(agg, elems):
    across = jnp.broadcast_to(agg, (elems, elems)).astype(F32)
    here = lax.broadcasted_iota(jnp.int32, (elems, elems), 0)
    there = lax.broadcasted_iota(jnp.int32, (elems, elems), 1)
    ahead = (across.T == across) & (here < there)
    rank = jnp.sum(jnp.where(ahead, 1.0, 0.0), axis=0, keepdims=True)
    place = jnp.broadcast_to(agg.astype(F32) * PER_AGG + rank, (elems, elems)).T
    found = jnp.where(place == there.astype(F32), here.astype(F32), 0.0)
    return jnp.sum(found, axis=0, keepdims=True).astype(jnp.int32)


def set_masks(masks):
    slots = masks.shape[0] // 2
    block = lax.broadcasted_iota(jnp.int32, (8, LANES), 1) // PAD
    for s in range(slots):
        for h in range(2):
            masks[s * 2 + h] = jnp.where(block + h * SPLIT == s, 1.0, 0.0).astype(HALF)


def masked(block, mask):
    return (block.reshape(PAD // 8, 8, LANES) * mask[None]).reshape(PAD, LANES)


def pack_kernel(axis, sub_axis, send_far, maps_far, maps2_far, *refs):
    keep_ref, give_ref, packed, turned2 = refs[:4]
    padded, flat, padded2, send_ref, maps_ref, maps2_ref, sems = refs[4:]
    send_rows, halo = send_far.shape
    members = maps2_ref.shape[1]
    reach = send_rows // 2
    copies = [
        pltpu.make_async_copy(far, near, sems.at[i])
        for i, (far, near) in enumerate(
            ((maps_far, maps_ref), (send_far, send_ref), (maps2_far, maps2_ref))
        )
    ]
    for copy in copies:
        copy.start()
    copies[0].wait()
    transposed_rows(maps_ref, padded, packed)
    copies[1].wait()
    every = rounds(reach)
    for t in range(reach):
        for mine, out in ((False, give_ref), (True, keep_ref)):
            row = row_of_pair(axis, sub_axis, every[2 * t : 2 * t + 2], reach, True, mine)
            for h in range(halo):
                flat[h * PACK : (h + 1) * PACK, :] = packed[send_ref[row, h]]
            out[t] = flat[...].astype(HALF)
    copies[2].wait()
    padded_members(maps2_ref, padded2, turned2)
    groups = members // SPLIT
    for g in range(groups):
        group = turned2[g * SPLIT : (g + 1) * SPLIT].reshape(SPLIT * PAD, LANES)
        high, low = split_two(group.T[:PAD])
        give_ref[reach, g * PAD : (g + 1) * PAD, :] = high
        give_ref[reach, (groups + g) * PAD : (groups + g + 1) * PAD, :] = low


def join_kernel(keep_ref, own_ref, got_ref, *out_refs):
    reach = keep_ref.shape[0]
    for t, out in enumerate(out_refs):
        rows = got_ref.shape[1]
        out[:rows, :] = keep_ref[t] if t < reach else own_ref[reach]
        out[rows:, :] = got_ref[t]


def part_kernel(*refs):
    rows = refs[-1].shape[1]
    for t, ref in enumerate(refs[1:-1]):
        refs[-1][t] = ref[rows:, :]


def rows_kernel(agg_far, diag_far, face_far, maps_far, packed, after, *refs):
    table_ref, order_ref, g_ref, self_g_ref = refs[:4]
    rows_ref, own_ref, slab, left, right, agg_ref, diag_ref, face_ref, maps_ref = refs[4:13]
    order_row, sems = refs[13:]
    order, _, elems = maps_ref.shape
    faces = face_ref.shape[0]
    copies = [
        pltpu.make_async_copy(far, near, sems.at[i])
        for i, (far, near) in enumerate(
            ((agg_far, agg_ref), (face_far, face_ref), (diag_far, diag_ref), (maps_far, maps_ref))
        )
    ]
    for copy in copies:
        copy.start()

    def table(i, carry):
        for u in range(16):
            e = i * 16 + u
            table_ref[e] = unpacked(packed[e]).astype(HALF)
        return carry

    lax.fori_loop(0, elems // 16, table, 0)
    copies[0].wait()
    order_row[...] = in_order(agg_ref[...], elems)
    order_copy = pltpu.make_async_copy(order_row, order_ref, sems.at[len(copies)])
    order_copy.start()
    for copy in copies[1:]:
        copy.wait()
    slab[...] = jnp.zeros_like(slab)
    tall = 2 * SPLIT * PAD
    for part in range(2):
        for rr in range(PAD // 2):
            r = part * (PAD // 2) + rr
            if r >= order:
                left[rr] = jnp.zeros((elems, LANES), F32)
                right[rr] = jnp.zeros((elems, LANES), F32)
                continue
            base = (r % 2) * tall
            sources = [face_ref[k, r] for k in range(faces)] + [diag_ref[r], maps_ref[r]]
            for k, source in enumerate(sources):
                slab[base + k * PAD : base + k * PAD + order, :] = source
            turned = slab[base : base + tall, :].T.astype(F32)
            left[rr] = turned[:, :LANES]
            right[rr] = turned[:, LANES:]

        def shuffle(i, carry, part=part):
            for v in range(2):
                e = pl.multiple_of(i * 16 + v * 8, 8)
                for h, half in enumerate((left, right)):
                    top = jnp.swapaxes(half[0:8, pl.ds(e, 8), :], 0, 1)
                    low = jnp.swapaxes(half[8:16, pl.ds(e, 8), :], 0, 1)
                    for u in range(8):
                        both = jnp.concatenate([top[u], low[u]], axis=0)
                        to = slice(part * 16, part * 16 + 16)
                        rows_ref[e + u, to, h * LANES : (h + 1) * LANES] = both.astype(HALF)
                        if h == 1:
                            own_ref[e + u, to, :] = pltpu.roll(both, PAD, axis=1).astype(HALF)
            return carry

        lax.fori_loop(0, elems // 16, shuffle, 0)
    order_copy.wait()
    block = lax.broadcasted_iota(jnp.int32, (PAD, LANES), 1) // PAD

    def products(i, carry):
        for v in range(4):
            selves = jnp.zeros((PAD, LANES), F32)
            for u in range(SPLIT):
                at = i * 16 + v * SPLIT + u
                e = order_ref[0, at]
                g = jnp.dot(own_ref[e][:, :PAD], rows_ref[e], preferred_element_type=F32)
                high, low = split_two(g)
                g_ref[at, 0:PAD, :] = high
                g_ref[at, PAD : 2 * PAD, :] = low
                turn = (u - faces) % SPLIT
                own = g[:, LANES:]
                own = pltpu.roll(own, turn * PAD, axis=1) if turn else own
                selves = jnp.where(block == u, own, selves)
            high, low = split_two(selves)
            self_g_ref[i * 4 + v, 0:PAD, :] = high
            self_g_ref[i * 4 + v, PAD : 2 * PAD, :] = low
        return carry

    lax.fori_loop(0, elems // 16, products, 0)


def local_kernel(axis, order_ref, agg2_ref, *refs):
    (table_ref, self_g_ref, turned2, mine_ref, mate_ref, other_ref, after) = refs[:7]
    far_refs, (two_hi, two_lo, near_ref, self_ref, z_ref) = refs[7:-5], refs[-5:]
    count = lax.axis_size(axis)
    members = agg2_ref.shape[0]
    groups = members // SPLIT

    for t, ref in enumerate(far_refs):
        for h in range(near_ref.shape[1]):
            near_ref[t, h] = unpacked(ref[h].astype(F32)).astype(HALF)

    me = lax.axis_index(axis)
    last = mine_ref.shape[0] - 1
    tall = mine_ref.shape[1]
    for k in range(count):
        first = partner(me, k, count) * members
        for which, two in enumerate((two_hi, two_lo)):
            for g in range(groups):
                start = (which * groups + g) * PAD
                if k < 2:
                    rows = (mine_ref, mate_ref)[k][last, start : start + PAD, :]
                else:
                    start += (k - 2) * tall
                    rows = other_ref[start : start + PAD, :]
                for q, block in enumerate(spread(rows.astype(F32))):
                    two[first + g * SPLIT + q] = block.astype(HALF)

    block = lax.broadcasted_iota(jnp.int32, (PAD, LANES), 1) // PAD
    rows = z_ref.shape[0] // 2
    for g in range(groups):
        merged = turned2[g * SPLIT]
        to = jnp.full((PAD, LANES), agg2_ref[g * SPLIT], jnp.int32)
        for q in range(1, SPLIT):
            merged = merged + pltpu.roll(turned2[g * SPLIT + q], q * PAD, axis=1)
            to = jnp.where(block == q, agg2_ref[g * SPLIT + q], to)
        for k in range(rows // PAD):
            high, low = split_two(jnp.where(to == k, merged, 0.0))
            z_ref[k * PAD : (k + 1) * PAD, g * LANES : (g + 1) * LANES] = high
            z_ref[rows + k * PAD : rows + (k + 1) * PAD, g * LANES : (g + 1) * LANES] = low

    def selves(i4, carry):
        for v in range(4):
            i = i4 * 4 + v
            own = [table_ref[order_ref[0, i * PER_AGG + u]] for u in range(PER_AGG)]
            total = jnp.dot(
                jnp.concatenate([self_g_ref[i * 2], self_g_ref[i * 2 + 1]], axis=1),
                jnp.concatenate(own, axis=0),
                preferred_element_type=F32,
            )
            self_ref[i] = jnp.where(block == 0, total[:PAD] + total[PAD:], 0.0)
        return carry

    lax.fori_loop(0, members // 4, selves, 0)


def combine_kernel(axis, sub_axis, order_ref, nbr_ref, slot_ref, nbr2_ref, slot2_ref, *refs):
    count = lax.axis_size(sub_axis)
    faces, elems = nbr_ref.shape
    slots = nbr2_ref.shape[0]
    own_ref, near_ref, post_ref, g_ref, self_ref, two_hi, two_lo, z_ref = refs[:8]
    one_refs = refs[8:10]
    part_refs = refs[10 : 10 + count]
    table, masks, w_hi, w_lo, acc0, acc1, sems = refs[10 + count :]
    reach, halo = near_ref.shape[:2]
    members = self_ref.shape[0]
    every = rounds(reach)

    def place(t, mine):
        row = row_of_pair(axis, sub_axis, every[2 * t : 2 * t + 2], reach, False, mine)
        return elems + row * halo

    copies = [pltpu.make_async_copy(own_ref, table.at[pl.ds(0, elems)], sems.at[reach])] + [
        pltpu.make_async_copy(near_ref.at[t], table.at[pl.ds(place(t, True), halo)], sems.at[t])
        for t in range(reach)
    ]
    for copy in copies:
        copy.start()
    set_masks(masks)
    for t in range(reach):
        first = place(t, False)
        for h in range(halo):
            table[first + h] = unpacked(post_ref[t, h].astype(F32)).astype(HALF)
    for copy in copies:
        copy.wait()

    def placed(block, slot):
        return jnp.concatenate([masked(block, masks[slot * 2 + h]) for h in range(2)], axis=1)

    def gather(i2, carry):
        for v in range(2):
            i = i2 * 2 + v
            total = jnp.zeros((2 * PAD, 2 * LANES), F32)
            for u in range(PER_AGG):
                at = i * PER_AGG + u
                e = order_ref[0, at]
                rows = [placed(table[nbr_ref[k, e]], slot_ref[k, e]) for k in range(faces)]
                total = total + jnp.dot(
                    g_ref[at][:, : faces * PAD],
                    jnp.concatenate(rows, axis=0),
                    preferred_element_type=F32,
                )
            one = total[:PAD] + total[PAD:]
            for h in range(2):
                half = one[:, h * LANES : (h + 1) * LANES]
                one_refs[h][i] = half + self_ref[i] if h == 0 else half
        return carry

    lax.fori_loop(0, members // 2, gather, 0)

    def second(i4, carry):
        for u in range(4):
            i = i4 * 4 + u
            one = jnp.concatenate([ref[i] for ref in one_refs], axis=1)
            high, low = split_two(one)
            at = [(nbr2_ref[j, i], slot2_ref[j, i]) for j in range(slots)]
            w = jnp.dot(
                jnp.concatenate([high, low], axis=0),
                jnp.concatenate([placed(two_hi[source], slot) for source, slot in at], axis=0),
                preferred_element_type=F32,
            )
            w_corrected = jnp.dot(
                high,
                jnp.concatenate([placed(two_lo[source], slot) for source, slot in at], axis=0),
                preferred_element_type=F32,
            )
            w_high, w_low = split_two((w[:PAD] + w[PAD:]) + w_corrected)
            at = pl.ds(pl.multiple_of(i * PAD, PAD), PAD)
            w_hi[at, :] = w_high
            w_lo[at, :] = w_low
        return carry

    lax.fori_loop(0, members // 4, second, 0)
    rows = z_ref.shape[0] // 2
    for h, acc in enumerate((acc0, acc1)):
        lanes = slice(h * LANES, (h + 1) * LANES)
        z = jnp.dot(z_ref[...], w_hi[:, lanes], preferred_element_type=F32)
        z_low = jnp.dot(z_ref[:rows, :], w_lo[:, lanes], preferred_element_type=F32)
        acc[...] = ((z[:rows] + z[rows:]) + z_low).reshape(acc.shape)
    me = lax.axis_index(sub_axis)
    owned = acc0.shape[0] // count
    for o in range(count):
        first = partner(me, o, count) * owned
        for h, acc in enumerate((acc0, acc1)):
            for k in range(owned):
                part_refs[o][h, k] = acc[first + k]


def write_rows(out_ref, h, a, rows):
    order = out_ref.shape[1]
    for q in range(SPLIT):
        turned = rows if q == 0 else pltpu.roll(rows, LANES - q * PAD, axis=1)
        out_ref[h * SPLIT + q, a] = turned[:, :order]


def one_kernel(one0_ref, one1_ref, out_ref):
    _, order, members, _ = out_ref.shape
    for h, ref in enumerate((one0_ref, one1_ref)):
        for b in range(0, PAD, 8):
            groups = [
                jnp.swapaxes(ref[i : i + 8, b : b + 8, :], 0, 1) for i in range(0, members, 8)
            ]
            for u in range(min(8, order - b)):
                write_rows(out_ref, h, b + u, jnp.concatenate([x[u] for x in groups], axis=0))


def two_kernel(*refs):
    part_refs, out_ref = refs[:-1], refs[-1]
    _, order, owned, _ = out_ref.shape
    for h in range(2):
        value = part_refs[0][h]
        for ref in part_refs[1:]:
            value = value + ref[h]
        for a in range(order):
            write_rows(
                out_ref, h, a, jnp.concatenate([value[k, a : a + 1] for k in range(owned)], axis=0)
            )


def per_device(
    diag_block,
    face_block,
    restrict1,
    neighbour,
    face_slot,
    agg_map,
    send_list,
    restrict2,
    coarse_nbr,
    agg2_map,
    coarse_slot,
):
    order, _, elems = restrict1.shape
    faces = face_block.shape[0]
    send_rows, halo = send_list.shape
    reach = send_rows // 2
    slots = coarse_nbr.shape[0]
    members = elems // PER_AGG
    owned = members // PER_AGG
    count = lax.axis_size("sub")
    shape = jax.ShapeDtypeStruct
    maps2 = jnp.transpose(restrict2, (0, 2, 1))

    near = pltpu.VMEM
    params = pltpu.CompilerParams(vmem_limit_bytes=36 * 2**20)
    tall = halo * PACK

    def call(kernel, name, in_specs, out_specs, out_shape, scratch, work):
        return pl.pallas_call(
            kernel,
            name=name,
            compiler_params=params,
            in_specs=in_specs,
            out_specs=out_specs,
            out_shape=out_shape,
            scratch_shapes=scratch,
            cost_estimate=pl.CostEstimate(
                flops=work * 1_000_000, bytes_accessed=work * 2_000, transcendentals=0
            ),
        )

    keep, give, own_rows, turned2 = call(
        functools.partial(pack_kernel, "dom", "sub"),
        "pack",
        [FAR] * 3,
        [VMEM] * 4,
        [
            near((reach, tall, LANES), HALF),
            near((reach + 1, tall, LANES), HALF),
            near((elems, PACK, LANES), F32),
            near((members, PAD, LANES), F32),
        ],
        [
            pltpu.VMEM((PAD, PAD, elems), F32),
            pltpu.VMEM((tall, LANES), F32),
            pltpu.VMEM((PAD, members, LANES), F32),
            pltpu.SMEM(send_list.shape, jnp.int32),
            pltpu.VMEM(restrict1.shape, HALF),
            pltpu.VMEM(maps2.shape, F32),
            pltpu.SemaphoreType.DMA((3,)),
        ],
        1000,
    )(*[far(x) for x in (send_list, restrict1, maps2)])
    if 2 * members * PAD // SPLIT != tall:
        raise ValueError("payload rows")
    got = swapped(give, "sub", 1)
    joined = call(
        join_kernel,
        "join",
        [VMEM] * 3,
        [VMEM] * (reach + 1),
        [near((2 * tall, LANES), HALF)] * (reach + 1),
        [],
        300,
    )(keep, give, got)
    other = swapped(joined[reach], "sub", 2)
    every = rounds(reach)
    arrived = [
        exchanged(joined[t], "dom", "sub", every[2 * t : 2 * t + 2]) for t in range(reach)
    ]
    table, order_list, g, self_g = call(
        rows_kernel,
        "rows",
        [FAR] * 4 + [VMEM, ANY],
        [VMEM, SMEM, VMEM, VMEM],
        [
            near((elems, PAD, LANES), HALF),
            shape((1, elems), jnp.int32),
            near((elems, 2 * PAD, 2 * LANES), HALF),
            near((elems // SPLIT, 2 * PAD, LANES), HALF),
        ],
        [
            pltpu.VMEM((elems, PAD, 2 * LANES), HALF),
            pltpu.VMEM((elems, PAD, LANES), HALF),
            pltpu.VMEM((4 * LANES, elems), HALF),
            pltpu.VMEM((PAD // 2, elems, LANES), F32),
            pltpu.VMEM((PAD // 2, elems, LANES), F32),
            pltpu.VMEM((1, elems), jnp.int32),
            pltpu.VMEM(diag_block.shape, HALF),
            pltpu.VMEM(face_block.shape, HALF),
            pltpu.VMEM(restrict1.shape, HALF),
            pltpu.VMEM((1, elems), jnp.int32),
            pltpu.SemaphoreType.DMA((5,)),
        ],
        8000,
    )(
        *[far(x) for x in (agg_map[None], diag_block, face_block, restrict1)],
        own_rows,
        joined[0],
    )
    post = call(
        part_kernel,
        "part",
        [ANY] + [VMEM] * reach,
        VMEM,
        near((reach, tall, LANES), HALF),
        [],
        300,
    )(self_g, *arrived)
    landed_post = swapped(post, "sub", 1)
    halves = [block.reshape(2 * halo, PACK, LANES) for block in arrived]
    two_hi, two_lo, near_halo, self_terms, z = call(
        functools.partial(local_kernel, "sub"),
        "local",
        [SMEM] * 2 + [VMEM] * 6 + [ANY] + [VMEM] * reach,
        [VMEM] * 5,
        [
            near((count * members, PAD, LANES), HALF),
            near((count * members, PAD, LANES), HALF),
            near((reach, halo, PAD, LANES), HALF),
            near((members, PAD, LANES), F32),
            near((2 * count * owned * PAD, members * PAD), HALF),
        ],
        [],
        2000,
    )(order_list, agg2_map, table, self_g, turned2, give, got, other, post, *halves)

    combined = pl.pallas_call(
        functools.partial(combine_kernel, "dom", "sub"),
        name="combine",
        compiler_params=params,
        in_specs=[SMEM] * 5 + [VMEM] * 8,
        out_specs=[VMEM] * (2 + count),
        out_shape=[near((members, PAD, LANES), F32)] * 2
        + [near((2, owned, PAD, LANES), F32)] * count,
        scratch_shapes=[
            pltpu.VMEM((elems + send_rows * halo, PAD, LANES), HALF),
            pltpu.VMEM((2 * SLOTS2, 8, LANES), HALF),
            pltpu.VMEM((members * PAD, 2 * LANES), HALF),
            pltpu.VMEM((members * PAD, 2 * LANES), HALF),
            pltpu.VMEM((count * owned, PAD, LANES), F32),
            pltpu.VMEM((count * owned, PAD, LANES), F32),
            pltpu.SemaphoreType.DMA((reach + 1,)),
        ],
    )(
        order_list,
        neighbour,
        face_slot,
        coarse_nbr,
        coarse_slot,
        table,
        near_halo,
        landed_post.reshape(reach, halo, PACK, LANES),
        g,
        self_terms,
        two_hi,
        two_lo,
        z,
    )
    one0, one1, parts = combined[0], combined[1], combined[2:]
    landed = [parts[0]] + [swapped(parts[k], "sub", k) for k in range(1, count)]
    coarse_one = pl.pallas_call(
        one_kernel,
        name="first",
        compiler_params=params,
        in_specs=[VMEM] * 2,
        out_specs=VMEM,
        out_shape=shape((slots, order, members, order), F32),
        cost_estimate=pl.CostEstimate(
            flops=2_000_000_000, bytes_accessed=4_000_000, transcendentals=0
        ),
    )(one0, one1)
    coarse_two = pl.pallas_call(
        two_kernel,
        name="second",
        compiler_params=params,
        in_specs=[VMEM] * count,
        out_specs=VMEM,
        out_shape=shape((SLOTS2, order, owned, order), F32),
    )(*landed)
    return (
        jnp.transpose(coarse_one, (0, 1, 3, 2)),
        jnp.transpose(coarse_two, (0, 1, 3, 2)),
    )


def solution(mesh):
    placed = (
        P(None, None, ("dom", "sub")),
        P(None, None, None, ("dom", "sub")),
        P(None, None, ("dom", "sub")),
        P(None, ("dom", "sub")),
        P(None, ("dom", "sub")),
        P(("dom", "sub")),
        P(None, ("dom", "sub")),
        P(None, None, ("dom", "sub")),
        P(None, ("dom", "sub")),
        P(("dom", "sub")),
        P(None, ("dom", "sub")),
    )
    return jax.shard_map(
        per_device,
        mesh=mesh,
        in_specs=placed,
        out_specs=(P(None, None, None, ("dom", "sub")), P(None, None, None, ("dom", "sub"))),
        check_vma=False,
    )
```

```python
import functools

import jax
import jax.numpy as jnp
from jax import lax
from jax.experimental import pallas as pl
from jax.experimental.pallas import tpu as pltpu
from jax.sharding import PartitionSpec as P

SLOTS2 = 8
PER_AGG = 8
PAD = 32
LANES = 128
SPLIT = LANES // PAD
PACK = PAD // SPLIT


F32 = jnp.float32
HALF = jnp.bfloat16

VMEM = pl.BlockSpec(memory_space=pltpu.VMEM)
SMEM = pl.BlockSpec(memory_space=pltpu.SMEM)
ANY = pl.BlockSpec(memory_space=pl.ANY)
FAR = pl.BlockSpec(memory_space=pltpu.HBM)


def rounds(reach):
    sides = [(offset, side) for side in (1, 0) for offset in range(1, reach + 1)]
    if reach == 3:
        sides = [(3, 1), (2, 1), (1, 1), (3, 0), (1, 0), (2, 0)]
    return [(offset, (offset & -offset).bit_length() - 1, side) for offset, side in sides]


def across(index, this, count):
    offset, level, side = this
    if count % (2 << level):
        raise ValueError("ring length")
    return (index + offset if (index >> level) & 1 == side else index - offset) % count


def exchanged(shard, axis, sub_axis, pair_rounds):
    count, members = lax.axis_size(axis), lax.axis_size(sub_axis)
    pairs = [
        (d * members + s, across(d, pair_rounds[s & 1], count) * members + s)
        for d in range(count)
        for s in range(members)
    ]
    return lax.ppermute(shard, (axis, sub_axis), pairs)


def far(array):
    return pltpu.with_memory_space_constraint(array, pltpu.HBM)


def listed(offset, reach):
    return offset + reach if offset < 0 else offset + reach - 1


def row_of(axis, this, reach, sending):
    offset, level, side = this
    ahead = ((lax.axis_index(axis) >> level) & 1) == side
    plus, minus = listed(offset, reach), listed(-offset, reach)
    return jnp.where(ahead, minus, plus) if sending else jnp.where(ahead, plus, minus)


def row_of_pair(axis, sub_axis, pair_rounds, reach, sending, mine):
    first = (lax.axis_index(sub_axis) & 1) == (0 if mine else 1)
    rows = [row_of(axis, this, reach, sending) for this in pair_rounds]
    return jnp.where(first, rows[0], rows[1])


def partner(me, k, count):
    if count != 4:
        raise ValueError("subgroup size")
    return me ^ k


def swapped(shard, axis, k):
    count = lax.axis_size(axis)
    return lax.ppermute(shard, axis, [(i, partner(i, k, count)) for i in range(count)])


def spread(rows):
    block = lax.broadcasted_iota(jnp.int32, rows.shape, 1) // PAD
    turned = [rows] + [pltpu.roll(rows, PAD * q, axis=1) for q in range(1, SPLIT)]
    results = []
    for part in range(SPLIT):
        result = turned[(SPLIT - 1 - part) % SPLIT]
        for b in range(SPLIT - 1):
            result = jnp.where(block == b, turned[(b - part) % SPLIT], result)
        results.append(result)
    return results


def unpacked(packed):
    return jnp.concatenate(spread(packed), axis=0)


def split_two(value):
    high = value.astype(HALF)
    return high, (value - high.astype(F32)).astype(HALF)


def transposed_rows(maps_ref, padded, packed):
    order, _, elems = maps_ref.shape
    padded[...] = jnp.zeros_like(padded)
    for j in range(order):
        padded[j, :order, :] = maps_ref[j].astype(F32)
    rows = []
    for M in range(PACK):
        rows.append([])
    turned = [
        [jnp.swapaxes(padded[8 * b : 8 * b + 8, 8 * q : 8 * q + 8, :], 0, 1) for b in range(PAD // 8)]
        for q in range(SPLIT)
    ]
    packs = [
        jnp.concatenate([turned[q][b][M] for q in range(SPLIT) for b in range(PAD // 8)], axis=0).T
        for M in range(PACK)
    ]
    for e in range(0, elems, 8):
        group = jnp.stack([pack[e : e + 8, :] for pack in packs], axis=0)
        packed[e : e + 8] = jnp.swapaxes(group, 0, 1)


def padded_members(maps2_ref, padded, turned):
    order, members, _ = maps2_ref.shape
    padded[...] = jnp.zeros_like(padded)
    for d in range(order):
        padded[d, :, :order] = maps2_ref[d]
    for d in range(0, PAD, 8):
        for i in range(0, members, 8):
            turned[i : i + 8, d : d + 8, :] = jnp.swapaxes(padded[d : d + 8, i : i + 8, :], 0, 1)


def in_order(agg, elems):
    across = jnp.broadcast_to(agg, (elems, elems)).astype(F32)
    here = lax.broadcasted_iota(jnp.int32, (elems, elems), 0)
    there = lax.broadcasted_iota(jnp.int32, (elems, elems), 1)
    ahead = (across.T == across) & (here < there)
    rank = jnp.sum(jnp.where(ahead, 1.0, 0.0), axis=0, keepdims=True)
    place = jnp.broadcast_to(agg.astype(F32) * PER_AGG + rank, (elems, elems)).T
    found = jnp.where(place == there.astype(F32), here.astype(F32), 0.0)
    return jnp.sum(found, axis=0, keepdims=True).astype(jnp.int32)


def set_masks(masks):
    slots = masks.shape[0] // 2
    block = lax.broadcasted_iota(jnp.int32, (8, LANES), 1) // PAD
    for s in range(slots):
        for h in range(2):
            masks[s * 2 + h] = jnp.where(block + h * SPLIT == s, 1.0, 0.0).astype(HALF)


def masked(block, mask):
    return (block.reshape(PAD // 8, 8, LANES) * mask[None]).reshape(PAD, LANES)


def pack_kernel(axis, sub_axis, send_far, maps_far, maps2_far, *refs):
    keep_ref, give_ref, packed, turned2 = refs[:4]
    padded, flat, padded2, send_ref, maps_ref, maps2_ref, sems = refs[4:]
    send_rows, halo = send_far.shape
    members = maps2_ref.shape[1]
    reach = send_rows // 2
    copies = [
        pltpu.make_async_copy(far, near, sems.at[i])
        for i, (far, near) in enumerate(
            ((maps_far, maps_ref), (send_far, send_ref), (maps2_far, maps2_ref))
        )
    ]
    for copy in copies:
        copy.start()
    copies[0].wait()
    transposed_rows(maps_ref, padded, packed)
    copies[1].wait()
    every = rounds(reach)
    for t in range(reach):
        for mine, out in ((False, give_ref), (True, keep_ref)):
            row = row_of_pair(axis, sub_axis, every[2 * t : 2 * t + 2], reach, True, mine)
            for h in range(halo):
                flat[h * PACK : (h + 1) * PACK, :] = packed[send_ref[row, h]]
            out[t] = flat[...].astype(HALF)
    copies[2].wait()
    padded_members(maps2_ref, padded2, turned2)
    groups = members // SPLIT
    for g in range(groups):
        group = turned2[g * SPLIT : (g + 1) * SPLIT].reshape(SPLIT * PAD, LANES)
        high, low = split_two(group.T[:PAD])
        give_ref[reach, g * PAD : (g + 1) * PAD, :] = high
        give_ref[reach, (groups + g) * PAD : (groups + g + 1) * PAD, :] = low


def join_kernel(after, keep_ref, own_ref, got_ref, *out_refs):
    reach = keep_ref.shape[0]
    for t, out in enumerate(out_refs):
        rows = got_ref.shape[1]
        out[:rows, :] = keep_ref[t] if t < reach else own_ref[reach]
        out[rows:, :] = got_ref[t]


def part_kernel(*refs):
    rows = refs[-1].shape[1]
    for t, ref in enumerate(refs[1:-1]):
        refs[-1][t] = ref[rows:, :]


def table_kernel(packed, table_ref):
    elems = packed.shape[0]
    step = 32

    def table(i, carry):
        for u in range(step):
            e = i * step + u
            table_ref[e] = unpacked(packed[e]).astype(HALF)
        return carry

    lax.fori_loop(0, elems // step, table, 0)


def rows_kernel(agg_far, diag_far, face_far, maps_far, after, *refs):
    order_ref, g_ref, self_g_ref = refs[:3]
    rows_ref, own_ref, slab, left, right, agg_ref, diag_ref, face_ref, maps_ref = refs[3:12]
    order_row, sems = refs[12:]
    order, _, elems = maps_ref.shape
    faces = face_ref.shape[0]
    copies = [
        pltpu.make_async_copy(far, near, sems.at[i])
        for i, (far, near) in enumerate(
            ((agg_far, agg_ref), (face_far, face_ref), (diag_far, diag_ref), (maps_far, maps_ref))
        )
    ]
    for copy in copies:
        copy.start()

    copies[0].wait()
    order_row[...] = in_order(agg_ref[...], elems)
    order_copy = pltpu.make_async_copy(order_row, order_ref, sems.at[len(copies)])
    order_copy.start()
    for copy in copies[1:]:
        copy.wait()
    slab[...] = jnp.zeros_like(slab)
    tall = 2 * SPLIT * PAD
    for part in range(2):
        for rr in range(PAD // 2):
            r = part * (PAD // 2) + rr
            if r >= order:
                left[rr] = jnp.zeros((elems, LANES), F32)
                right[rr] = jnp.zeros((elems, LANES), F32)
                continue
            base = (r % 2) * tall
            sources = [face_ref[k, r] for k in range(faces)] + [diag_ref[r], maps_ref[r]]
            for k, source in enumerate(sources):
                slab[base + k * PAD : base + k * PAD + order, :] = source
            turned = slab[base : base + tall, :].T.astype(F32)
            left[rr] = turned[:, :LANES]
            right[rr] = turned[:, LANES:]

        def shuffle(i, carry, part=part):
            for v in range(4):
                e = pl.multiple_of(i * 32 + v * 8, 8)
                for h, half in enumerate((left, right)):
                    top = jnp.swapaxes(half[0:8, pl.ds(e, 8), :], 0, 1)
                    low = jnp.swapaxes(half[8:16, pl.ds(e, 8), :], 0, 1)
                    for u in range(8):
                        both = jnp.concatenate([top[u], low[u]], axis=0)
                        to = slice(part * 16, part * 16 + 16)
                        rows_ref[e + u, to, h * LANES : (h + 1) * LANES] = both.astype(HALF)
                        if h == 1:
                            own_ref[e + u, to, :] = pltpu.roll(both, PAD, axis=1).astype(HALF)
            return carry

        lax.fori_loop(0, elems // 32, shuffle, 0)
    order_copy.wait()
    block = lax.broadcasted_iota(jnp.int32, (PAD, LANES), 1) // PAD

    def products(i, carry):
        for v in range(8):
            selves = jnp.zeros((PAD, LANES), F32)
            for u in range(SPLIT):
                at = i * 32 + v * SPLIT + u
                e = order_ref[0, at]
                g = jnp.dot(own_ref[e][:, :PAD], rows_ref[e], preferred_element_type=F32)
                high, low = split_two(g)
                g_ref[at, 0:PAD, :] = high
                g_ref[at, PAD : 2 * PAD, :] = low
                turn = (u - faces) % SPLIT
                own = g[:, LANES:]
                own = pltpu.roll(own, turn * PAD, axis=1) if turn else own
                selves = jnp.where(block == u, own, selves)
            high, low = split_two(selves)
            self_g_ref[i * 8 + v, 0:PAD, :] = high
            self_g_ref[i * 8 + v, PAD : 2 * PAD, :] = low
        return carry

    lax.fori_loop(0, elems // 32, products, 0)


def local_kernel(axis, order_ref, agg2_ref, *refs):
    (table_ref, self_g_ref, turned2, mine_ref, mate_ref, other_ref, after) = refs[:7]
    far_refs, (two_hi, two_lo, near_ref, self_ref, z_ref) = refs[7:-5], refs[-5:]
    count = lax.axis_size(axis)
    members = agg2_ref.shape[0]
    groups = members // SPLIT

    for t, ref in enumerate(far_refs):
        for h in range(near_ref.shape[1]):
            near_ref[t, h] = unpacked(ref[h].astype(F32)).astype(HALF)

    me = lax.axis_index(axis)
    last = mine_ref.shape[0] - 1
    tall = mine_ref.shape[1]
    for k in range(count):
        first = partner(me, k, count) * members
        for which, two in enumerate((two_hi, two_lo)):
            for g in range(groups):
                start = (which * groups + g) * PAD
                if k < 2:
                    rows = (mine_ref, mate_ref)[k][last, start : start + PAD, :]
                else:
                    start += (k - 2) * tall
                    rows = other_ref[start : start + PAD, :]
                for q, block in enumerate(spread(rows.astype(F32))):
                    two[first + g * SPLIT + q] = block.astype(HALF)

    block = lax.broadcasted_iota(jnp.int32, (PAD, LANES), 1) // PAD
    rows = z_ref.shape[0] // 2
    for g in range(groups):
        merged = turned2[g * SPLIT]
        to = jnp.full((PAD, LANES), agg2_ref[g * SPLIT], jnp.int32)
        for q in range(1, SPLIT):
            merged = merged + pltpu.roll(turned2[g * SPLIT + q], q * PAD, axis=1)
            to = jnp.where(block == q, agg2_ref[g * SPLIT + q], to)
        for k in range(rows // PAD):
            high, low = split_two(jnp.where(to == k, merged, 0.0))
            z_ref[k * PAD : (k + 1) * PAD, g * LANES : (g + 1) * LANES] = high
            z_ref[rows + k * PAD : rows + (k + 1) * PAD, g * LANES : (g + 1) * LANES] = low

    def selves(i4, carry):
        for v in range(4):
            i = i4 * 4 + v
            own = [table_ref[order_ref[0, i * PER_AGG + u]] for u in range(PER_AGG)]
            total = jnp.dot(
                jnp.concatenate([self_g_ref[i * 2], self_g_ref[i * 2 + 1]], axis=1),
                jnp.concatenate(own, axis=0),
                preferred_element_type=F32,
            )
            self_ref[i] = jnp.where(block == 0, total[:PAD] + total[PAD:], 0.0)
        return carry

    lax.fori_loop(0, members // 4, selves, 0)


def combine_kernel(axis, sub_axis, order_ref, nbr_ref, slot_ref, nbr2_ref, slot2_ref, *refs):
    count = lax.axis_size(sub_axis)
    faces, elems = nbr_ref.shape
    slots = nbr2_ref.shape[0]
    own_ref, near_ref, post_ref, g_ref, self_ref, two_hi, two_lo, z_ref = refs[:8]
    one_refs = refs[8:10]
    part_refs = refs[10 : 10 + count]
    table, masks, w_hi, w_lo, acc0, acc1, sems = refs[10 + count :]
    reach, halo = near_ref.shape[:2]
    members = self_ref.shape[0]
    every = rounds(reach)

    def place(t, mine):
        row = row_of_pair(axis, sub_axis, every[2 * t : 2 * t + 2], reach, False, mine)
        return elems + row * halo

    copies = [pltpu.make_async_copy(own_ref, table.at[pl.ds(0, elems)], sems.at[reach])] + [
        pltpu.make_async_copy(near_ref.at[t], table.at[pl.ds(place(t, True), halo)], sems.at[t])
        for t in range(reach)
    ]
    for copy in copies:
        copy.start()
    set_masks(masks)
    for t in range(reach):
        first = place(t, False)
        for h in range(halo):
            table[first + h] = unpacked(post_ref[t, h].astype(F32)).astype(HALF)
    for copy in copies:
        copy.wait()

    def placed(block, slot):
        return jnp.concatenate([masked(block, masks[slot * 2 + h]) for h in range(2)], axis=1)

    def gather(i2):
        for v in range(2):
            i = i2 * 2 + v
            total = jnp.zeros((2 * PAD, 2 * LANES), F32)
            for u in range(PER_AGG):
                at = i * PER_AGG + u
                e = order_ref[0, at]
                rows = [placed(table[nbr_ref[k, e]], slot_ref[k, e]) for k in range(faces)]
                total = total + jnp.dot(
                    g_ref[at][:, : faces * PAD],
                    jnp.concatenate(rows, axis=0),
                    preferred_element_type=F32,
                )
            one = total[:PAD] + total[PAD:]
            for h in range(2):
                half = one[:, h * LANES : (h + 1) * LANES]
                one_refs[h][i] = half + self_ref[i] if h == 0 else half

    def second(i2):
        for v in range(2):
            i = i2 * 2 + v
            one = jnp.concatenate([ref[i] for ref in one_refs], axis=1)
            high, low = split_two(one)
            to = [(nbr2_ref[j, i], slot2_ref[j, i]) for j in range(slots)]
            w = jnp.dot(
                jnp.concatenate([high, low], axis=0),
                jnp.concatenate([placed(two_hi[source], slot) for source, slot in to], axis=0),
                preferred_element_type=F32,
            )
            w_corrected = jnp.dot(
                high,
                jnp.concatenate([placed(two_lo[source], slot) for source, slot in to], axis=0),
                preferred_element_type=F32,
            )
            w_high, w_low = split_two((w[:PAD] + w[PAD:]) + w_corrected)
            at = pl.ds(pl.multiple_of(i * PAD, PAD), PAD)
            w_hi[at, :] = w_high
            w_lo[at, :] = w_low

    def both(i2, carry):
        second(i2 - 1)
        gather(i2)
        return carry

    gather(0)
    lax.fori_loop(1, members // 2, both, 0)
    second(members // 2 - 1)
    rows = z_ref.shape[0] // 2
    for h, acc in enumerate((acc0, acc1)):
        lanes = slice(h * LANES, (h + 1) * LANES)
        z = jnp.dot(z_ref[...], w_hi[:, lanes], preferred_element_type=F32)
        z_low = jnp.dot(z_ref[:rows, :], w_lo[:, lanes], preferred_element_type=F32)
        acc[...] = ((z[:rows] + z[rows:]) + z_low).reshape(acc.shape)
    me = lax.axis_index(sub_axis)
    owned = acc0.shape[0] // count
    for o in range(count):
        first = partner(me, o, count) * owned
        for h, acc in enumerate((acc0, acc1)):
            for k in range(owned):
                part_refs[o][h, k] = acc[first + k]


def write_rows(out_ref, h, a, rows):
    order = out_ref.shape[1]
    for q in range(SPLIT):
        turned = rows if q == 0 else pltpu.roll(rows, LANES - q * PAD, axis=1)
        out_ref[h * SPLIT + q, a] = turned[:, :order]


def one_kernel(one0_ref, one1_ref, out_ref):
    _, order, members, _ = out_ref.shape
    for h, ref in enumerate((one0_ref, one1_ref)):
        for b in range(0, PAD, 8):
            groups = [
                jnp.swapaxes(ref[i : i + 8, b : b + 8, :], 0, 1) for i in range(0, members, 8)
            ]
            for u in range(min(8, order - b)):
                write_rows(out_ref, h, b + u, jnp.concatenate([x[u] for x in groups], axis=0))


def two_kernel(*refs):
    part_refs, out_ref = refs[:-1], refs[-1]
    _, order, owned, _ = out_ref.shape
    for h in range(2):
        value = part_refs[0][h]
        for ref in part_refs[1:]:
            value = value + ref[h]
        for a in range(order):
            write_rows(
                out_ref, h, a, jnp.concatenate([value[k, a : a + 1] for k in range(owned)], axis=0)
            )


def per_device(
    diag_block,
    face_block,
    restrict1,
    neighbour,
    face_slot,
    agg_map,
    send_list,
    restrict2,
    coarse_nbr,
    agg2_map,
    coarse_slot,
):
    order, _, elems = restrict1.shape
    faces = face_block.shape[0]
    send_rows, halo = send_list.shape
    reach = send_rows // 2
    slots = coarse_nbr.shape[0]
    members = elems // PER_AGG
    owned = members // PER_AGG
    count = lax.axis_size("sub")
    shape = jax.ShapeDtypeStruct
    maps2 = jnp.transpose(restrict2, (0, 2, 1))

    near = pltpu.VMEM
    params = pltpu.CompilerParams(vmem_limit_bytes=36 * 2**20)
    tall = halo * PACK

    def call(kernel, name, in_specs, out_specs, out_shape, scratch, work):
        return pl.pallas_call(
            kernel,
            name=name,
            compiler_params=params,
            in_specs=in_specs,
            out_specs=out_specs,
            out_shape=out_shape,
            scratch_shapes=scratch,
            cost_estimate=pl.CostEstimate(
                flops=work * 1_000_000, bytes_accessed=work * 2_000, transcendentals=0
            ),
        )

    keep, give, own_rows, turned2 = call(
        functools.partial(pack_kernel, "dom", "sub"),
        "pack",
        [FAR] * 3,
        [VMEM] * 4,
        [
            near((reach, tall, LANES), HALF),
            near((reach + 1, tall, LANES), HALF),
            near((elems, PACK, LANES), F32),
            near((members, PAD, LANES), F32),
        ],
        [
            pltpu.VMEM((PAD, PAD, elems), F32),
            pltpu.VMEM((tall, LANES), F32),
            pltpu.VMEM((PAD, members, LANES), F32),
            pltpu.SMEM(send_list.shape, jnp.int32),
            pltpu.VMEM(restrict1.shape, HALF),
            pltpu.VMEM(maps2.shape, F32),
            pltpu.SemaphoreType.DMA((3,)),
        ],
        1000,
    )(*[far(x) for x in (send_list, restrict1, maps2)])
    if 2 * members * PAD // SPLIT != tall:
        raise ValueError("payload rows")
    got = swapped(give, "sub", 1)
    table = call(
        table_kernel, "table", [VMEM], VMEM, near((elems, PAD, LANES), HALF), [], 1000
    )(own_rows)
    joined = call(
        join_kernel,
        "join",
        [ANY] + [VMEM] * 3,
        [VMEM] * (reach + 1),
        [near((2 * tall, LANES), HALF)] * (reach + 1),
        [],
        300,
    )(table, keep, give, got)
    other = swapped(joined[reach], "sub", 2)
    every = rounds(reach)
    arrived = [
        exchanged(joined[t], "dom", "sub", every[2 * t : 2 * t + 2]) for t in range(reach)
    ]
    order_list, g, self_g = call(
        rows_kernel,
        "rows",
        [FAR] * 4 + [ANY],
        [SMEM, VMEM, VMEM],
        [
            shape((1, elems), jnp.int32),
            near((elems, 2 * PAD, 2 * LANES), HALF),
            near((elems // SPLIT, 2 * PAD, LANES), HALF),
        ],
        [
            pltpu.VMEM((elems, PAD, 2 * LANES), HALF),
            pltpu.VMEM((elems, PAD, LANES), HALF),
            pltpu.VMEM((4 * LANES, elems), HALF),
            pltpu.VMEM((PAD // 2, elems, LANES), F32),
            pltpu.VMEM((PAD // 2, elems, LANES), F32),
            pltpu.VMEM((1, elems), jnp.int32),
            pltpu.VMEM(diag_block.shape, HALF),
            pltpu.VMEM(face_block.shape, HALF),
            pltpu.VMEM(restrict1.shape, HALF),
            pltpu.VMEM((1, elems), jnp.int32),
            pltpu.SemaphoreType.DMA((5,)),
        ],
        8000,
    )(
        *[far(x) for x in (agg_map[None], diag_block, face_block, restrict1)],
        joined[0],
    )
    post = call(
        part_kernel,
        "part",
        [ANY] + [VMEM] * reach,
        VMEM,
        near((reach, tall, LANES), HALF),
        [],
        300,
    )(self_g, *arrived)
    landed_post = swapped(post, "sub", 1)
    halves = [block.reshape(2 * halo, PACK, LANES) for block in arrived]
    two_hi, two_lo, near_halo, self_terms, z = call(
        functools.partial(local_kernel, "sub"),
        "local",
        [SMEM] * 2 + [VMEM] * 6 + [ANY] + [VMEM] * reach,
        [VMEM] * 5,
        [
            near((count * members, PAD, LANES), HALF),
            near((count * members, PAD, LANES), HALF),
            near((reach, halo, PAD, LANES), HALF),
            near((members, PAD, LANES), F32),
            near((2 * count * owned * PAD, members * PAD), HALF),
        ],
        [],
        2000,
    )(order_list, agg2_map, table, self_g, turned2, give, got, other, post, *halves)

    combined = pl.pallas_call(
        functools.partial(combine_kernel, "dom", "sub"),
        name="combine",
        compiler_params=params,
        in_specs=[SMEM] * 5 + [VMEM] * 8,
        out_specs=[VMEM] * (2 + count),
        out_shape=[near((members, PAD, LANES), F32)] * 2
        + [near((2, owned, PAD, LANES), F32)] * count,
        scratch_shapes=[
            pltpu.VMEM((elems + send_rows * halo, PAD, LANES), HALF),
            pltpu.VMEM((2 * SLOTS2, 8, LANES), HALF),
            pltpu.VMEM((members * PAD, 2 * LANES), HALF),
            pltpu.VMEM((members * PAD, 2 * LANES), HALF),
            pltpu.VMEM((count * owned, PAD, LANES), F32),
            pltpu.VMEM((count * owned, PAD, LANES), F32),
            pltpu.SemaphoreType.DMA((reach + 1,)),
        ],
    )(
        order_list,
        neighbour,
        face_slot,
        coarse_nbr,
        coarse_slot,
        table,
        near_halo,
        landed_post.reshape(reach, halo, PACK, LANES),
        g,
        self_terms,
        two_hi,
        two_lo,
        z,
    )
    one0, one1, parts = combined[0], combined[1], combined[2:]
    landed = [parts[0]] + [swapped(parts[k], "sub", k) for k in range(1, count)]
    coarse_one = pl.pallas_call(
        one_kernel,
        name="first",
        compiler_params=params,
        in_specs=[VMEM] * 2,
        out_specs=VMEM,
        out_shape=shape((slots, order, members, order), F32),
        cost_estimate=pl.CostEstimate(
            flops=2_000_000_000, bytes_accessed=4_000_000, transcendentals=0
        ),
    )(one0, one1)
    coarse_two = pl.pallas_call(
        two_kernel,
        name="second",
        compiler_params=params,
        in_specs=[VMEM] * count,
        out_specs=VMEM,
        out_shape=shape((SLOTS2, order, owned, order), F32),
    )(*landed)
    return (
        jnp.transpose(coarse_one, (0, 1, 3, 2)),
        jnp.transpose(coarse_two, (0, 1, 3, 2)),
    )


def solution(mesh):
    placed = (
        P(None, None, ("dom", "sub")),
        P(None, None, None, ("dom", "sub")),
        P(None, None, ("dom", "sub")),
        P(None, ("dom", "sub")),
        P(None, ("dom", "sub")),
        P(("dom", "sub")),
        P(None, ("dom", "sub")),
        P(None, None, ("dom", "sub")),
        P(None, ("dom", "sub")),
        P(("dom", "sub")),
        P(None, ("dom", "sub")),
    )
    return jax.shard_map(
        per_device,
        mesh=mesh,
        in_specs=placed,
        out_specs=(P(None, None, None, ("dom", "sub")), P(None, None, None, ("dom", "sub"))),
        check_vma=False,
    )
```

```python
import functools

import jax
import jax.numpy as jnp
from jax import lax
from jax.experimental import pallas as pl
from jax.experimental.pallas import tpu as pltpu
from jax.sharding import PartitionSpec as P

SLOTS2 = 8
PER_AGG = 8
PAD = 32
LANES = 128
SPLIT = LANES // PAD
PACK = PAD // SPLIT


F32 = jnp.float32
HALF = jnp.bfloat16

VMEM = pl.BlockSpec(memory_space=pltpu.VMEM)
SMEM = pl.BlockSpec(memory_space=pltpu.SMEM)
ANY = pl.BlockSpec(memory_space=pl.ANY)
FAR = pl.BlockSpec(memory_space=pltpu.HBM)


def rounds(reach):
    sides = [(offset, side) for side in (1, 0) for offset in range(1, reach + 1)]
    if reach == 3:
        sides = [(3, 1), (2, 1), (1, 1), (3, 0), (1, 0), (2, 0)]
    return [(offset, (offset & -offset).bit_length() - 1, side) for offset, side in sides]


def across(index, this, count):
    offset, level, side = this
    if count % (2 << level):
        raise ValueError("ring length")
    return (index + offset if (index >> level) & 1 == side else index - offset) % count


def exchanged(shard, axis, sub_axis, pair_rounds):
    count, members = lax.axis_size(axis), lax.axis_size(sub_axis)
    pairs = [
        (d * members + s, across(d, pair_rounds[s & 1], count) * members + s)
        for d in range(count)
        for s in range(members)
    ]
    return lax.ppermute(shard, (axis, sub_axis), pairs)


def far(array):
    return pltpu.with_memory_space_constraint(array, pltpu.HBM)


def listed(offset, reach):
    return offset + reach if offset < 0 else offset + reach - 1


def row_of(axis, this, reach, sending):
    offset, level, side = this
    ahead = ((lax.axis_index(axis) >> level) & 1) == side
    plus, minus = listed(offset, reach), listed(-offset, reach)
    return jnp.where(ahead, minus, plus) if sending else jnp.where(ahead, plus, minus)


def row_of_pair(axis, sub_axis, pair_rounds, reach, sending, mine):
    first = (lax.axis_index(sub_axis) & 1) == (0 if mine else 1)
    rows = [row_of(axis, this, reach, sending) for this in pair_rounds]
    return jnp.where(first, rows[0], rows[1])


def partner(me, k, count):
    if count != 4:
        raise ValueError("subgroup size")
    return me ^ k


def swapped(shard, axis, k):
    count = lax.axis_size(axis)
    return lax.ppermute(shard, axis, [(i, partner(i, k, count)) for i in range(count)])


def spread(rows):
    block = lax.broadcasted_iota(jnp.int32, rows.shape, 1) // PAD
    turned = [rows] + [pltpu.roll(rows, PAD * q, axis=1) for q in range(1, SPLIT)]
    results = []
    for part in range(SPLIT):
        result = turned[(SPLIT - 1 - part) % SPLIT]
        for b in range(SPLIT - 1):
            result = jnp.where(block == b, turned[(b - part) % SPLIT], result)
        results.append(result)
    return results


def unpacked(packed):
    return jnp.concatenate(spread(packed), axis=0)


def split_two(value):
    high = value.astype(HALF)
    return high, (value - high.astype(F32)).astype(HALF)


def transposed_rows(maps_ref, padded, packed):
    order, _, elems = maps_ref.shape
    padded[...] = jnp.zeros_like(padded)
    for j in range(order):
        padded[j, :order, :] = maps_ref[j].astype(F32)
    rows = []
    for M in range(PACK):
        rows.append([])
    turned = [
        [jnp.swapaxes(padded[8 * b : 8 * b + 8, 8 * q : 8 * q + 8, :], 0, 1) for b in range(PAD // 8)]
        for q in range(SPLIT)
    ]
    packs = [
        jnp.concatenate([turned[q][b][M] for q in range(SPLIT) for b in range(PAD // 8)], axis=0).T
        for M in range(PACK)
    ]
    for e in range(0, elems, 8):
        group = jnp.stack([pack[e : e + 8, :] for pack in packs], axis=0)
        packed[e : e + 8] = jnp.swapaxes(group, 0, 1)


def padded_members(maps2_ref, padded, turned):
    order, members, _ = maps2_ref.shape
    padded[...] = jnp.zeros_like(padded)
    for d in range(order):
        padded[d, :, :order] = maps2_ref[d]
    for d in range(0, PAD, 8):
        for i in range(0, members, 8):
            turned[i : i + 8, d : d + 8, :] = jnp.swapaxes(padded[d : d + 8, i : i + 8, :], 0, 1)


def in_order(agg, elems):
    across = jnp.broadcast_to(agg, (elems, elems)).astype(F32)
    here = lax.broadcasted_iota(jnp.int32, (elems, elems), 0)
    there = lax.broadcasted_iota(jnp.int32, (elems, elems), 1)
    ahead = (across.T == across) & (here < there)
    rank = jnp.sum(jnp.where(ahead, 1.0, 0.0), axis=0, keepdims=True)
    place = jnp.broadcast_to(agg.astype(F32) * PER_AGG + rank, (elems, elems)).T
    found = jnp.where(place == there.astype(F32), here.astype(F32), 0.0)
    return jnp.sum(found, axis=0, keepdims=True).astype(jnp.int32)


def set_masks(masks):
    slots = masks.shape[0] // 2
    block = lax.broadcasted_iota(jnp.int32, (8, LANES), 1) // PAD
    for s in range(slots):
        for h in range(2):
            masks[s * 2 + h] = jnp.where(block + h * SPLIT == s, 1.0, 0.0).astype(HALF)


def masked(block, mask):
    return (block.reshape(PAD // 8, 8, LANES) * mask[None]).reshape(PAD, LANES)


def pack_kernel(axis, sub_axis, send_far, maps_far, maps2_far, *refs):
    keep_ref, give_ref, packed, turned2 = refs[:4]
    padded, flat, padded2, send_ref, maps_ref, maps2_ref, sems = refs[4:]
    send_rows, halo = send_far.shape
    members = maps2_ref.shape[1]
    reach = send_rows // 2
    copies = [
        pltpu.make_async_copy(far, near, sems.at[i])
        for i, (far, near) in enumerate(
            ((maps_far, maps_ref), (send_far, send_ref), (maps2_far, maps2_ref))
        )
    ]
    for copy in copies:
        copy.start()
    copies[0].wait()
    transposed_rows(maps_ref, padded, packed)
    copies[1].wait()
    every = rounds(reach)
    for t in range(reach):
        for mine, out in ((False, give_ref), (True, keep_ref)):
            row = row_of_pair(axis, sub_axis, every[2 * t : 2 * t + 2], reach, True, mine)
            for h in range(halo):
                flat[h * PACK : (h + 1) * PACK, :] = packed[send_ref[row, h]]
            out[t] = flat[...].astype(HALF)
    copies[2].wait()
    padded_members(maps2_ref, padded2, turned2)
    groups = members // SPLIT
    for g in range(groups):
        group = turned2[g * SPLIT : (g + 1) * SPLIT].reshape(SPLIT * PAD, LANES)
        high, low = split_two(group.T[:PAD])
        give_ref[reach, g * PAD : (g + 1) * PAD, :] = high
        give_ref[reach, (groups + g) * PAD : (groups + g + 1) * PAD, :] = low


def join_kernel(after, keep_ref, own_ref, got_ref, *out_refs):
    reach = keep_ref.shape[0]
    for t, out in enumerate(out_refs):
        rows = got_ref.shape[1]
        out[:rows, :] = keep_ref[t] if t < reach else own_ref[reach]
        out[rows:, :] = got_ref[t]


def part_kernel(*refs):
    rows = refs[-1].shape[1]
    for t, ref in enumerate(refs[1:-1]):
        refs[-1][t] = ref[rows:, :]


def table_kernel(packed, table_ref):
    elems = packed.shape[0]
    step = 32

    def table(i, carry):
        for u in range(step):
            e = i * step + u
            table_ref[e] = unpacked(packed[e]).astype(HALF)
        return carry

    lax.fori_loop(0, elems // step, table, 0)


def rows_kernel(agg_far, diag_far, face_far, maps_far, after, *refs):
    order_ref, g_ref, self_g_ref = refs[:3]
    rows_ref, own_ref, slab, left, right, agg_ref, diag_ref, face_ref, maps_ref = refs[3:12]
    order_row, sems = refs[12:]
    order, _, elems = maps_ref.shape
    faces = face_ref.shape[0]
    copies = [
        pltpu.make_async_copy(far, near, sems.at[i])
        for i, (far, near) in enumerate(
            ((agg_far, agg_ref), (face_far, face_ref), (diag_far, diag_ref), (maps_far, maps_ref))
        )
    ]
    for copy in copies:
        copy.start()

    copies[0].wait()
    order_row[...] = in_order(agg_ref[...], elems)
    order_copy = pltpu.make_async_copy(order_row, order_ref, sems.at[len(copies)])
    order_copy.start()
    for copy in copies[1:]:
        copy.wait()
    slab[...] = jnp.zeros_like(slab)
    tall = 2 * SPLIT * PAD
    for part in range(2):
        for rr in range(PAD // 2):
            r = part * (PAD // 2) + rr
            if r >= order:
                left[rr] = jnp.zeros((elems, LANES), F32)
                right[rr] = jnp.zeros((elems, LANES), F32)
                continue
            base = (r % 2) * tall
            sources = [face_ref[k, r] for k in range(faces)] + [diag_ref[r], maps_ref[r]]
            for k, source in enumerate(sources):
                slab[base + k * PAD : base + k * PAD + order, :] = source
            turned = slab[base : base + tall, :].T.astype(F32)
            left[rr] = turned[:, :LANES]
            right[rr] = turned[:, LANES:]

        def shuffle(i, carry, part=part):
            for v in range(4):
                e = pl.multiple_of(i * 32 + v * 8, 8)
                for h, half in enumerate((left, right)):
                    top = jnp.swapaxes(half[0:8, pl.ds(e, 8), :], 0, 1)
                    low = jnp.swapaxes(half[8:16, pl.ds(e, 8), :], 0, 1)
                    for u in range(8):
                        both = jnp.concatenate([top[u], low[u]], axis=0)
                        to = slice(part * 16, part * 16 + 16)
                        rows_ref[e + u, to, h * LANES : (h + 1) * LANES] = both.astype(HALF)
                        if h == 1:
                            own_ref[e + u, to, :] = pltpu.roll(both, PAD, axis=1).astype(HALF)
            return carry

        lax.fori_loop(0, elems // 32, shuffle, 0)
    order_copy.wait()
    block = lax.broadcasted_iota(jnp.int32, (PAD, LANES), 1) // PAD

    def products(i, carry):
        for v in range(8):
            selves = jnp.zeros((PAD, LANES), F32)
            for u in range(SPLIT):
                at = i * 32 + v * SPLIT + u
                e = order_ref[0, at]
                g = jnp.dot(own_ref[e][:, :PAD], rows_ref[e], preferred_element_type=F32)
                high, low = split_two(g)
                g_ref[at, 0:PAD, :] = high
                g_ref[at, PAD : 2 * PAD, :] = low
                turn = (u - faces) % SPLIT
                own = g[:, LANES:]
                own = pltpu.roll(own, turn * PAD, axis=1) if turn else own
                selves = jnp.where(block == u, own, selves)
            high, low = split_two(selves)
            self_g_ref[i * 8 + v, 0:PAD, :] = high
            self_g_ref[i * 8 + v, PAD : 2 * PAD, :] = low
        return carry

    lax.fori_loop(0, elems // 32, products, 0)


def local_kernel(axis, order_any, agg2_any, *refs):
    (table_ref, self_g_ref, turned2, mine_ref, mate_ref, other_ref, after) = refs[:7]
    far_refs, (two_hi, two_lo, near_ref, self_ref, z_ref) = refs[7:-8], refs[-8:-3]
    order_ref, agg2_ref, sems = refs[-3:]
    count = lax.axis_size(axis)
    members = agg2_ref.shape[0]
    copies = [
        pltpu.make_async_copy(order_any, order_ref, sems.at[0]),
        pltpu.make_async_copy(agg2_any, agg2_ref, sems.at[1]),
    ]
    for copy in copies:
        copy.start()
    groups = members // SPLIT

    for t, ref in enumerate(far_refs):
        for h in range(near_ref.shape[1]):
            near_ref[t, h] = unpacked(ref[h].astype(F32)).astype(HALF)

    me = lax.axis_index(axis)
    last = mine_ref.shape[0] - 1
    tall = mine_ref.shape[1]
    for k in range(count):
        first = partner(me, k, count) * members
        for which, two in enumerate((two_hi, two_lo)):
            for g in range(groups):
                start = (which * groups + g) * PAD
                if k < 2:
                    rows = (mine_ref, mate_ref)[k][last, start : start + PAD, :]
                else:
                    start += (k - 2) * tall
                    rows = other_ref[start : start + PAD, :]
                for q, block in enumerate(spread(rows.astype(F32))):
                    two[first + g * SPLIT + q] = block.astype(HALF)

    block = lax.broadcasted_iota(jnp.int32, (PAD, LANES), 1) // PAD
    rows = z_ref.shape[0] // 2
    for copy in copies:
        copy.wait()
    for g in range(groups):
        merged = turned2[g * SPLIT]
        to = jnp.full((PAD, LANES), agg2_ref[g * SPLIT], jnp.int32)
        for q in range(1, SPLIT):
            merged = merged + pltpu.roll(turned2[g * SPLIT + q], q * PAD, axis=1)
            to = jnp.where(block == q, agg2_ref[g * SPLIT + q], to)
        for k in range(rows // PAD):
            high, low = split_two(jnp.where(to == k, merged, 0.0))
            z_ref[k * PAD : (k + 1) * PAD, g * LANES : (g + 1) * LANES] = high
            z_ref[rows + k * PAD : rows + (k + 1) * PAD, g * LANES : (g + 1) * LANES] = low

    def selves(i4, carry):
        for v in range(4):
            i = i4 * 4 + v
            own = [table_ref[order_ref[0, i * PER_AGG + u]] for u in range(PER_AGG)]
            total = jnp.dot(
                jnp.concatenate([self_g_ref[i * 2], self_g_ref[i * 2 + 1]], axis=1),
                jnp.concatenate(own, axis=0),
                preferred_element_type=F32,
            )
            self_ref[i] = jnp.where(block == 0, total[:PAD] + total[PAD:], 0.0)
        return carry

    lax.fori_loop(0, members // 4, selves, 0)


def combine_kernel(axis, sub_axis, order_any, nbr_any, slot_any, nbr2_any, slot2_any, *refs):
    count = lax.axis_size(sub_axis)
    faces, elems = nbr_any.shape
    slots = nbr2_any.shape[0]
    own_ref, near_ref, post_ref, g_ref, self_ref, two_hi, two_lo, z_ref = refs[:8]
    one_refs = refs[8:10]
    part_refs = refs[10 : 10 + count]
    table, masks, w_hi, w_lo, acc0, acc1 = refs[10 + count : 16 + count]
    tables, sems = refs[16 + count : 21 + count], refs[21 + count]
    order_ref, nbr_ref, slot_ref, nbr2_ref, slot2_ref = tables
    reach, halo = near_ref.shape[:2]
    members = self_ref.shape[0]
    every = rounds(reach)

    def place(t, mine):
        row = row_of_pair(axis, sub_axis, every[2 * t : 2 * t + 2], reach, False, mine)
        return elems + row * halo

    copies = [pltpu.make_async_copy(own_ref, table.at[pl.ds(0, elems)], sems.at[reach])] + [
        pltpu.make_async_copy(near_ref.at[t], table.at[pl.ds(place(t, True), halo)], sems.at[t])
        for t in range(reach)
    ]
    copies += [
        pltpu.make_async_copy(source, to, sems.at[reach + 1 + i])
        for i, (source, to) in enumerate(
            zip((order_any, nbr_any, slot_any, nbr2_any, slot2_any), tables)
        )
    ]
    for copy in copies:
        copy.start()
    set_masks(masks)
    for t in range(reach):
        first = place(t, False)
        for h in range(halo):
            table[first + h] = unpacked(post_ref[t, h].astype(F32)).astype(HALF)
    for copy in copies:
        copy.wait()

    def placed(block, slot):
        return jnp.concatenate([masked(block, masks[slot * 2 + h]) for h in range(2)], axis=1)

    def gather(i2):
        for v in range(2):
            i = i2 * 2 + v
            total = jnp.zeros((2 * PAD, 2 * LANES), F32)
            for u in range(PER_AGG):
                at = i * PER_AGG + u
                e = order_ref[0, at]
                rows = [placed(table[nbr_ref[k, e]], slot_ref[k, e]) for k in range(faces)]
                total = total + jnp.dot(
                    g_ref[at][:, : faces * PAD],
                    jnp.concatenate(rows, axis=0),
                    preferred_element_type=F32,
                )
            one = total[:PAD] + total[PAD:]
            for h in range(2):
                half = one[:, h * LANES : (h + 1) * LANES]
                one_refs[h][i] = half + self_ref[i] if h == 0 else half

    def second(i2):
        for v in range(2):
            i = i2 * 2 + v
            one = jnp.concatenate([ref[i] for ref in one_refs], axis=1)
            high, low = split_two(one)
            to = [(nbr2_ref[j, i], slot2_ref[j, i]) for j in range(slots)]
            w = jnp.dot(
                jnp.concatenate([high, low], axis=0),
                jnp.concatenate([placed(two_hi[source], slot) for source, slot in to], axis=0),
                preferred_element_type=F32,
            )
            w_corrected = jnp.dot(
                high,
                jnp.concatenate([placed(two_lo[source], slot) for source, slot in to], axis=0),
                preferred_element_type=F32,
            )
            w_high, w_low = split_two((w[:PAD] + w[PAD:]) + w_corrected)
            at = pl.ds(pl.multiple_of(i * PAD, PAD), PAD)
            w_hi[at, :] = w_high
            w_lo[at, :] = w_low

    def both(i2, carry):
        second(i2 - 1)
        gather(i2)
        return carry

    gather(0)
    lax.fori_loop(1, members // 2, both, 0)
    second(members // 2 - 1)
    rows = z_ref.shape[0] // 2
    for h, acc in enumerate((acc0, acc1)):
        lanes = slice(h * LANES, (h + 1) * LANES)
        z = jnp.dot(z_ref[...], w_hi[:, lanes], preferred_element_type=F32)
        z_low = jnp.dot(z_ref[:rows, :], w_lo[:, lanes], preferred_element_type=F32)
        acc[...] = ((z[:rows] + z[rows:]) + z_low).reshape(acc.shape)
    me = lax.axis_index(sub_axis)
    owned = acc0.shape[0] // count
    for o in range(count):
        first = partner(me, o, count) * owned
        for h, acc in enumerate((acc0, acc1)):
            for k in range(owned):
                part_refs[o][h, k] = acc[first + k].astype(part_refs[o].dtype)


def write_rows(out_ref, h, a, rows):
    order = out_ref.shape[1]
    for q in range(SPLIT):
        turned = rows if q == 0 else pltpu.roll(rows, LANES - q * PAD, axis=1)
        out_ref[h * SPLIT + q, a] = turned[:, :order]


def one_kernel(one0_ref, one1_ref, out_ref):
    _, order, members, _ = out_ref.shape
    for h, ref in enumerate((one0_ref, one1_ref)):
        for b in range(0, PAD, 8):
            groups = [
                jnp.swapaxes(ref[i : i + 8, b : b + 8, :], 0, 1) for i in range(0, members, 8)
            ]
            for u in range(min(8, order - b)):
                write_rows(out_ref, h, b + u, jnp.concatenate([x[u] for x in groups], axis=0))


def two_kernel(*refs):
    part_refs, out_ref = refs[:-1], refs[-1]
    _, order, owned, _ = out_ref.shape
    for h in range(2):
        value = part_refs[0][h]
        for ref in part_refs[1:]:
            value = value + ref[h].astype(F32)
        for a in range(order):
            write_rows(
                out_ref, h, a, jnp.concatenate([value[k, a : a + 1] for k in range(owned)], axis=0)
            )


def per_device(
    diag_block,
    face_block,
    restrict1,
    neighbour,
    face_slot,
    agg_map,
    send_list,
    restrict2,
    coarse_nbr,
    agg2_map,
    coarse_slot,
):
    order, _, elems = restrict1.shape
    faces = face_block.shape[0]
    send_rows, halo = send_list.shape
    reach = send_rows // 2
    slots = coarse_nbr.shape[0]
    members = elems // PER_AGG
    owned = members // PER_AGG
    count = lax.axis_size("sub")
    shape = jax.ShapeDtypeStruct
    maps2 = jnp.transpose(restrict2, (0, 2, 1))

    near = pltpu.VMEM
    params = pltpu.CompilerParams(vmem_limit_bytes=36 * 2**20)
    tall = halo * PACK

    def call(kernel, name, in_specs, out_specs, out_shape, scratch, work):
        return pl.pallas_call(
            kernel,
            name=name,
            compiler_params=params,
            in_specs=in_specs,
            out_specs=out_specs,
            out_shape=out_shape,
            scratch_shapes=scratch,
            cost_estimate=pl.CostEstimate(
                flops=work * 1_000_000, bytes_accessed=work * 2_000, transcendentals=0
            ),
        )

    keep, give, own_rows, turned2 = call(
        functools.partial(pack_kernel, "dom", "sub"),
        "pack",
        [FAR] * 3,
        [VMEM] * 4,
        [
            near((reach, tall, LANES), HALF),
            near((reach + 1, tall, LANES), HALF),
            near((elems, PACK, LANES), F32),
            near((members, PAD, LANES), F32),
        ],
        [
            pltpu.VMEM((PAD, PAD, elems), F32),
            pltpu.VMEM((tall, LANES), F32),
            pltpu.VMEM((PAD, members, LANES), F32),
            pltpu.SMEM(send_list.shape, jnp.int32),
            pltpu.VMEM(restrict1.shape, HALF),
            pltpu.VMEM(maps2.shape, F32),
            pltpu.SemaphoreType.DMA((3,)),
        ],
        1000,
    )(*[far(x) for x in (send_list, restrict1, maps2)])
    if 2 * members * PAD // SPLIT != tall:
        raise ValueError("payload rows")
    got = swapped(give, "sub", 1)
    table = call(
        table_kernel, "table", [VMEM], VMEM, near((elems, PAD, LANES), HALF), [], 1000
    )(own_rows)
    joined = call(
        join_kernel,
        "join",
        [ANY] + [VMEM] * 3,
        [VMEM] * (reach + 1),
        [near((2 * tall, LANES), HALF)] * (reach + 1),
        [],
        300,
    )(table, keep, give, got)
    other = swapped(joined[reach], "sub", 2)
    every = rounds(reach)
    arrived = [
        exchanged(joined[t], "dom", "sub", every[2 * t : 2 * t + 2]) for t in range(reach)
    ]
    order_list, g, self_g = call(
        rows_kernel,
        "rows",
        [FAR] * 4 + [ANY],
        [SMEM, VMEM, VMEM],
        [
            shape((1, elems), jnp.int32),
            near((elems, 2 * PAD, 2 * LANES), HALF),
            near((elems // SPLIT, 2 * PAD, LANES), HALF),
        ],
        [
            pltpu.VMEM((elems, PAD, 2 * LANES), HALF),
            pltpu.VMEM((elems, PAD, LANES), HALF),
            pltpu.VMEM((4 * LANES, elems), HALF),
            pltpu.VMEM((PAD // 2, elems, LANES), F32),
            pltpu.VMEM((PAD // 2, elems, LANES), F32),
            pltpu.VMEM((1, elems), jnp.int32),
            pltpu.VMEM(diag_block.shape, HALF),
            pltpu.VMEM(face_block.shape, HALF),
            pltpu.VMEM(restrict1.shape, HALF),
            pltpu.VMEM((1, elems), jnp.int32),
            pltpu.SemaphoreType.DMA((5,)),
        ],
        8000,
    )(
        *[far(x) for x in (agg_map[None], diag_block, face_block, restrict1)],
        joined[0],
    )
    post = call(
        part_kernel,
        "part",
        [ANY] + [VMEM] * reach,
        VMEM,
        near((reach, tall, LANES), HALF),
        [],
        300,
    )(self_g, *arrived)
    landed_post = swapped(post, "sub", 1)
    halves = [block.reshape(2 * halo, PACK, LANES) for block in arrived]
    two_hi, two_lo, near_halo, self_terms, z = call(
        functools.partial(local_kernel, "sub"),
        "local",
        [ANY] * 2 + [VMEM] * 6 + [ANY] + [VMEM] * reach,
        [VMEM] * 5,
        [
            near((count * members, PAD, LANES), HALF),
            near((count * members, PAD, LANES), HALF),
            near((reach, halo, PAD, LANES), HALF),
            near((members, PAD, LANES), F32),
            near((2 * count * owned * PAD, members * PAD), HALF),
        ],
        [
            pltpu.SMEM((1, elems), jnp.int32),
            pltpu.SMEM(agg2_map.shape, jnp.int32),
            pltpu.SemaphoreType.DMA((2,)),
        ],
        2000,
    )(order_list, agg2_map, table, self_g, turned2, give, got, other, post, *halves)

    combined = pl.pallas_call(
        functools.partial(combine_kernel, "dom", "sub"),
        name="combine",
        compiler_params=params,
        in_specs=[ANY] * 5 + [VMEM] * 8,
        out_specs=[VMEM] * (2 + count),
        out_shape=[near((members, PAD, LANES), F32)] * 2
        + [near((2, owned, PAD, LANES), F32 if k < 2 else HALF) for k in range(count)],
        scratch_shapes=[
            pltpu.VMEM((elems + send_rows * halo, PAD, LANES), HALF),
            pltpu.VMEM((2 * SLOTS2, 8, LANES), HALF),
            pltpu.VMEM((members * PAD, 2 * LANES), HALF),
            pltpu.VMEM((members * PAD, 2 * LANES), HALF),
            pltpu.VMEM((count * owned, PAD, LANES), F32),
            pltpu.VMEM((count * owned, PAD, LANES), F32),
            pltpu.SMEM((1, elems), jnp.int32),
            pltpu.SMEM(neighbour.shape, jnp.int32),
            pltpu.SMEM(face_slot.shape, jnp.int32),
            pltpu.SMEM(coarse_nbr.shape, jnp.int32),
            pltpu.SMEM(coarse_slot.shape, jnp.int32),
            pltpu.SemaphoreType.DMA((reach + 6,)),
        ],
    )(
        order_list,
        neighbour,
        face_slot,
        coarse_nbr,
        coarse_slot,
        table,
        near_halo,
        landed_post.reshape(reach, halo, PACK, LANES),
        g,
        self_terms,
        two_hi,
        two_lo,
        z,
    )
    one0, one1, parts = combined[0], combined[1], combined[2:]
    landed = [parts[0]] + [swapped(parts[k], "sub", k) for k in range(1, count)]
    coarse_one = pl.pallas_call(
        one_kernel,
        name="first",
        compiler_params=params,
        in_specs=[VMEM] * 2,
        out_specs=VMEM,
        out_shape=shape((slots, order, members, order), F32),
        cost_estimate=pl.CostEstimate(
            flops=2_000_000_000, bytes_accessed=4_000_000, transcendentals=0
        ),
    )(one0, one1)
    coarse_two = pl.pallas_call(
        two_kernel,
        name="second",
        compiler_params=params,
        in_specs=[VMEM] * count,
        out_specs=VMEM,
        out_shape=shape((SLOTS2, order, owned, order), F32),
    )(*landed)
    return (
        jnp.transpose(coarse_one, (0, 1, 3, 2)),
        jnp.transpose(coarse_two, (0, 1, 3, 2)),
    )


def solution(mesh):
    placed = (
        P(None, None, ("dom", "sub")),
        P(None, None, None, ("dom", "sub")),
        P(None, None, ("dom", "sub")),
        P(None, ("dom", "sub")),
        P(None, ("dom", "sub")),
        P(("dom", "sub")),
        P(None, ("dom", "sub")),
        P(None, None, ("dom", "sub")),
        P(None, ("dom", "sub")),
        P(("dom", "sub")),
        P(None, ("dom", "sub")),
    )
    return jax.shard_map(
        per_device,
        mesh=mesh,
        in_specs=placed,
        out_specs=(P(None, None, None, ("dom", "sub")), P(None, None, None, ("dom", "sub"))),
        check_vma=False,
    )
```

```python
import functools

import jax
import jax.numpy as jnp
from jax import lax
from jax.experimental import pallas as pl
from jax.experimental.pallas import tpu as pltpu
from jax.sharding import PartitionSpec as P

SLOTS2 = 8
PER_AGG = 8
PAD = 32
LANES = 128
SPLIT = LANES // PAD
PACK = PAD // SPLIT


F32 = jnp.float32
HALF = jnp.bfloat16

VMEM = pl.BlockSpec(memory_space=pltpu.VMEM)
SMEM = pl.BlockSpec(memory_space=pltpu.SMEM)
ANY = pl.BlockSpec(memory_space=pl.ANY)
FAR = pl.BlockSpec(memory_space=pltpu.HBM)


def rounds(reach):
    sides = [(offset, side) for side in (1, 0) for offset in range(1, reach + 1)]
    if reach == 3:
        sides = [(2, 1), (3, 1), (3, 0), (1, 1), (2, 0), (1, 0)]
    return [(offset, (offset & -offset).bit_length() - 1, side) for offset, side in sides]


def across(index, this, count):
    offset, level, side = this
    if count % (2 << level):
        raise ValueError("ring length")
    return (index + offset if (index >> level) & 1 == side else index - offset) % count


def exchanged(shard, axis, sub_axis, pair_rounds):
    count, members = lax.axis_size(axis), lax.axis_size(sub_axis)
    pairs = [
        (d * members + s, across(d, pair_rounds[s & 1], count) * members + s)
        for d in range(count)
        for s in range(members)
    ]
    return lax.ppermute(shard, (axis, sub_axis), pairs)


def far(array):
    return pltpu.with_memory_space_constraint(array, pltpu.HBM)


def listed(offset, reach):
    return offset + reach if offset < 0 else offset + reach - 1


def row_of(axis, this, reach, sending):
    offset, level, side = this
    ahead = ((lax.axis_index(axis) >> level) & 1) == side
    plus, minus = listed(offset, reach), listed(-offset, reach)
    return jnp.where(ahead, minus, plus) if sending else jnp.where(ahead, plus, minus)


def row_of_pair(axis, sub_axis, pair_rounds, reach, sending, mine):
    first = (lax.axis_index(sub_axis) & 1) == (0 if mine else 1)
    rows = [row_of(axis, this, reach, sending) for this in pair_rounds]
    return jnp.where(first, rows[0], rows[1])


def partner(me, k, count):
    if count != 4:
        raise ValueError("subgroup size")
    return me ^ k


def swapped(shard, axis, k):
    count = lax.axis_size(axis)
    return lax.ppermute(shard, axis, [(i, partner(i, k, count)) for i in range(count)])


def spread(rows):
    block = lax.broadcasted_iota(jnp.int32, rows.shape, 1) // PAD
    turned = [rows] + [pltpu.roll(rows, PAD * q, axis=1) for q in range(1, SPLIT)]
    results = []
    for part in range(SPLIT):
        result = turned[(SPLIT - 1 - part) % SPLIT]
        for b in range(SPLIT - 1):
            result = jnp.where(block == b, turned[(b - part) % SPLIT], result)
        results.append(result)
    return results


def unpacked(packed):
    return jnp.concatenate(spread(packed), axis=0)


def split_two(value):
    high = value.astype(HALF)
    return high, (value - high.astype(F32)).astype(HALF)


def transposed_rows(maps_ref, padded, packed):
    order, _, elems = maps_ref.shape
    padded[...] = jnp.zeros_like(padded)
    for j in range(order):
        padded[j, :order, :] = maps_ref[j].astype(F32)
    rows = []
    for M in range(PACK):
        rows.append([])
    turned = [
        [jnp.swapaxes(padded[8 * b : 8 * b + 8, 8 * q : 8 * q + 8, :], 0, 1) for b in range(PAD // 8)]
        for q in range(SPLIT)
    ]
    packs = [
        jnp.concatenate([turned[q][b][M] for q in range(SPLIT) for b in range(PAD // 8)], axis=0).T
        for M in range(PACK)
    ]
    for e in range(0, elems, 8):
        group = jnp.stack([pack[e : e + 8, :] for pack in packs], axis=0)
        packed[e : e + 8] = jnp.swapaxes(group, 0, 1)


def padded_members(maps2_ref, padded, turned):
    order, members, _ = maps2_ref.shape
    padded[...] = jnp.zeros_like(padded)
    for d in range(order):
        padded[d, :, :order] = maps2_ref[d]
    for d in range(0, PAD, 8):
        for i in range(0, members, 8):
            turned[i : i + 8, d : d + 8, :] = jnp.swapaxes(padded[d : d + 8, i : i + 8, :], 0, 1)


def in_order(agg, elems):
    across = jnp.broadcast_to(agg, (elems, elems)).astype(F32)
    here = lax.broadcasted_iota(jnp.int32, (elems, elems), 0)
    there = lax.broadcasted_iota(jnp.int32, (elems, elems), 1)
    ahead = (across.T == across) & (here < there)
    rank = jnp.sum(jnp.where(ahead, 1.0, 0.0), axis=0, keepdims=True)
    place = jnp.broadcast_to(agg.astype(F32) * PER_AGG + rank, (elems, elems)).T
    found = jnp.where(place == there.astype(F32), here.astype(F32), 0.0)
    return jnp.sum(found, axis=0, keepdims=True).astype(jnp.int32)


def set_masks(masks):
    slots = masks.shape[0] // 2
    block = lax.broadcasted_iota(jnp.int32, (8, LANES), 1) // PAD
    for s in range(slots):
        for h in range(2):
            masks[s * 2 + h] = jnp.where(block + h * SPLIT == s, 1.0, 0.0).astype(HALF)


def masked(block, mask):
    return (block.reshape(PAD // 8, 8, LANES) * mask[None]).reshape(PAD, LANES)


def pack_kernel(axis, sub_axis, send_far, maps_far, maps2_far, *refs):
    keep_ref, give_ref, packed, turned2 = refs[:4]
    padded, flat, padded2, send_ref, maps_ref, maps2_ref, sems = refs[4:]
    send_rows, halo = send_far.shape
    members = maps2_ref.shape[1]
    reach = send_rows // 2
    copies = [
        pltpu.make_async_copy(far, near, sems.at[i])
        for i, (far, near) in enumerate(
            ((maps_far, maps_ref), (send_far, send_ref), (maps2_far, maps2_ref))
        )
    ]
    for copy in copies:
        copy.start()
    copies[0].wait()
    transposed_rows(maps_ref, padded, packed)
    copies[1].wait()
    every = rounds(reach)
    for t in range(reach):
        for mine, out in ((False, give_ref), (True, keep_ref)):
            row = row_of_pair(axis, sub_axis, every[2 * t : 2 * t + 2], reach, True, mine)
            for h in range(halo):
                flat[h * PACK : (h + 1) * PACK, :] = packed[send_ref[row, h]]
            out[t] = flat[...].astype(HALF)
    copies[2].wait()
    padded_members(maps2_ref, padded2, turned2)
    groups = members // SPLIT
    for g in range(groups):
        group = turned2[g * SPLIT : (g + 1) * SPLIT].reshape(SPLIT * PAD, LANES)
        high, low = split_two(group.T[:PAD])
        give_ref[reach, g * PAD : (g + 1) * PAD, :] = high
        give_ref[reach, (groups + g) * PAD : (groups + g + 1) * PAD, :] = low


def join_kernel(after, keep_ref, own_ref, got_ref, *out_refs):
    reach = keep_ref.shape[0]
    for t, out in enumerate(out_refs):
        rows = got_ref.shape[1]
        out[:rows, :] = keep_ref[t] if t < reach else own_ref[reach]
        out[rows:, :] = got_ref[t]


def part_kernel(*refs):
    rows = refs[-1].shape[1]
    for t, ref in enumerate(refs[1:-1]):
        refs[-1][t] = ref[rows:, :]


def table_kernel(packed, table_ref):
    elems = packed.shape[0]
    step = 32

    def table(i, carry):
        for u in range(step):
            e = i * step + u
            table_ref[e] = unpacked(packed[e]).astype(HALF)
        return carry

    lax.fori_loop(0, elems // step, table, 0)


def rows_kernel(agg_far, diag_far, face_far, maps_far, after, *refs):
    order_ref, g_ref, self_g_ref = refs[:3]
    rows_ref, own_ref, slab, left, right, agg_ref, diag_ref, face_ref, maps_ref = refs[3:12]
    order_row, sems = refs[12:]
    order, _, elems = maps_ref.shape
    faces = face_ref.shape[0]
    copies = [
        pltpu.make_async_copy(far, near, sems.at[i])
        for i, (far, near) in enumerate(
            ((agg_far, agg_ref), (face_far, face_ref), (diag_far, diag_ref), (maps_far, maps_ref))
        )
    ]
    for copy in copies:
        copy.start()

    copies[0].wait()
    order_row[...] = in_order(agg_ref[...], elems)
    order_copy = pltpu.make_async_copy(order_row, order_ref, sems.at[len(copies)])
    order_copy.start()
    for copy in copies[1:]:
        copy.wait()
    slab[...] = jnp.zeros_like(slab)
    tall = 2 * SPLIT * PAD
    for part in range(2):
        for rr in range(PAD // 2):
            r = part * (PAD // 2) + rr
            if r >= order:
                left[rr] = jnp.zeros((elems, LANES), F32)
                right[rr] = jnp.zeros((elems, LANES), F32)
                continue
            base = (r % 2) * tall
            sources = [face_ref[k, r] for k in range(faces)] + [diag_ref[r], maps_ref[r]]
            for k, source in enumerate(sources):
                slab[base + k * PAD : base + k * PAD + order, :] = source
            turned = slab[base : base + tall, :].T.astype(F32)
            left[rr] = turned[:, :LANES]
            right[rr] = turned[:, LANES:]

        def shuffle(i, carry, part=part):
            for v in range(4):
                e = pl.multiple_of(i * 32 + v * 8, 8)
                for h, half in enumerate((left, right)):
                    top = jnp.swapaxes(half[0:8, pl.ds(e, 8), :], 0, 1)
                    low = jnp.swapaxes(half[8:16, pl.ds(e, 8), :], 0, 1)
                    for u in range(8):
                        both = jnp.concatenate([top[u], low[u]], axis=0)
                        to = slice(part * 16, part * 16 + 16)
                        rows_ref[e + u, to, h * LANES : (h + 1) * LANES] = both.astype(HALF)
                        if h == 1:
                            own_ref[e + u, to, :] = pltpu.roll(both, PAD, axis=1).astype(HALF)
            return carry

        lax.fori_loop(0, elems // 32, shuffle, 0)
    order_copy.wait()
    block = lax.broadcasted_iota(jnp.int32, (PAD, LANES), 1) // PAD

    def products(i, carry):
        for v in range(8):
            selves = jnp.zeros((PAD, LANES), F32)
            for u in range(SPLIT):
                at = i * 32 + v * SPLIT + u
                e = order_ref[0, at]
                g = jnp.dot(own_ref[e][:, :PAD], rows_ref[e], preferred_element_type=F32)
                high, low = split_two(g)
                g_ref[at, 0:PAD, :] = high
                g_ref[at, PAD : 2 * PAD, :] = low
                turn = (u - faces) % SPLIT
                own = g[:, LANES:]
                own = pltpu.roll(own, turn * PAD, axis=1) if turn else own
                selves = jnp.where(block == u, own, selves)
            high, low = split_two(selves)
            self_g_ref[i * 8 + v, 0:PAD, :] = high
            self_g_ref[i * 8 + v, PAD : 2 * PAD, :] = low
        return carry

    lax.fori_loop(0, elems // 32, products, 0)


def local_kernel(axis, order_any, agg2_any, *refs):
    (table_ref, self_g_ref, turned2, mine_ref, mate_ref, other_ref, after) = refs[:7]
    far_refs, (two_hi, two_lo, near_ref, self_ref, z_ref) = refs[7:-8], refs[-8:-3]
    order_ref, agg2_ref, sems = refs[-3:]
    count = lax.axis_size(axis)
    members = agg2_ref.shape[0]
    copies = [
        pltpu.make_async_copy(order_any, order_ref, sems.at[0]),
        pltpu.make_async_copy(agg2_any, agg2_ref, sems.at[1]),
    ]
    for copy in copies:
        copy.start()
    groups = members // SPLIT

    for t, ref in enumerate(far_refs):
        for h in range(near_ref.shape[1]):
            near_ref[t, h] = unpacked(ref[h].astype(F32)).astype(HALF)

    me = lax.axis_index(axis)
    last = mine_ref.shape[0] - 1
    tall = mine_ref.shape[1]
    for k in range(count):
        first = partner(me, k, count) * members
        for which, two in enumerate((two_hi, two_lo)):
            for g in range(groups):
                start = (which * groups + g) * PAD
                if k < 2:
                    rows = (mine_ref, mate_ref)[k][last, start : start + PAD, :]
                else:
                    start += (k - 2) * tall
                    rows = other_ref[start : start + PAD, :]
                for q, block in enumerate(spread(rows.astype(F32))):
                    two[first + g * SPLIT + q] = block.astype(HALF)

    block = lax.broadcasted_iota(jnp.int32, (PAD, LANES), 1) // PAD
    rows = z_ref.shape[0] // 2
    for copy in copies:
        copy.wait()
    for g in range(groups):
        merged = turned2[g * SPLIT]
        to = jnp.full((PAD, LANES), agg2_ref[g * SPLIT], jnp.int32)
        for q in range(1, SPLIT):
            merged = merged + pltpu.roll(turned2[g * SPLIT + q], q * PAD, axis=1)
            to = jnp.where(block == q, agg2_ref[g * SPLIT + q], to)
        for k in range(rows // PAD):
            high, low = split_two(jnp.where(to == k, merged, 0.0))
            z_ref[k * PAD : (k + 1) * PAD, g * LANES : (g + 1) * LANES] = high
            z_ref[rows + k * PAD : rows + (k + 1) * PAD, g * LANES : (g + 1) * LANES] = low

    for i in range(members):
        own = [table_ref[order_ref[0, i * PER_AGG + u]] for u in range(PER_AGG)]
        total = jnp.dot(
            jnp.concatenate([self_g_ref[i * 2], self_g_ref[i * 2 + 1]], axis=1),
            jnp.concatenate(own, axis=0),
            preferred_element_type=F32,
        )
        self_ref[i] = jnp.where(block == 0, total[:PAD] + total[PAD:], 0.0)


def combine_kernel(axis, sub_axis, order_any, nbr_any, slot_any, nbr2_any, slot2_any, *refs):
    count = lax.axis_size(sub_axis)
    faces, elems = nbr_any.shape
    slots = nbr2_any.shape[0]
    own_ref, near_ref, post_ref, g_ref, self_ref, two_hi, two_lo, z_ref = refs[:8]
    one_refs = refs[8:10]
    keep_ref, give_ref = refs[10:12]
    table, masks, w_hi, w_lo, acc0, acc1 = refs[12:18]
    tables, sems = refs[18:23], refs[23]
    order_ref, nbr_ref, slot_ref, nbr2_ref, slot2_ref = tables
    reach, halo = near_ref.shape[:2]
    members = self_ref.shape[0]
    every = rounds(reach)

    def place(t, mine):
        row = row_of_pair(axis, sub_axis, every[2 * t : 2 * t + 2], reach, False, mine)
        return elems + row * halo

    copies = [pltpu.make_async_copy(own_ref, table.at[pl.ds(0, elems)], sems.at[reach])] + [
        pltpu.make_async_copy(near_ref.at[t], table.at[pl.ds(place(t, True), halo)], sems.at[t])
        for t in range(reach)
    ]
    copies += [
        pltpu.make_async_copy(source, to, sems.at[reach + 1 + i])
        for i, (source, to) in enumerate(
            zip((order_any, nbr_any, slot_any, nbr2_any, slot2_any), tables)
        )
    ]
    for copy in copies:
        copy.start()
    set_masks(masks)
    for t in range(reach):
        first = place(t, False)
        for h in range(halo):
            table[first + h] = unpacked(post_ref[t, h].astype(F32)).astype(HALF)
    for copy in copies:
        copy.wait()

    def placed(block, slot):
        return jnp.concatenate([masked(block, masks[slot * 2 + h]) for h in range(2)], axis=1)

    def gather(i2):
        for v in range(2):
            i = i2 * 2 + v
            total = jnp.zeros((2 * PAD, 2 * LANES), F32)
            for u in range(PER_AGG):
                at = i * PER_AGG + u
                e = order_ref[0, at]
                rows = [placed(table[nbr_ref[k, e]], slot_ref[k, e]) for k in range(faces)]
                total = total + jnp.dot(
                    g_ref[at][:, : faces * PAD],
                    jnp.concatenate(rows, axis=0),
                    preferred_element_type=F32,
                )
            one = total[:PAD] + total[PAD:]
            for h in range(2):
                half = one[:, h * LANES : (h + 1) * LANES]
                one_refs[h][i] = half + self_ref[i] if h == 0 else half

    def second(i2):
        for v in range(2):
            i = i2 * 2 + v
            one = jnp.concatenate([ref[i] for ref in one_refs], axis=1)
            high, low = split_two(one)
            to = [(nbr2_ref[j, i], slot2_ref[j, i]) for j in range(slots)]
            w = jnp.dot(
                jnp.concatenate([high, low], axis=0),
                jnp.concatenate([placed(two_hi[source], slot) for source, slot in to], axis=0),
                preferred_element_type=F32,
            )
            w_corrected = jnp.dot(
                high,
                jnp.concatenate([placed(two_lo[source], slot) for source, slot in to], axis=0),
                preferred_element_type=F32,
            )
            w_high, w_low = split_two((w[:PAD] + w[PAD:]) + w_corrected)
            at = pl.ds(pl.multiple_of(i * PAD, PAD), PAD)
            w_hi[at, :] = w_high
            w_lo[at, :] = w_low

    def both(i2, carry):
        second(i2 - 1)
        gather(i2)
        return carry

    gather(0)
    lax.fori_loop(1, members // 2, both, 0)
    second(members // 2 - 1)
    rows = z_ref.shape[0] // 2
    for h, acc in enumerate((acc0, acc1)):
        lanes = slice(h * LANES, (h + 1) * LANES)
        z = jnp.dot(z_ref[...], w_hi[:, lanes], preferred_element_type=F32)
        z_low = jnp.dot(z_ref[:rows, :], w_lo[:, lanes], preferred_element_type=F32)
        acc[...] = ((z[:rows] + z[rows:]) + z_low).reshape(acc.shape)
    me = lax.axis_index(sub_axis)
    owned = acc0.shape[0] // count
    for o in range(count):
        first = partner(me, o, count) * owned
        out = give_ref if o & 1 else keep_ref
        for h, acc in enumerate((acc0, acc1)):
            for k in range(owned):
                out[o // 2, h, k] = acc[first + k]


def sum_kernel(keep_ref, got_ref, near_ref, far_ref):
    near_ref[...] = keep_ref[0] + got_ref[0]
    far_ref[...] = (keep_ref[1] + got_ref[1]).astype(far_ref.dtype)


def write_rows(out_ref, h, a, rows):
    order = out_ref.shape[1]
    for q in range(SPLIT):
        turned = rows if q == 0 else pltpu.roll(rows, LANES - q * PAD, axis=1)
        out_ref[h * SPLIT + q, a] = turned[:, :order]


def one_kernel(one0_ref, one1_ref, after, out_ref):
    _, order, members, _ = out_ref.shape
    for h, ref in enumerate((one0_ref, one1_ref)):
        for b in range(0, PAD, 8):
            groups = [
                jnp.swapaxes(ref[i : i + 8, b : b + 8, :], 0, 1) for i in range(0, members, 8)
            ]
            for u in range(min(8, order - b)):
                write_rows(out_ref, h, b + u, jnp.concatenate([x[u] for x in groups], axis=0))


def two_kernel(*refs):
    part_refs, out_ref = refs[:-1], refs[-1]
    _, order, owned, _ = out_ref.shape
    for h in range(2):
        value = part_refs[0][h]
        for ref in part_refs[1:]:
            value = value + ref[h].astype(F32)
        for a in range(order):
            write_rows(
                out_ref, h, a, jnp.concatenate([value[k, a : a + 1] for k in range(owned)], axis=0)
            )


def per_device(
    diag_block,
    face_block,
    restrict1,
    neighbour,
    face_slot,
    agg_map,
    send_list,
    restrict2,
    coarse_nbr,
    agg2_map,
    coarse_slot,
):
    order, _, elems = restrict1.shape
    faces = face_block.shape[0]
    send_rows, halo = send_list.shape
    reach = send_rows // 2
    slots = coarse_nbr.shape[0]
    members = elems // PER_AGG
    owned = members // PER_AGG
    count = lax.axis_size("sub")
    shape = jax.ShapeDtypeStruct
    maps2 = jnp.transpose(restrict2, (0, 2, 1))

    near = pltpu.VMEM
    params = pltpu.CompilerParams(vmem_limit_bytes=36 * 2**20)
    tall = halo * PACK

    def call(kernel, name, in_specs, out_specs, out_shape, scratch, work):
        return pl.pallas_call(
            kernel,
            name=name,
            compiler_params=params,
            in_specs=in_specs,
            out_specs=out_specs,
            out_shape=out_shape,
            scratch_shapes=scratch,
            cost_estimate=pl.CostEstimate(
                flops=work * 1_000_000, bytes_accessed=work * 2_000, transcendentals=0
            ),
        )

    keep, give, own_rows, turned2 = call(
        functools.partial(pack_kernel, "dom", "sub"),
        "pack",
        [FAR] * 3,
        [VMEM] * 4,
        [
            near((reach, tall, LANES), HALF),
            near((reach + 1, tall, LANES), HALF),
            near((elems, PACK, LANES), F32),
            near((members, PAD, LANES), F32),
        ],
        [
            pltpu.VMEM((PAD, PAD, elems), F32),
            pltpu.VMEM((tall, LANES), F32),
            pltpu.VMEM((PAD, members, LANES), F32),
            pltpu.SMEM(send_list.shape, jnp.int32),
            pltpu.VMEM(restrict1.shape, HALF),
            pltpu.VMEM(maps2.shape, F32),
            pltpu.SemaphoreType.DMA((3,)),
        ],
        1000,
    )(*[far(x) for x in (send_list, restrict1, maps2)])
    if 2 * members * PAD // SPLIT != tall:
        raise ValueError("payload rows")
    got = swapped(give, "sub", 1)
    table = call(
        table_kernel, "table", [VMEM], VMEM, near((elems, PAD, LANES), HALF), [], 1000
    )(own_rows)
    joined = call(
        join_kernel,
        "join",
        [ANY] + [VMEM] * 3,
        [VMEM] * (reach + 1),
        [near((2 * tall, LANES), HALF)] * (reach + 1),
        [],
        300,
    )(table, keep, give, got)
    other = swapped(joined[reach], "sub", 2)
    every = rounds(reach)
    arrived = [
        exchanged(joined[t], "dom", "sub", every[2 * t : 2 * t + 2]) for t in range(reach)
    ]
    order_list, g, self_g = call(
        rows_kernel,
        "rows",
        [FAR] * 4 + [ANY],
        [SMEM, VMEM, VMEM],
        [
            shape((1, elems), jnp.int32),
            near((elems, 2 * PAD, 2 * LANES), HALF),
            near((elems // SPLIT, 2 * PAD, LANES), HALF),
        ],
        [
            pltpu.VMEM((elems, PAD, 2 * LANES), HALF),
            pltpu.VMEM((elems, PAD, LANES), HALF),
            pltpu.VMEM((4 * LANES, elems), HALF),
            pltpu.VMEM((PAD // 2, elems, LANES), F32),
            pltpu.VMEM((PAD // 2, elems, LANES), F32),
            pltpu.VMEM((1, elems), jnp.int32),
            pltpu.VMEM(diag_block.shape, HALF),
            pltpu.VMEM(face_block.shape, HALF),
            pltpu.VMEM(restrict1.shape, HALF),
            pltpu.VMEM((1, elems), jnp.int32),
            pltpu.SemaphoreType.DMA((5,)),
        ],
        8000,
    )(
        *[far(x) for x in (agg_map[None], diag_block, face_block, restrict1)],
        joined[0],
    )
    post = call(
        part_kernel,
        "part",
        [ANY] + [VMEM] * reach,
        VMEM,
        near((reach, tall, LANES), HALF),
        [],
        300,
    )(self_g, *arrived)
    landed_post = swapped(post, "sub", 1)
    halves = [block.reshape(2 * halo, PACK, LANES) for block in arrived]
    two_hi, two_lo, near_halo, self_terms, z = call(
        functools.partial(local_kernel, "sub"),
        "local",
        [ANY] * 2 + [VMEM] * 6 + [ANY] + [VMEM] * reach,
        [VMEM] * 5,
        [
            near((count * members, PAD, LANES), HALF),
            near((count * members, PAD, LANES), HALF),
            near((reach, halo, PAD, LANES), HALF),
            near((members, PAD, LANES), F32),
            near((2 * count * owned * PAD, members * PAD), HALF),
        ],
        [
            pltpu.SMEM((1, elems), jnp.int32),
            pltpu.SMEM(agg2_map.shape, jnp.int32),
            pltpu.SemaphoreType.DMA((2,)),
        ],
        2000,
    )(order_list, agg2_map, table, self_g, turned2, give, got, other, post, *halves)

    combined = pl.pallas_call(
        functools.partial(combine_kernel, "dom", "sub"),
        name="combine",
        compiler_params=params,
        in_specs=[ANY] * 5 + [VMEM] * 8,
        out_specs=[VMEM] * 4,
        out_shape=[near((members, PAD, LANES), F32)] * 2
        + [near((count // 2, 2, owned, PAD, LANES), F32)] * 2,
        scratch_shapes=[
            pltpu.VMEM((elems + send_rows * halo, PAD, LANES), HALF),
            pltpu.VMEM((2 * SLOTS2, 8, LANES), HALF),
            pltpu.VMEM((members * PAD, 2 * LANES), HALF),
            pltpu.VMEM((members * PAD, 2 * LANES), HALF),
            pltpu.VMEM((count * owned, PAD, LANES), F32),
            pltpu.VMEM((count * owned, PAD, LANES), F32),
            pltpu.SMEM((1, elems), jnp.int32),
            pltpu.SMEM(neighbour.shape, jnp.int32),
            pltpu.SMEM(face_slot.shape, jnp.int32),
            pltpu.SMEM(coarse_nbr.shape, jnp.int32),
            pltpu.SMEM(coarse_slot.shape, jnp.int32),
            pltpu.SemaphoreType.DMA((reach + 6,)),
        ],
    )(
        order_list,
        neighbour,
        face_slot,
        coarse_nbr,
        coarse_slot,
        table,
        near_halo,
        landed_post.reshape(reach, halo, PACK, LANES),
        g,
        self_terms,
        two_hi,
        two_lo,
        z,
    )
    one0, one1, keep2, give2 = combined
    pair_sum, far_sum = call(
        sum_kernel,
        "sum",
        [VMEM] * 2,
        [VMEM] * 2,
        [near((2, owned, PAD, LANES), F32), near((2, owned, PAD, LANES), HALF)],
        [],
        100,
    )(keep2, swapped(give2, "sub", 1))
    landed = [pair_sum, swapped(far_sum, "sub", 2)]
    coarse_one = pl.pallas_call(
        one_kernel,
        name="first",
        compiler_params=params,
        in_specs=[VMEM] * 2 + [ANY],
        out_specs=VMEM,
        out_shape=shape((slots, order, members, order), F32),
        cost_estimate=pl.CostEstimate(
            flops=2_000_000_000, bytes_accessed=4_000_000, transcendentals=0
        ),
    )(one0, one1, far_sum)
    coarse_two = pl.pallas_call(
        two_kernel,
        name="second",
        compiler_params=params,
        in_specs=[VMEM] * len(landed),
        out_specs=VMEM,
        out_shape=shape((SLOTS2, order, owned, order), F32),
    )(*landed)
    return (
        jnp.transpose(coarse_one, (0, 1, 3, 2)),
        jnp.transpose(coarse_two, (0, 1, 3, 2)),
    )


def solution(mesh):
    placed = (
        P(None, None, ("dom", "sub")),
        P(None, None, None, ("dom", "sub")),
        P(None, None, ("dom", "sub")),
        P(None, ("dom", "sub")),
        P(None, ("dom", "sub")),
        P(("dom", "sub")),
        P(None, ("dom", "sub")),
        P(None, None, ("dom", "sub")),
        P(None, ("dom", "sub")),
        P(("dom", "sub")),
        P(None, ("dom", "sub")),
    )
    return jax.shard_map(
        per_device,
        mesh=mesh,
        in_specs=placed,
        out_specs=(P(None, None, None, ("dom", "sub")), P(None, None, None, ("dom", "sub"))),
        check_vma=False,
    )
```

```python
import functools

import jax
import jax.numpy as jnp
from jax import lax
from jax.experimental import pallas as pl
from jax.experimental.pallas import tpu as pltpu
from jax.sharding import PartitionSpec as P

SLOTS2 = 8
PER_AGG = 8
PAD = 32
LANES = 128
SPLIT = LANES // PAD
PACK = PAD // SPLIT


F32 = jnp.float32
HALF = jnp.bfloat16

VMEM = pl.BlockSpec(memory_space=pltpu.VMEM)
SMEM = pl.BlockSpec(memory_space=pltpu.SMEM)
ANY = pl.BlockSpec(memory_space=pl.ANY)
FAR = pl.BlockSpec(memory_space=pltpu.HBM)


def rounds(reach):
    sides = [(offset, side) for side in (1, 0) for offset in range(1, reach + 1)]
    if reach == 3:
        sides = [(2, 1), (3, 1), (3, 0), (1, 1), (2, 0), (1, 0)]
    return [(offset, (offset & -offset).bit_length() - 1, side) for offset, side in sides]


def across(index, this, count):
    offset, level, side = this
    if count % (2 << level):
        raise ValueError("ring length")
    return (index + offset if (index >> level) & 1 == side else index - offset) % count


def exchanged(shard, axis, sub_axis, pair_rounds):
    count, members = lax.axis_size(axis), lax.axis_size(sub_axis)
    pairs = [
        (d * members + s, across(d, pair_rounds[s & 1], count) * members + s)
        for d in range(count)
        for s in range(members)
    ]
    return lax.ppermute(shard, (axis, sub_axis), pairs)


def far(array):
    return pltpu.with_memory_space_constraint(array, pltpu.HBM)


def listed(offset, reach):
    return offset + reach if offset < 0 else offset + reach - 1


def row_of(axis, this, reach, sending):
    offset, level, side = this
    ahead = ((lax.axis_index(axis) >> level) & 1) == side
    plus, minus = listed(offset, reach), listed(-offset, reach)
    return jnp.where(ahead, minus, plus) if sending else jnp.where(ahead, plus, minus)


def row_of_pair(axis, sub_axis, pair_rounds, reach, sending, mine):
    first = (lax.axis_index(sub_axis) & 1) == (0 if mine else 1)
    rows = [row_of(axis, this, reach, sending) for this in pair_rounds]
    return jnp.where(first, rows[0], rows[1])


def partner(me, k, count):
    if count != 4:
        raise ValueError("subgroup size")
    return me ^ k


def swapped(shard, axis, k):
    count = lax.axis_size(axis)
    return lax.ppermute(shard, axis, [(i, partner(i, k, count)) for i in range(count)])


def spread(rows):
    block = lax.broadcasted_iota(jnp.int32, rows.shape, 1) // PAD
    turned = [rows] + [pltpu.roll(rows, PAD * q, axis=1) for q in range(1, SPLIT)]
    results = []
    for part in range(SPLIT):
        result = turned[(SPLIT - 1 - part) % SPLIT]
        for b in range(SPLIT - 1):
            result = jnp.where(block == b, turned[(b - part) % SPLIT], result)
        results.append(result)
    return results


def unpacked(packed):
    return jnp.concatenate(spread(packed), axis=0)


def split_two(value):
    high = value.astype(HALF)
    return high, (value - high.astype(F32)).astype(HALF)


def transposed_rows(maps_ref, padded, packed):
    order, _, elems = maps_ref.shape
    for j in range(order):
        padded[j, :order, :] = maps_ref[j].astype(F32)
    rows = []
    for M in range(PACK):
        rows.append([])
    turned = [
        [jnp.swapaxes(padded[8 * b : 8 * b + 8, 8 * q : 8 * q + 8, :], 0, 1) for b in range(PAD // 8)]
        for q in range(SPLIT)
    ]
    packs = [
        jnp.concatenate([turned[q][b][M] for q in range(SPLIT) for b in range(PAD // 8)], axis=0).T
        for M in range(PACK)
    ]
    for e in range(0, elems, 8):
        group = jnp.stack([pack[e : e + 8, :] for pack in packs], axis=0)
        packed[e : e + 8] = jnp.swapaxes(group, 0, 1)


def padded_members(maps2_ref, padded, turned):
    order, members, _ = maps2_ref.shape
    for d in range(order):
        padded[d, :, :order] = maps2_ref[d]
    for d in range(0, PAD, 8):
        for i in range(0, members, 8):
            turned[i : i + 8, d : d + 8, :] = jnp.swapaxes(padded[d : d + 8, i : i + 8, :], 0, 1)


def in_order(agg, elems):
    across = jnp.broadcast_to(agg, (elems, elems)).astype(F32)
    here = lax.broadcasted_iota(jnp.int32, (elems, elems), 0)
    there = lax.broadcasted_iota(jnp.int32, (elems, elems), 1)
    ahead = (across.T == across) & (here < there)
    rank = jnp.sum(jnp.where(ahead, 1.0, 0.0), axis=0, keepdims=True)
    place = jnp.broadcast_to(agg.astype(F32) * PER_AGG + rank, (elems, elems)).T
    found = jnp.where(place == there.astype(F32), here.astype(F32), 0.0)
    return jnp.sum(found, axis=0, keepdims=True).astype(jnp.int32)


def set_masks(masks):
    slots = masks.shape[0] // 2
    block = lax.broadcasted_iota(jnp.int32, (8, LANES), 1) // PAD
    for s in range(slots):
        for h in range(2):
            masks[s * 2 + h] = jnp.where(block + h * SPLIT == s, 1.0, 0.0).astype(HALF)


def masked(block, mask):
    return (block.reshape(PAD // 8, 8, LANES) * mask[None]).reshape(PAD, LANES)


def pack_kernel(axis, sub_axis, send_far, maps_far, maps2_far, *refs):
    keep_ref, give_ref, packed, turned2 = refs[:4]
    padded, flat, padded2, send_ref, maps_ref, maps2_ref, sems = refs[4:]
    send_rows, halo = send_far.shape
    members = maps2_ref.shape[1]
    reach = send_rows // 2
    copies = [
        pltpu.make_async_copy(far, near, sems.at[i])
        for i, (far, near) in enumerate(
            ((maps_far, maps_ref), (send_far, send_ref), (maps2_far, maps2_ref))
        )
    ]
    for copy in copies:
        copy.start()
    padded[...] = jnp.zeros_like(padded)
    padded2[...] = jnp.zeros_like(padded2)
    copies[0].wait()
    transposed_rows(maps_ref, padded, packed)
    copies[1].wait()
    every = rounds(reach)
    for t in range(reach):
        for mine, out in ((False, give_ref), (True, keep_ref)):
            row = row_of_pair(axis, sub_axis, every[2 * t : 2 * t + 2], reach, True, mine)
            for h in range(halo):
                flat[h * PACK : (h + 1) * PACK, :] = packed[send_ref[row, h]]
            out[t] = flat[...].astype(HALF)
    copies[2].wait()
    padded_members(maps2_ref, padded2, turned2)
    groups = members // SPLIT
    for g in range(groups):
        group = turned2[g * SPLIT : (g + 1) * SPLIT].reshape(SPLIT * PAD, LANES)
        high, low = split_two(group.T[:PAD])
        give_ref[reach, g * PAD : (g + 1) * PAD, :] = high
        give_ref[reach, (groups + g) * PAD : (groups + g + 1) * PAD, :] = low


def join_kernel(after, keep_ref, own_ref, got_ref, *out_refs):
    reach = keep_ref.shape[0]
    for t, out in enumerate(out_refs):
        rows = got_ref.shape[1]
        out[:rows, :] = keep_ref[t] if t < reach else own_ref[reach]
        out[rows:, :] = got_ref[t]


def part_kernel(*refs):
    rows = refs[-1].shape[1]
    for t, ref in enumerate(refs[1:-1]):
        refs[-1][t] = ref[rows:, :]


def table_kernel(packed, table_ref):
    elems = packed.shape[0]
    step = 32

    def table(i, carry):
        for u in range(step):
            e = i * step + u
            table_ref[e] = unpacked(packed[e]).astype(HALF)
        return carry

    lax.fori_loop(0, elems // step, table, 0)


def rows_kernel(agg_far, diag_far, face_far, maps_far, after, *refs):
    order_ref, g_ref, self_g_ref = refs[:3]
    rows_ref, own_ref, slab, left, right, agg_ref, diag_ref, face_ref, maps_ref = refs[3:12]
    order_row, sems = refs[12:]
    order, _, elems = maps_ref.shape
    faces = face_ref.shape[0]
    copies = [
        pltpu.make_async_copy(far, near, sems.at[i])
        for i, (far, near) in enumerate(
            ((agg_far, agg_ref), (face_far, face_ref), (diag_far, diag_ref), (maps_far, maps_ref))
        )
    ]
    for copy in copies:
        copy.start()

    copies[0].wait()
    order_row[...] = in_order(agg_ref[...], elems)
    order_copy = pltpu.make_async_copy(order_row, order_ref, sems.at[len(copies)])
    order_copy.start()
    for copy in copies[1:]:
        copy.wait()
    slab[...] = jnp.zeros_like(slab)
    tall = 2 * SPLIT * PAD
    for part in range(2):
        for rr in range(PAD // 2):
            r = part * (PAD // 2) + rr
            if r >= order:
                left[rr] = jnp.zeros((elems, LANES), F32)
                right[rr] = jnp.zeros((elems, LANES), F32)
                continue
            base = (r % 2) * tall
            sources = [face_ref[k, r] for k in range(faces)] + [diag_ref[r], maps_ref[r]]
            for k, source in enumerate(sources):
                slab[base + k * PAD : base + k * PAD + order, :] = source
            turned = slab[base : base + tall, :].T.astype(F32)
            left[rr] = turned[:, :LANES]
            right[rr] = turned[:, LANES:]

        def shuffle(i, carry, part=part):
            for v in range(4):
                e = pl.multiple_of(i * 32 + v * 8, 8)
                for h, half in enumerate((left, right)):
                    top = jnp.swapaxes(half[0:8, pl.ds(e, 8), :], 0, 1)
                    low = jnp.swapaxes(half[8:16, pl.ds(e, 8), :], 0, 1)
                    for u in range(8):
                        both = jnp.concatenate([top[u], low[u]], axis=0)
                        to = slice(part * 16, part * 16 + 16)
                        rows_ref[e + u, to, h * LANES : (h + 1) * LANES] = both.astype(HALF)
                        if h == 1:
                            own_ref[e + u, to, :] = pltpu.roll(both, PAD, axis=1).astype(HALF)
            return carry

        lax.fori_loop(0, elems // 32, shuffle, 0)
    order_copy.wait()
    block = lax.broadcasted_iota(jnp.int32, (PAD, LANES), 1) // PAD

    def products(i, carry):
        for v in range(8):
            selves = jnp.zeros((PAD, LANES), F32)
            for u in range(SPLIT):
                at = i * 32 + v * SPLIT + u
                e = order_ref[0, at]
                g = jnp.dot(own_ref[e][:, :PAD], rows_ref[e], preferred_element_type=F32)
                high, low = split_two(g)
                g_ref[at, 0:PAD, :] = high
                g_ref[at, PAD : 2 * PAD, :] = low
                turn = (u - faces) % SPLIT
                own = g[:, LANES:]
                own = pltpu.roll(own, turn * PAD, axis=1) if turn else own
                selves = jnp.where(block == u, own, selves)
            high, low = split_two(selves)
            self_g_ref[i * 8 + v, 0:PAD, :] = high
            self_g_ref[i * 8 + v, PAD : 2 * PAD, :] = low
        return carry

    lax.fori_loop(0, elems // 32, products, 0)


def local_kernel(axis, order_any, agg2_any, *refs):
    (table_ref, self_g_ref, turned2, mine_ref, mate_ref, other_ref, after) = refs[:7]
    far_refs, (two_hi, two_lo, near_ref, self_ref, z_ref) = refs[7:-8], refs[-8:-3]
    order_ref, agg2_ref, sems = refs[-3:]
    count = lax.axis_size(axis)
    members = agg2_ref.shape[0]
    copies = [
        pltpu.make_async_copy(order_any, order_ref, sems.at[0]),
        pltpu.make_async_copy(agg2_any, agg2_ref, sems.at[1]),
    ]
    for copy in copies:
        copy.start()
    groups = members // SPLIT

    for t, ref in enumerate(far_refs):
        for h in range(near_ref.shape[1]):
            near_ref[t, h] = unpacked(ref[h].astype(F32)).astype(HALF)

    me = lax.axis_index(axis)
    last = mine_ref.shape[0] - 1
    tall = mine_ref.shape[1]
    for k in range(count):
        first = partner(me, k, count) * members
        for which, two in enumerate((two_hi, two_lo)):
            for g in range(groups):
                start = (which * groups + g) * PAD
                if k < 2:
                    rows = (mine_ref, mate_ref)[k][last, start : start + PAD, :]
                else:
                    start += (k - 2) * tall
                    rows = other_ref[start : start + PAD, :]
                for q, block in enumerate(spread(rows.astype(F32))):
                    two[first + g * SPLIT + q] = block.astype(HALF)

    block = lax.broadcasted_iota(jnp.int32, (PAD, LANES), 1) // PAD
    rows = z_ref.shape[0] // 2
    for copy in copies:
        copy.wait()
    for g in range(groups):
        merged = turned2[g * SPLIT]
        to = jnp.full((PAD, LANES), agg2_ref[g * SPLIT], jnp.int32)
        for q in range(1, SPLIT):
            merged = merged + pltpu.roll(turned2[g * SPLIT + q], q * PAD, axis=1)
            to = jnp.where(block == q, agg2_ref[g * SPLIT + q], to)
        for k in range(rows // PAD):
            high, low = split_two(jnp.where(to == k, merged, 0.0))
            z_ref[k * PAD : (k + 1) * PAD, g * LANES : (g + 1) * LANES] = high
            z_ref[rows + k * PAD : rows + (k + 1) * PAD, g * LANES : (g + 1) * LANES] = low

    for i in range(members):
        own = [table_ref[order_ref[0, i * PER_AGG + u]] for u in range(PER_AGG)]
        total = jnp.dot(
            jnp.concatenate([self_g_ref[i * 2], self_g_ref[i * 2 + 1]], axis=1),
            jnp.concatenate(own, axis=0),
            preferred_element_type=F32,
        )
        self_ref[i] = jnp.where(block == 0, total[:PAD] + total[PAD:], 0.0)


def combine_kernel(axis, sub_axis, order_any, nbr_any, slot_any, nbr2_any, slot2_any, *refs):
    count = lax.axis_size(sub_axis)
    faces, elems = nbr_any.shape
    slots = nbr2_any.shape[0]
    own_ref, near_ref, post_ref, g_ref, self_ref, two_hi, two_lo, z_ref = refs[:8]
    one_refs = refs[8:10]
    keep_ref, give_ref = refs[10:12]
    table, masks, w_hi, w_lo, acc0, acc1 = refs[12:18]
    tables, sems = refs[18:23], refs[23]
    order_ref, nbr_ref, slot_ref, nbr2_ref, slot2_ref = tables
    reach, halo = near_ref.shape[:2]
    members = self_ref.shape[0]
    every = rounds(reach)

    def place(t, mine):
        row = row_of_pair(axis, sub_axis, every[2 * t : 2 * t + 2], reach, False, mine)
        return elems + row * halo

    copies = [pltpu.make_async_copy(own_ref, table.at[pl.ds(0, elems)], sems.at[reach])] + [
        pltpu.make_async_copy(near_ref.at[t], table.at[pl.ds(place(t, True), halo)], sems.at[t])
        for t in range(reach)
    ]
    copies += [
        pltpu.make_async_copy(source, to, sems.at[reach + 1 + i])
        for i, (source, to) in enumerate(
            zip((order_any, nbr_any, slot_any, nbr2_any, slot2_any), tables)
        )
    ]
    for copy in copies:
        copy.start()
    set_masks(masks)
    for t in range(reach):
        first = place(t, False)
        for h in range(halo):
            table[first + h] = unpacked(post_ref[t, h].astype(F32)).astype(HALF)
    for copy in copies:
        copy.wait()

    def placed(block, slot):
        return jnp.concatenate([masked(block, masks[slot * 2 + h]) for h in range(2)], axis=1)

    def gather(i2):
        for v in range(2):
            i = i2 * 2 + v
            total = jnp.zeros((2 * PAD, 2 * LANES), F32)
            for u in range(PER_AGG):
                at = i * PER_AGG + u
                e = order_ref[0, at]
                rows = [placed(table[nbr_ref[k, e]], slot_ref[k, e]) for k in range(faces)]
                total = total + jnp.dot(
                    g_ref[at][:, : faces * PAD],
                    jnp.concatenate(rows, axis=0),
                    preferred_element_type=F32,
                )
            one = total[:PAD] + total[PAD:]
            for h in range(2):
                half = one[:, h * LANES : (h + 1) * LANES]
                one_refs[h][i] = half + self_ref[i] if h == 0 else half

    def second(i2):
        for v in range(2):
            i = i2 * 2 + v
            one = jnp.concatenate([ref[i] for ref in one_refs], axis=1)
            high, low = split_two(one)
            to = [(nbr2_ref[j, i], slot2_ref[j, i]) for j in range(slots)]
            w = jnp.dot(
                jnp.concatenate([high, low], axis=0),
                jnp.concatenate([placed(two_hi[source], slot) for source, slot in to], axis=0),
                preferred_element_type=F32,
            )
            w_corrected = jnp.dot(
                high,
                jnp.concatenate([placed(two_lo[source], slot) for source, slot in to], axis=0),
                preferred_element_type=F32,
            )
            w_high, w_low = split_two((w[:PAD] + w[PAD:]) + w_corrected)
            at = pl.ds(pl.multiple_of(i * PAD, PAD), PAD)
            w_hi[at, :] = w_high
            w_lo[at, :] = w_low

    def both(i2, carry):
        second(i2 - 1)
        gather(i2)
        return carry

    gather(0)
    lax.fori_loop(1, members // 2, both, 0)
    second(members // 2 - 1)
    rows = z_ref.shape[0] // 2
    for h, acc in enumerate((acc0, acc1)):
        lanes = slice(h * LANES, (h + 1) * LANES)
        z = jnp.dot(z_ref[...], w_hi[:, lanes], preferred_element_type=F32)
        z_low = jnp.dot(z_ref[:rows, :], w_lo[:, lanes], preferred_element_type=F32)
        acc[...] = ((z[:rows] + z[rows:]) + z_low).reshape(acc.shape)
    me = lax.axis_index(sub_axis)
    owned = acc0.shape[0] // count
    for o in range(count):
        first = partner(me, o, count) * owned
        out = give_ref if o & 1 else keep_ref
        for h, acc in enumerate((acc0, acc1)):
            for k in range(owned):
                out[o // 2, h, k] = acc[first + k]


def sum_kernel(keep_ref, got_ref, near_ref, far_ref):
    near_ref[...] = keep_ref[0] + got_ref[0]
    far_ref[...] = (keep_ref[1] + got_ref[1]).astype(far_ref.dtype)


def write_rows(out_ref, h, a, rows):
    order = out_ref.shape[1]
    for q in range(SPLIT):
        turned = rows if q == 0 else pltpu.roll(rows, LANES - q * PAD, axis=1)
        out_ref[h * SPLIT + q, a] = turned[:, :order]


def one_kernel(one0_ref, one1_ref, after, out_ref):
    _, order, members, _ = out_ref.shape
    for h, ref in enumerate((one0_ref, one1_ref)):
        for b in range(0, PAD, 8):
            groups = [
                jnp.swapaxes(ref[i : i + 8, b : b + 8, :], 0, 1) for i in range(0, members, 8)
            ]
            for u in range(min(8, order - b)):
                write_rows(out_ref, h, b + u, jnp.concatenate([x[u] for x in groups], axis=0))


def two_kernel(*refs):
    part_refs, out_ref = refs[:-1], refs[-1]
    _, order, owned, _ = out_ref.shape
    for h in range(2):
        value = part_refs[0][h]
        for ref in part_refs[1:]:
            value = value + ref[h].astype(F32)
        for a in range(order):
            write_rows(
                out_ref, h, a, jnp.concatenate([value[k, a : a + 1] for k in range(owned)], axis=0)
            )


def per_device(
    diag_block,
    face_block,
    restrict1,
    neighbour,
    face_slot,
    agg_map,
    send_list,
    restrict2,
    coarse_nbr,
    agg2_map,
    coarse_slot,
):
    order, _, elems = restrict1.shape
    faces = face_block.shape[0]
    send_rows, halo = send_list.shape
    reach = send_rows // 2
    slots = coarse_nbr.shape[0]
    members = elems // PER_AGG
    owned = members // PER_AGG
    count = lax.axis_size("sub")
    shape = jax.ShapeDtypeStruct
    maps2 = jnp.transpose(restrict2, (0, 2, 1))

    near = pltpu.VMEM
    params = pltpu.CompilerParams(vmem_limit_bytes=36 * 2**20)
    tall = halo * PACK

    def call(kernel, name, in_specs, out_specs, out_shape, scratch, work):
        return pl.pallas_call(
            kernel,
            name=name,
            compiler_params=params,
            in_specs=in_specs,
            out_specs=out_specs,
            out_shape=out_shape,
            scratch_shapes=scratch,
            cost_estimate=pl.CostEstimate(
                flops=work * 1_000_000, bytes_accessed=work * 2_000, transcendentals=0
            ),
        )

    keep, give, own_rows, turned2 = call(
        functools.partial(pack_kernel, "dom", "sub"),
        "pack",
        [FAR] * 3,
        [VMEM] * 4,
        [
            near((reach, tall, LANES), HALF),
            near((reach + 1, tall, LANES), HALF),
            near((elems, PACK, LANES), F32),
            near((members, PAD, LANES), F32),
        ],
        [
            pltpu.VMEM((PAD, PAD, elems), F32),
            pltpu.VMEM((tall, LANES), F32),
            pltpu.VMEM((PAD, members, LANES), F32),
            pltpu.SMEM(send_list.shape, jnp.int32),
            pltpu.VMEM(restrict1.shape, HALF),
            pltpu.VMEM(maps2.shape, F32),
            pltpu.SemaphoreType.DMA((3,)),
        ],
        1000,
    )(*[far(x) for x in (send_list, restrict1, maps2)])
    if 2 * members * PAD // SPLIT != tall:
        raise ValueError("payload rows")
    got = swapped(give, "sub", 1)
    table = call(
        table_kernel, "table", [VMEM], VMEM, near((elems, PAD, LANES), HALF), [], 1000
    )(own_rows)
    joined = call(
        join_kernel,
        "join",
        [ANY] + [VMEM] * 3,
        [VMEM] * (reach + 1),
        [near((2 * tall, LANES), HALF)] * (reach + 1),
        [],
        300,
    )(table, keep, give, got)
    other = swapped(joined[reach], "sub", 2)
    every = rounds(reach)
    arrived = [
        exchanged(joined[t], "dom", "sub", every[2 * t : 2 * t + 2]) for t in range(reach)
    ]
    order_list, g, self_g = call(
        rows_kernel,
        "rows",
        [FAR] * 4 + [ANY],
        [SMEM, VMEM, VMEM],
        [
            shape((1, elems), jnp.int32),
            near((elems, 2 * PAD, 2 * LANES), HALF),
            near((elems // SPLIT, 2 * PAD, LANES), HALF),
        ],
        [
            pltpu.VMEM((elems, PAD, 2 * LANES), HALF),
            pltpu.VMEM((elems, PAD, LANES), HALF),
            pltpu.VMEM((4 * LANES, elems), HALF),
            pltpu.VMEM((PAD // 2, elems, LANES), F32),
            pltpu.VMEM((PAD // 2, elems, LANES), F32),
            pltpu.VMEM((1, elems), jnp.int32),
            pltpu.VMEM(diag_block.shape, HALF),
            pltpu.VMEM(face_block.shape, HALF),
            pltpu.VMEM(restrict1.shape, HALF),
            pltpu.VMEM((1, elems), jnp.int32),
            pltpu.SemaphoreType.DMA((5,)),
        ],
        8000,
    )(
        *[far(x) for x in (agg_map[None], diag_block, face_block, restrict1)],
        joined[0],
    )
    post = call(
        part_kernel,
        "part",
        [ANY] + [VMEM] * reach,
        VMEM,
        near((reach, tall, LANES), HALF),
        [],
        300,
    )(self_g, *arrived)
    landed_post = swapped(post, "sub", 1)
    halves = [block.reshape(2 * halo, PACK, LANES) for block in arrived]
    two_hi, two_lo, near_halo, self_terms, z = call(
        functools.partial(local_kernel, "sub"),
        "local",
        [ANY] * 2 + [VMEM] * 6 + [ANY] + [VMEM] * reach,
        [VMEM] * 5,
        [
            near((count * members, PAD, LANES), HALF),
            near((count * members, PAD, LANES), HALF),
            near((reach, halo, PAD, LANES), HALF),
            near((members, PAD, LANES), F32),
            near((2 * count * owned * PAD, members * PAD), HALF),
        ],
        [
            pltpu.SMEM((1, elems), jnp.int32),
            pltpu.SMEM(agg2_map.shape, jnp.int32),
            pltpu.SemaphoreType.DMA((2,)),
        ],
        2000,
    )(order_list, agg2_map, table, self_g, turned2, give, got, other, post, *halves)

    combined = pl.pallas_call(
        functools.partial(combine_kernel, "dom", "sub"),
        name="combine",
        compiler_params=params,
        in_specs=[ANY] * 5 + [VMEM] * 8,
        out_specs=[VMEM] * 4,
        out_shape=[near((members, PAD, LANES), F32)] * 2
        + [near((count // 2, 2, owned, PAD, LANES), F32)] * 2,
        scratch_shapes=[
            pltpu.VMEM((elems + send_rows * halo, PAD, LANES), HALF),
            pltpu.VMEM((2 * SLOTS2, 8, LANES), HALF),
            pltpu.VMEM((members * PAD, 2 * LANES), HALF),
            pltpu.VMEM((members * PAD, 2 * LANES), HALF),
            pltpu.VMEM((count * owned, PAD, LANES), F32),
            pltpu.VMEM((count * owned, PAD, LANES), F32),
            pltpu.SMEM((1, elems), jnp.int32),
            pltpu.SMEM(neighbour.shape, jnp.int32),
            pltpu.SMEM(face_slot.shape, jnp.int32),
            pltpu.SMEM(coarse_nbr.shape, jnp.int32),
            pltpu.SMEM(coarse_slot.shape, jnp.int32),
            pltpu.SemaphoreType.DMA((reach + 6,)),
        ],
    )(
        order_list,
        neighbour,
        face_slot,
        coarse_nbr,
        coarse_slot,
        table,
        near_halo,
        landed_post.reshape(reach, halo, PACK, LANES),
        g,
        self_terms,
        two_hi,
        two_lo,
        z,
    )
    one0, one1, keep2, give2 = combined
    pair_sum, far_sum = call(
        sum_kernel,
        "sum",
        [VMEM] * 2,
        [VMEM] * 2,
        [near((2, owned, PAD, LANES), F32), near((2, owned, PAD, LANES), HALF)],
        [],
        100,
    )(keep2, swapped(give2, "sub", 1))
    landed = [pair_sum, swapped(far_sum, "sub", 2)]
    coarse_one = pl.pallas_call(
        one_kernel,
        name="first",
        compiler_params=params,
        in_specs=[VMEM] * 2 + [ANY],
        out_specs=VMEM,
        out_shape=shape((slots, order, members, order), F32),
        cost_estimate=pl.CostEstimate(
            flops=2_000_000_000, bytes_accessed=4_000_000, transcendentals=0
        ),
    )(one0, one1, far_sum)
    coarse_two = pl.pallas_call(
        two_kernel,
        name="second",
        compiler_params=params,
        in_specs=[VMEM] * len(landed),
        out_specs=VMEM,
        out_shape=shape((SLOTS2, order, owned, order), F32),
    )(*landed)
    return (
        jnp.transpose(coarse_one, (0, 1, 3, 2)),
        jnp.transpose(coarse_two, (0, 1, 3, 2)),
    )


def solution(mesh):
    placed = (
        P(None, None, ("dom", "sub")),
        P(None, None, None, ("dom", "sub")),
        P(None, None, ("dom", "sub")),
        P(None, ("dom", "sub")),
        P(None, ("dom", "sub")),
        P(("dom", "sub")),
        P(None, ("dom", "sub")),
        P(None, None, ("dom", "sub")),
        P(None, ("dom", "sub")),
        P(("dom", "sub")),
        P(None, ("dom", "sub")),
    )
    return jax.shard_map(
        per_device,
        mesh=mesh,
        in_specs=placed,
        out_specs=(P(None, None, None, ("dom", "sub")), P(None, None, None, ("dom", "sub"))),
        check_vma=False,
    )
```
